256 devices in a mesh: dp: 16 (over y, x), expert: 16 (over z, core).
Axes of the slice: x: 4, y: 4, z: 8, core: 2. Of those that a mesh axis runs over, the one named last changes fastest.
Arguments:
- tokens: bfloat16 [16384, 2048], P(('dp', 'expert')), may hold values from -6 to 6
- expert_ids: int32 [16384, 8], P(('dp', 'expert')), may hold values from 0 to 31, all different within a row; in each aligned block of 64 rows (0 to 63, 64 to 127, ...) at most 24 rows name the same one
- gate_fixed: int32 [16384, 8], P(('dp', 'expert')), may hold values from 1 to 65535
- scorer_id: int32 [1024], P(('dp', 'expert')), may hold values from 0 to 1
- direction_tags: bfloat16 [2, 2048], replicated, may hold values from -6 to 6
- w_gate: bfloat16 [32, 2048, 512], P('expert'), may hold values from -0.125 to 0.125
- w_up: bfloat16 [32, 2048, 512], P('expert'), may hold values from -0.125 to 0.125
- w_down: bfloat16 [32, 512, 2048], P('expert'), may hold values from -0.25 to 0.25
- score_head: float32 [2048], replicated, may hold values from -0.125 to 0.125
Outputs:
- mixed: bfloat16 [16384, 2048], P(('dp', 'expert'))
- pair_score: float32 [1024], P(('dp', 'expert'))
The draws below stay inside these ranges and needn't reach their ends.
Inputs may be any that keep to these rules, and one draw needn't show every extreme that they name: `expert_ids`: each row names 8 different experts. Among the rows of one device no expert is named by more than 24 rows, and in some devices' rows an expert is named by exactly 24.
All inputs are finite; a program needn't handle non-finite values.
Results may differ from the reference program's by a relative error of at most 0.04.
Values may be sent and summed in bfloat16 or wider, within the bound.
A program may use at most 64 MiB of HBM per device.

```python
import math
import jax
import jax.numpy as jnp
import numpy as np
from jax import lax

D = 2048
FF = 512
EXPERTS = 32
TOP = 8
SEQ_LEN = 16
TOK_DEV = 64
MOST = 24
TOKENS = 16384
SEQS = 1024


def plant(result, own_key, smallest, top_value):
    longest = result.shape.index(max(result.shape))
    spots = []
    for shift in (0, 1):
        where = [jax.random.randint(jax.random.fold_in(own_key, axis), (), 0, length) for axis, length in enumerate(result.shape)]
        where[longest] = (where[longest] + shift) % result.shape[longest]
        spots.append(tuple(where))
    return result.at[spots[0]].set(smallest).at[spots[1]].set(top_value)


def block_scale(stream_key, shape, split, least, largest):
    def one(position, shards_of):
        steps = jax.random.uniform(jax.random.fold_in(jax.random.fold_in(stream_key, 6), position), (shards_of,), jnp.float32, least / len(split), largest / len(split))
        return jnp.repeat(jnp.exp(steps), shape[position] // shards_of).reshape((-1,) + (1,) * (len(shape) - position - 1))

    factor_of = one(*split[0])
    for cut in split[1:]:
        factor_of = factor_of * one(*cut)
    return factor_of


def shared_out(own_key, own, number, rows, count, top, bound, slope):
    sequence = jax.random.permutation(own_key, count)
    crowded, ordinary = shares(count, rows * top, bound, slope, True), shares(count, rows * top, bound, slope, False)
    places = jnp.arange(count)

    def named(tallies, rotation):
        used = int((tallies > 0).sum())
        fixed = max(1, used // 4)
        passed = fixed + (places - fixed + rotation * (used - fixed)) % max(1, count - fixed)
        return jnp.zeros((count,), jnp.int32).at[sequence[jnp.where(places < fixed, places, passed)]].set(jnp.asarray(tallies, jnp.int32))

    tallies = jnp.where(number % 4 == 0, named(crowded, number // 4), named(ordinary, number - number // 4 - 1))
    mixed = jax.random.permutation(jax.random.fold_in(own, 3), count)
    giver, sink = mixed[0:count // 2 * 2:2], mixed[1:count // 2 * 2:2]
    room = jnp.minimum(tallies[giver] - 1, bound - tallies[sink]) // 2
    room = jnp.where((giver == sequence[0]) | (sink == sequence[0]) | (tallies[sink] == 0), 0, jnp.maximum(room, 0))
    passed = jax.random.randint(jax.random.fold_in(own, 4), (count // 2,), 0, 1 << 20) % (room + 1)
    tallies = tallies.at[giver].add(-passed).at[sink].add(passed)
    labels = jnp.searchsorted(jnp.cumsum(tallies), jnp.arange(rows * top), side="right").astype(jnp.int32)
    table = labels.reshape(top, rows).T
    table = table[jax.random.permutation(jax.random.fold_in(own, 1), rows)]
    rotation = jax.random.randint(jax.random.fold_in(own, 2), (rows, 1), 0, top)
    return jnp.take_along_axis(table, (jnp.arange(top)[None, :] + rotation) % top, axis=1)


def shares(number_of, total, most, slope, full):
    weights = [(1 << 20) // math.isqrt(standing ** slope) + 1 for standing in range(1, number_of + 1)]
    largest = most if full else min(most, max(-(-total // number_of), total * weights[0] // sum(weights)))
    least = 1 if total - largest >= number_of - 1 else 0
    counts, rest = [largest] + [least] * (number_of - 1), total - largest - least * (number_of - 1)
    while rest > 0:
        free = [i for i in range(1, number_of) if counts[i] < largest] or [i for i in range(1, number_of) if counts[i] < most]
        pool, remaining = sum([weights[i] for i in free]), rest
        for i in free:
            addition = min(most - counts[i], max(1, remaining * weights[i] // pool), rest)
            counts[i] = counts[i] + addition
            rest = rest - addition
    return np.array(counts)


def normal_values(stream_key, dims, width, bound, shards=(), kind=jnp.bfloat16):
    array = width * jax.random.normal(stream_key, dims, jnp.float32)
    if shards:
        array = array * block_scale(stream_key, dims, shards, -0.22, 0.18)
    return jnp.clip(array, -bound, bound).astype(kind)


def setup_inputs(seed: int = 0) -> dict:
    splits = jax.random.split(jax.random.key(seed), 10)
    tokens = normal_values(splits[0], (TOKENS, D), 1.0, 6.0, ((0, 256),))
    expert_ids_keys = jax.random.split(jax.random.fold_in(splits[1], 1), TOKENS // TOK_DEV)
    expert_ids_turns = jax.random.permutation(jax.random.fold_in(splits[1], 3), TOKENS // TOK_DEV)
    expert_ids = jax.vmap(lambda own, number: shared_out(jax.random.fold_in(splits[1], 2), own, number, TOK_DEV, EXPERTS, TOP, MOST, 2))(expert_ids_keys, expert_ids_turns).reshape((TOKENS, TOP))
    gate_fixed = plant(jax.random.randint(splits[2], (TOKENS, TOP), 1, 65536), jax.random.fold_in(splits[2], 1), 1, 65535).astype(jnp.int32)
    scorer_id = plant(jax.random.randint(splits[3], (SEQS,), 0, 2), jax.random.fold_in(splits[3], 1), 0, 1).astype(jnp.int32)
    direction_tags = normal_values(splits[4], (2, D), 1.0, 6.0)
    w_gate = normal_values(splits[5], (EXPERTS, D, FF), D ** -0.5, 0.125, ((0, 16),))
    w_up = normal_values(splits[6], (EXPERTS, D, FF), D ** -0.5, 0.125, ((0, 16),))
    w_down = normal_values(splits[7], (EXPERTS, FF, D), FF ** -0.5, 0.25, ((0, 16),))
    score_head = normal_values(splits[8], (D,), D ** -0.5, 0.125, (), jnp.float32)
    return dict(tokens=tokens, expert_ids=expert_ids, gate_fixed=gate_fixed, scorer_id=scorer_id, direction_tags=direction_tags, w_gate=w_gate, w_up=w_up, w_down=w_down, score_head=score_head)


def reference(tokens, expert_ids, gate_fixed, scorer_id, direction_tags, w_gate, w_up, w_down, score_head):
    tok_scorer = jnp.repeat(scorer_id, SEQ_LEN)
    tag_rows = direction_tags.astype(jnp.float32)[tok_scorer]
    inputs = (tokens.astype(jnp.float32) + tag_rows).astype(jnp.bfloat16)
    fixed_val = gate_fixed.astype(jnp.float32)
    weight = fixed_val / jnp.sum(fixed_val, axis=1, keepdims=True)
    blocks = TOKENS // TOK_DEV
    flat_ids = expert_ids.reshape(blocks, TOK_DEV * TOP)
    onehot = (flat_ids[:, :, None] == jnp.arange(EXPERTS, dtype=jnp.int32)[None, None, :]).astype(jnp.int32)
    rank_in = jnp.sum(jnp.cumsum(onehot, axis=1) * onehot, axis=2) - 1
    block_index = jnp.arange(blocks, dtype=jnp.int32)[:, None]
    slot_index = block_index * MOST + rank_in
    token_of = block_index * TOK_DEV + jnp.arange(TOK_DEV * TOP, dtype=jnp.int32)[None, :] // TOP
    capacity = blocks * MOST
    slot_table = jnp.zeros((EXPERTS, capacity), jnp.int32).at[flat_ids, slot_index].set(token_of)
    slot_weight = jnp.zeros((EXPERTS, capacity), jnp.float32).at[flat_ids, slot_index].set(weight.reshape(blocks, TOK_DEV * TOP))

    def scan_step(summed, expert_index):
        picked = slot_table[expert_index]
        row_block = inputs[picked]
        gate_proj = jnp.dot(row_block, w_gate[expert_index], preferred_element_type=jnp.float32)
        up_proj = jnp.dot(row_block, w_up[expert_index], preferred_element_type=jnp.float32)
        hidden = (jax.nn.silu(gate_proj) * up_proj).astype(jnp.bfloat16)
        down_out = jnp.dot(hidden, w_down[expert_index], preferred_element_type=jnp.float32)
        expert_out = (slot_weight[expert_index][:, None] * down_out).astype(jnp.bfloat16)
        return summed.at[picked].add(expert_out.astype(jnp.float32)), None

    summed, _ = lax.scan(scan_step, jnp.zeros((TOKENS, D), jnp.float32), jnp.arange(EXPERTS, dtype=jnp.int32))
    mixed = summed.astype(jnp.bfloat16)
    token_score = jnp.dot(mixed.astype(jnp.float32), score_head, precision=lax.Precision.HIGHEST)
    seq_score = token_score.reshape(SEQS, SEQ_LEN).sum(axis=1)
    partner = jnp.roll(seq_score, SEQS // 2)
    pair_score = jnp.abs(seq_score - partner) + 0.5 * (seq_score + partner)
    return mixed, pair_score
```

```python
import jax
import jax.numpy as jnp
from jax import lax
from jax.sharding import Mesh
from jax.sharding import PartitionSpec as P

SEQ_LEN = 16
MOST = 24


def from_partner(block, axis, bit):
    count = lax.axis_size(axis)
    route = []
    for low in range(count):
        high = low | 1 << bit
        if high != low and high < count:
            route += [(low, high), (high, low)]
    return lax.ppermute(block, axis, route)


def route_ranks(expert_ids, expert_total):
    flat_ids = expert_ids.reshape(-1)
    entry_count = flat_ids.shape[0]
    onehot = flat_ids[:, None] == jnp.arange(expert_total, dtype=jnp.int32)[None, :]
    positions = jnp.arange(entry_count, dtype=jnp.int32)
    earlier = (positions[:, None] > positions[None, :]).astype(jnp.bfloat16)
    counts = jnp.dot(earlier, onehot.astype(jnp.bfloat16), preferred_element_type=jnp.float32)
    rank_in = jnp.sum(jnp.where(onehot, counts, 0.0), axis=1).astype(jnp.int32)
    return rank_in.reshape(expert_ids.shape)


def gather_expert(block):
    along_z = lax.all_gather(block, "z", axis=0, tiled=False)
    return lax.all_gather(along_z, "c", axis=0, tiled=False)


def body(
    tokens, expert_ids, gate_fixed, scorer_id, direction_tags, w_gate, w_up, w_down, score_head
):
    z_count = lax.axis_size("z")
    c_count = lax.axis_size("c")
    expert_count = z_count * c_count
    per_device = w_gate.shape[0]
    tok_rows, model_width = tokens.shape
    top_count = expert_ids.shape[1]
    which_tag = jnp.repeat(scorer_id, SEQ_LEN)[:, None]
    tag_rows = jnp.where(
        which_tag == 1, direction_tags[1][None, :], direction_tags[0][None, :]
    ).astype(jnp.float32)
    inputs = (tokens.astype(jnp.float32) + tag_rows).astype(jnp.bfloat16)
    rank_in = route_ranks(expert_ids, per_device * expert_count)
    packed = jnp.concatenate([expert_ids, gate_fixed, rank_in], axis=1)
    inputs_all = gather_expert(inputs).reshape(expert_count, tok_rows, model_width)
    packed_all = gather_expert(packed).reshape(expert_count, tok_rows, 3 * top_count)
    ids_cube = packed_all[..., :top_count]
    fixed_val = packed_all[..., top_count : 2 * top_count].astype(jnp.float32)
    rank_cube = packed_all[..., 2 * top_count :]
    weight_cube = fixed_val / jnp.sum(fixed_val, axis=2, keepdims=True)
    my_index = lax.axis_index("z") * c_count + lax.axis_index("c")
    local_count = per_device * MOST
    local_slot = ids_cube - my_index * per_device
    is_mine = (local_slot >= 0) & (local_slot < per_device)
    local_key = jnp.where(is_mine, local_slot * MOST + rank_cube, -1)
    match = (
        local_key[:, None, :, :] == jnp.arange(local_count, dtype=jnp.int32)[None, :, None, None]
    )
    picker = jnp.any(match, axis=3).astype(jnp.bfloat16)
    slot_weight = jnp.sum(jnp.where(match, weight_cube[:, None, :, :], 0.0), axis=(2, 3)).reshape(
        expert_count, per_device, MOST
    )
    row_block = jnp.einsum(
        "sqt,std->sqd", picker, inputs_all, preferred_element_type=jnp.float32
    ).astype(jnp.bfloat16)
    row_block = row_block.reshape(expert_count, per_device, MOST, model_width)
    gate_proj = jnp.einsum("nemd,edf->nemf", row_block, w_gate, preferred_element_type=jnp.float32)
    up_proj = jnp.einsum("nemd,edf->nemf", row_block, w_up, preferred_element_type=jnp.float32)
    hidden = (jax.nn.silu(gate_proj) * up_proj).astype(jnp.bfloat16)
    down_out = jnp.einsum("nemf,efd->nemd", hidden, w_down, preferred_element_type=jnp.float32)
    result = (slot_weight[..., None] * down_out).astype(jnp.bfloat16)
    partial_value = jnp.einsum(
        "sqt,sqd->std",
        picker,
        result.reshape(expert_count, local_count, model_width),
        preferred_element_type=jnp.float32,
    )
    partial_value = partial_value.reshape(c_count, z_count * tok_rows, model_width)
    half = lax.psum_scatter(partial_value, "c", scatter_dimension=0, tiled=False)
    half = half.reshape(z_count, tok_rows, model_width).astype(jnp.bfloat16)
    summed = lax.psum_scatter(half, "z", scatter_dimension=0, tiled=False)
    mixed = summed.astype(jnp.bfloat16)
    token_score = jnp.dot(mixed.astype(jnp.float32), score_head, precision=lax.Precision.HIGHEST)
    seq_score = token_score.reshape(-1, SEQ_LEN).sum(axis=1)
    partner = from_partner(seq_score, "dp", lax.axis_size("dp").bit_length() - 2)
    pair_score = jnp.abs(seq_score - partner) + 0.5 * (seq_score + partner)
    return (mixed, pair_score)


def solution(mesh):
    dp_count, expert_count = mesh.devices.shape
    split = Mesh(mesh.devices.reshape(dp_count, expert_count // 2, 2), ("dp", "z", "c"))
    rows = P(("dp", "z", "c"), None)
    return jax.shard_map(
        body,
        mesh=split,
        in_specs=(
            rows,
            rows,
            rows,
            P(("dp", "z", "c")),
            P(),
            P(("z", "c"), None, None),
            P(("z", "c"), None, None),
            P(("z", "c"), None, None),
            P(),
        ),
        out_specs=(rows, P(("dp", "z", "c"))),
        check_vma=False,
    )
```

```python
import functools

import jax
import jax.numpy as jnp
from jax import lax
from jax.experimental import pallas as pl
from jax.experimental.pallas import tpu as pltpu
from jax.sharding import Mesh
from jax.sharding import PartitionSpec as P

SEQ_LEN = 16
MOST = 24


def from_partner(block, axis, bit):
    count = lax.axis_size(axis)
    route = []
    for low in range(count):
        high = low | 1 << bit
        if high != low and high < count:
            route += [(low, high), (high, low)]
    return lax.ppermute(block, axis, route)


def route_ranks(expert_ids, expert_total):
    flat_ids = expert_ids.reshape(-1)
    entry_count = flat_ids.shape[0]
    onehot = flat_ids[:, None] == jnp.arange(expert_total, dtype=jnp.int32)[None, :]
    positions = jnp.arange(entry_count, dtype=jnp.int32)
    earlier = (positions[:, None] > positions[None, :]).astype(jnp.bfloat16)
    counts = jnp.dot(earlier, onehot.astype(jnp.bfloat16), preferred_element_type=jnp.float32)
    rank_in = jnp.sum(jnp.where(onehot, counts, 0.0), axis=1).astype(jnp.int32)
    return rank_in.reshape(expert_ids.shape)


MESH = pl.DeviceIdType.MESH


def dispatch_kernel(z_count, blk_ref, out_ref, send_sem, recv_sem, local_sem):
    z = lax.axis_index("z")
    c = lax.axis_index("c")
    row = lax.axis_index("dp")
    other = 1 - c
    step = 1 - 2 * c
    fwd = lax.rem(z + step + z_count, z_count)
    bwd = lax.rem(z - step + z_count, z_count)
    fwd_id, bwd_id, pair_id = (row, fwd, c), (row, bwd, c), (row, z, other)

    barrier = pltpu.get_barrier_semaphore()
    for target in (fwd_id, bwd_id, pair_id):
        pl.semaphore_signal(barrier, 1, device_id=target, device_id_type=MESH)
    pl.semaphore_wait(barrier, 3)

    mine = c * z_count + z
    local = pltpu.make_async_copy(blk_ref, out_ref.at[mine], local_sem.at[0])
    local.start()
    sends = []

    def send(src, slot, target):
        copy = pltpu.make_async_remote_copy(
            src_ref=src,
            dst_ref=out_ref.at[slot],
            send_sem=send_sem.at[len(sends)],
            recv_sem=recv_sem.at[slot],
            device_id=target,
            device_id_type=MESH,
        )
        copy.start()
        sends.append(copy)

    def arrive(slot):
        pltpu.make_async_remote_copy(
            src_ref=out_ref.at[slot],
            dst_ref=out_ref.at[slot],
            send_sem=send_sem.at[0],
            recv_sem=recv_sem.at[slot],
            device_id=pair_id,
            device_id_type=MESH,
        ).wait_recv()

    send(blk_ref, mine, fwd_id)
    send(blk_ref, mine, bwd_id)
    send(blk_ref, mine, pair_id)
    fwd_hops = z_count // 2
    bwd_hops = z_count - 1 - fwd_hops
    for hop in range(1, fwd_hops + 1):
        slot = c * z_count + lax.rem(z - step * hop + 2 * z_count, z_count)
        arrive(slot)
        if hop < fwd_hops:
            send(out_ref.at[slot], slot, fwd_id)
        send(out_ref.at[slot], slot, pair_id)
        if hop <= bwd_hops:
            slot = c * z_count + lax.rem(z + step * hop + 2 * z_count, z_count)
            arrive(slot)
            if hop < bwd_hops:
                send(out_ref.at[slot], slot, bwd_id)
            send(out_ref.at[slot], slot, pair_id)
    for zz in range(z_count):
        arrive(other * z_count + zz)
    local.wait()
    for copy in sends:
        copy.wait_send()


def gather_blocks(block, z_count):
    count = 2 * z_count
    return pl.pallas_call(
        functools.partial(dispatch_kernel, z_count),
        out_shape=jax.ShapeDtypeStruct((count,) + block.shape, block.dtype),
        in_specs=[pl.BlockSpec(memory_space=pl.ANY)],
        out_specs=pl.BlockSpec(memory_space=pl.ANY),
        scratch_shapes=[
            pltpu.SemaphoreType.DMA((count,)),
            pltpu.SemaphoreType.DMA((count,)),
            pltpu.SemaphoreType.DMA((1,)),
        ],
        compiler_params=pltpu.CompilerParams(collective_id=0, has_side_effects=True),
    )(block)


def gather_expert(block):
    along_z = lax.all_gather(block, "z", axis=0, tiled=False)
    return lax.all_gather(along_z, "c", axis=0, tiled=False)


def body(
    tokens, expert_ids, gate_fixed, scorer_id, direction_tags, w_gate, w_up, w_down, score_head
):
    z_count = lax.axis_size("z")
    c_count = lax.axis_size("c")
    expert_count = z_count * c_count
    per_device = w_gate.shape[0]
    tok_rows, model_width = tokens.shape
    top_count = expert_ids.shape[1]
    which_tag = jnp.repeat(scorer_id, SEQ_LEN)[:, None]
    tag_rows = jnp.where(
        which_tag == 1, direction_tags[1][None, :], direction_tags[0][None, :]
    ).astype(jnp.float32)
    inputs = (tokens.astype(jnp.float32) + tag_rows).astype(jnp.bfloat16)
    rank_in = route_ranks(expert_ids, per_device * expert_count)
    routes = jnp.concatenate(
        [expert_ids, rank_in, gate_fixed // 256, gate_fixed % 256], axis=1
    ).astype(jnp.bfloat16)
    block = jnp.concatenate([inputs, routes.reshape(-1, model_width)], axis=0)
    gathered = gather_blocks(block, z_count)
    inputs_all = gathered[:, :tok_rows, :]
    routes_all = gathered[:, tok_rows:, :].reshape(expert_count, tok_rows, 4 * top_count)
    routes_all = routes_all.astype(jnp.int32)
    ids_cube = routes_all[..., :top_count]
    rank_cube = routes_all[..., top_count : 2 * top_count]
    fixed_val = (
        routes_all[..., 2 * top_count : 3 * top_count] * 256 + routes_all[..., 3 * top_count :]
    ).astype(jnp.float32)
    weight_cube = fixed_val / jnp.sum(fixed_val, axis=2, keepdims=True)
    my_index = lax.axis_index("z") * c_count + lax.axis_index("c")
    local_count = per_device * MOST
    local_slot = ids_cube - my_index * per_device
    is_mine = (local_slot >= 0) & (local_slot < per_device)
    local_key = jnp.where(is_mine, local_slot * MOST + rank_cube, -1)
    match = (
        local_key[:, None, :, :] == jnp.arange(local_count, dtype=jnp.int32)[None, :, None, None]
    )
    picker = jnp.any(match, axis=3).astype(jnp.bfloat16)
    slot_weight = jnp.sum(jnp.where(match, weight_cube[:, None, :, :], 0.0), axis=(2, 3)).reshape(
        expert_count, per_device, MOST
    )
    row_block = jnp.einsum(
        "sqt,std->sqd", picker, inputs_all, preferred_element_type=jnp.float32
    ).astype(jnp.bfloat16)
    row_block = row_block.reshape(expert_count, per_device, MOST, model_width)
    gate_proj = jnp.einsum("nemd,edf->nemf", row_block, w_gate, preferred_element_type=jnp.float32)
    up_proj = jnp.einsum("nemd,edf->nemf", row_block, w_up, preferred_element_type=jnp.float32)
    hidden = (jax.nn.silu(gate_proj) * up_proj).astype(jnp.bfloat16)
    down_out = jnp.einsum("nemf,efd->nemd", hidden, w_down, preferred_element_type=jnp.float32)
    result = (slot_weight[..., None] * down_out).astype(jnp.bfloat16)
    partial_value = jnp.einsum(
        "sqt,sqd->std",
        picker,
        result.reshape(expert_count, local_count, model_width),
        preferred_element_type=jnp.float32,
    )
    partial_value = partial_value.reshape(c_count, z_count * tok_rows, model_width)
    half = lax.psum_scatter(partial_value, "c", scatter_dimension=0, tiled=False)
    half = half.reshape(z_count, tok_rows, model_width).astype(jnp.bfloat16)
    summed = lax.psum_scatter(half, "z", scatter_dimension=0, tiled=False)
    mixed = summed.astype(jnp.bfloat16)
    token_score = jnp.dot(mixed.astype(jnp.float32), score_head, precision=lax.Precision.HIGHEST)
    seq_score = token_score.reshape(-1, SEQ_LEN).sum(axis=1)
    partner = from_partner(seq_score, "dp", lax.axis_size("dp").bit_length() - 2)
    pair_score = jnp.abs(seq_score - partner) + 0.5 * (seq_score + partner)
    return (mixed, pair_score)


def solution(mesh):
    dp_count, expert_count = mesh.devices.shape
    split = Mesh(mesh.devices.reshape(dp_count, expert_count // 2, 2), ("dp", "z", "c"))
    rows = P(("dp", "z", "c"), None)
    return jax.shard_map(
        body,
        mesh=split,
        in_specs=(
            rows,
            rows,
            rows,
            P(("dp", "z", "c")),
            P(),
            P(("z", "c"), None, None),
            P(("z", "c"), None, None),
            P(("z", "c"), None, None),
            P(),
        ),
        out_specs=(rows, P(("dp", "z", "c"))),
        check_vma=False,
    )
```

```python
import functools

import jax
import jax.numpy as jnp
from jax import lax
from jax.experimental import pallas as pl
from jax.experimental.pallas import tpu as pltpu
from jax.sharding import Mesh
from jax.sharding import PartitionSpec as P

SEQ_LEN = 16
MOST = 24


def from_partner(block, axis, bit):
    count = lax.axis_size(axis)
    route = []
    for low in range(count):
        high = low | 1 << bit
        if high != low and high < count:
            route += [(low, high), (high, low)]
    return lax.ppermute(block, axis, route)


def route_ranks(expert_ids, expert_total):
    flat_ids = expert_ids.reshape(-1)
    entry_count = flat_ids.shape[0]
    onehot = flat_ids[:, None] == jnp.arange(expert_total, dtype=jnp.int32)[None, :]
    positions = jnp.arange(entry_count, dtype=jnp.int32)
    earlier = (positions[:, None] > positions[None, :]).astype(jnp.bfloat16)
    counts = jnp.dot(earlier, onehot.astype(jnp.bfloat16), preferred_element_type=jnp.float32)
    rank_in = jnp.sum(jnp.where(onehot, counts, 0.0), axis=1).astype(jnp.int32)
    return rank_in.reshape(expert_ids.shape)


MESH = pl.DeviceIdType.MESH


def dispatch_kernel(z_count, blk_ref, out_ref, send_sem, recv_sem, local_sem):
    z = lax.axis_index("z")
    c = lax.axis_index("c")
    row = lax.axis_index("dp")
    other = 1 - c
    step = 1 - 2 * c
    fwd = lax.rem(z + step + z_count, z_count)
    bwd = lax.rem(z - step + z_count, z_count)
    fwd_id, bwd_id, pair_id = (row, fwd, c), (row, bwd, c), (row, z, other)

    barrier = pltpu.get_barrier_semaphore()
    for target in (fwd_id, bwd_id, pair_id):
        pl.semaphore_signal(barrier, 1, device_id=target, device_id_type=MESH)
    pl.semaphore_wait(barrier, 3)

    mine = c * z_count + z
    local = pltpu.make_async_copy(blk_ref, out_ref.at[mine], local_sem.at[0])
    local.start()
    sends = []

    def send(src, slot, target):
        copy = pltpu.make_async_remote_copy(
            src_ref=src,
            dst_ref=out_ref.at[slot],
            send_sem=send_sem.at[len(sends)],
            recv_sem=recv_sem.at[slot],
            device_id=target,
            device_id_type=MESH,
        )
        copy.start()
        sends.append(copy)

    def arrive(slot):
        pltpu.make_async_remote_copy(
            src_ref=out_ref.at[slot],
            dst_ref=out_ref.at[slot],
            send_sem=send_sem.at[0],
            recv_sem=recv_sem.at[slot],
            device_id=pair_id,
            device_id_type=MESH,
        ).wait_recv()

    send(blk_ref, mine, fwd_id)
    send(blk_ref, mine, bwd_id)
    send(blk_ref, mine, pair_id)
    fwd_hops = z_count // 2
    bwd_hops = z_count - 1 - fwd_hops
    for hop in range(1, fwd_hops + 1):
        slot = c * z_count + lax.rem(z - step * hop + 2 * z_count, z_count)
        arrive(slot)
        if hop < fwd_hops:
            send(out_ref.at[slot], slot, fwd_id)
        send(out_ref.at[slot], slot, pair_id)
        if hop <= bwd_hops:
            slot = c * z_count + lax.rem(z + step * hop + 2 * z_count, z_count)
            arrive(slot)
            if hop < bwd_hops:
                send(out_ref.at[slot], slot, bwd_id)
            send(out_ref.at[slot], slot, pair_id)
    for zz in range(z_count):
        arrive(other * z_count + zz)
    local.wait()
    for copy in sends:
        copy.wait_send()


def gather_blocks(block, z_count):
    count = 2 * z_count
    return pl.pallas_call(
        functools.partial(dispatch_kernel, z_count),
        out_shape=jax.ShapeDtypeStruct((count,) + block.shape, block.dtype),
        in_specs=[pl.BlockSpec(memory_space=pl.ANY)],
        out_specs=pl.BlockSpec(memory_space=pl.ANY),
        scratch_shapes=[
            pltpu.SemaphoreType.DMA((count,)),
            pltpu.SemaphoreType.DMA((count,)),
            pltpu.SemaphoreType.DMA((1,)),
        ],
        compiler_params=pltpu.CompilerParams(collective_id=0, has_side_effects=True),
    )(block)


def combine_kernel(
    z_count, part_ref, out_ref, pair_buf, fwd_buf, bwd_buf, fwd_out, bwd_out, send_sem, recv_sem
):
    z = lax.axis_index("z")
    c = lax.axis_index("c")
    row = lax.axis_index("dp")
    other = 1 - c
    step = 1 - 2 * c
    fwd = lax.rem(z + step + z_count, z_count)
    bwd = lax.rem(z - step + z_count, z_count)
    fwd_id, bwd_id, pair_id = (row, fwd, c), (row, bwd, c), (row, z, other)
    fwd_hops = z_count // 2
    bwd_hops = z_count - 1 - fwd_hops

    barrier = pltpu.get_barrier_semaphore()
    for target in (fwd_id, bwd_id, pair_id):
        pl.semaphore_signal(barrier, 1, device_id=target, device_id_type=MESH)
    pl.semaphore_wait(barrier, 3)

    sends = []

    def send(src, dst, sem, target):
        copy = pltpu.make_async_remote_copy(
            src_ref=src,
            dst_ref=dst,
            send_sem=send_sem.at[len(sends)],
            recv_sem=recv_sem.at[sem],
            device_id=target,
            device_id_type=MESH,
        )
        copy.start()
        sends.append(copy)

    def arrive(dst, sem):
        pltpu.make_async_remote_copy(
            src_ref=dst,
            dst_ref=dst,
            send_sem=send_sem.at[0],
            recv_sem=recv_sem.at[sem],
            device_id=pair_id,
            device_id_type=MESH,
        ).wait_recv()

    for zz in range(z_count):
        send(part_ref.at[other, zz], pair_buf.at[zz], zz, pair_id)

    def own(dest):
        arrive(pair_buf.at[dest], dest)
        return part_ref[c, dest].astype(jnp.float32) + pair_buf[dest].astype(jnp.float32)

    fwd_sem = z_count
    bwd_sem = z_count + fwd_hops
    for hop in range(1, fwd_hops + 1):
        dest = lax.rem(z + step * (fwd_hops + 1 - hop) + 2 * z_count, z_count)
        total = own(dest)
        if hop > 1:
            arrive(fwd_buf.at[hop - 2], fwd_sem + hop - 2)
            total = total + fwd_buf[hop - 2].astype(jnp.float32)
        fwd_out[hop - 1] = total.astype(fwd_out.dtype)
        send(fwd_out.at[hop - 1], fwd_buf.at[hop - 1], fwd_sem + hop - 1, fwd_id)
        if hop <= bwd_hops:
            dest = lax.rem(z - step * (bwd_hops + 1 - hop) + 2 * z_count, z_count)
            total = own(dest)
            if hop > 1:
                arrive(bwd_buf.at[hop - 2], bwd_sem + hop - 2)
                total = total + bwd_buf[hop - 2].astype(jnp.float32)
            bwd_out[hop - 1] = total.astype(bwd_out.dtype)
            send(bwd_out.at[hop - 1], bwd_buf.at[hop - 1], bwd_sem + hop - 1, bwd_id)
    total = own(z)
    arrive(fwd_buf.at[fwd_hops - 1], fwd_sem + fwd_hops - 1)
    total = total + fwd_buf[fwd_hops - 1].astype(jnp.float32)
    if bwd_hops > 0:
        arrive(bwd_buf.at[bwd_hops - 1], bwd_sem + bwd_hops - 1)
        total = total + bwd_buf[bwd_hops - 1].astype(jnp.float32)
    out_ref[...] = total.astype(out_ref.dtype)
    for copy in sends:
        copy.wait_send()


def scatter_sums(partial):
    c_count, z_count, rows, width = partial.shape
    fwd_hops = z_count // 2
    bwd_hops = max(z_count - 1 - fwd_hops, 1)
    block = (rows, width)
    vmem = pl.BlockSpec(memory_space=pltpu.VMEM)
    return pl.pallas_call(
        functools.partial(combine_kernel, z_count),
        out_shape=jax.ShapeDtypeStruct(block, partial.dtype),
        in_specs=[vmem],
        out_specs=vmem,
        scratch_shapes=[
            pltpu.VMEM((z_count,) + block, partial.dtype),
            pltpu.VMEM((fwd_hops,) + block, partial.dtype),
            pltpu.VMEM((bwd_hops,) + block, partial.dtype),
            pltpu.VMEM((fwd_hops,) + block, partial.dtype),
            pltpu.VMEM((bwd_hops,) + block, partial.dtype),
            pltpu.SemaphoreType.DMA((2 * z_count,)),
            pltpu.SemaphoreType.DMA((2 * z_count,)),
        ],
        compiler_params=pltpu.CompilerParams(
            collective_id=1, has_side_effects=True, vmem_limit_bytes=48 * 1024 * 1024
        ),
    )(partial)


def body(
    tokens, expert_ids, gate_fixed, scorer_id, direction_tags, w_gate, w_up, w_down, score_head
):
    z_count = lax.axis_size("z")
    c_count = lax.axis_size("c")
    expert_count = z_count * c_count
    per_device = w_gate.shape[0]
    tok_rows, model_width = tokens.shape
    top_count = expert_ids.shape[1]
    which_tag = jnp.repeat(scorer_id, SEQ_LEN)[:, None]
    tag_rows = jnp.where(
        which_tag == 1, direction_tags[1][None, :], direction_tags[0][None, :]
    ).astype(jnp.float32)
    inputs = (tokens.astype(jnp.float32) + tag_rows).astype(jnp.bfloat16)
    rank_in = route_ranks(expert_ids, per_device * expert_count)
    routes = jnp.concatenate(
        [expert_ids, rank_in, gate_fixed // 256, gate_fixed % 256], axis=1
    ).astype(jnp.bfloat16)
    block = jnp.concatenate([inputs, routes.reshape(-1, model_width)], axis=0)
    gathered = gather_blocks(block, z_count)
    inputs_all = gathered[:, :tok_rows, :]
    routes_all = gathered[:, tok_rows:, :].reshape(expert_count, tok_rows, 4 * top_count)
    routes_all = routes_all.astype(jnp.int32)
    ids_cube = routes_all[..., :top_count]
    rank_cube = routes_all[..., top_count : 2 * top_count]
    fixed_val = (
        routes_all[..., 2 * top_count : 3 * top_count] * 256 + routes_all[..., 3 * top_count :]
    ).astype(jnp.float32)
    weight_cube = fixed_val / jnp.sum(fixed_val, axis=2, keepdims=True)
    my_index = lax.axis_index("z") * c_count + lax.axis_index("c")
    local_count = per_device * MOST
    local_slot = ids_cube - my_index * per_device
    is_mine = (local_slot >= 0) & (local_slot < per_device)
    local_key = jnp.where(is_mine, local_slot * MOST + rank_cube, -1)
    match = (
        local_key[:, None, :, :] == jnp.arange(local_count, dtype=jnp.int32)[None, :, None, None]
    )
    picker = jnp.any(match, axis=3).astype(jnp.bfloat16)
    slot_weight = jnp.sum(jnp.where(match, weight_cube[:, None, :, :], 0.0), axis=(2, 3)).reshape(
        expert_count, per_device, MOST
    )
    row_block = jnp.einsum(
        "sqt,std->sqd", picker, inputs_all, preferred_element_type=jnp.float32
    ).astype(jnp.bfloat16)
    row_block = row_block.reshape(expert_count, per_device, MOST, model_width)
    gate_proj = jnp.einsum("nemd,edf->nemf", row_block, w_gate, preferred_element_type=jnp.float32)
    up_proj = jnp.einsum("nemd,edf->nemf", row_block, w_up, preferred_element_type=jnp.float32)
    hidden = (jax.nn.silu(gate_proj) * up_proj).astype(jnp.bfloat16)
    down_out = jnp.einsum("nemf,efd->nemd", hidden, w_down, preferred_element_type=jnp.float32)
    result = (slot_weight[..., None] * down_out).astype(jnp.bfloat16)
    partial_value = jnp.einsum(
        "sqt,sqd->std",
        picker,
        result.reshape(expert_count, local_count, model_width),
        preferred_element_type=jnp.float32,
    )
    partial_value = partial_value.reshape(c_count, z_count, tok_rows, model_width)
    mixed = scatter_sums(partial_value.astype(jnp.bfloat16))
    token_score = jnp.dot(mixed.astype(jnp.float32), score_head, precision=lax.Precision.HIGHEST)
    seq_score = token_score.reshape(-1, SEQ_LEN).sum(axis=1)
    partner = from_partner(seq_score, "dp", lax.axis_size("dp").bit_length() - 2)
    pair_score = jnp.abs(seq_score - partner) + 0.5 * (seq_score + partner)
    return (mixed, pair_score)


def solution(mesh):
    dp_count, expert_count = mesh.devices.shape
    split = Mesh(mesh.devices.reshape(dp_count, expert_count // 2, 2), ("dp", "z", "c"))
    rows = P(("dp", "z", "c"), None)
    return jax.shard_map(
        body,
        mesh=split,
        in_specs=(
            rows,
            rows,
            rows,
            P(("dp", "z", "c")),
            P(),
            P(("z", "c"), None, None),
            P(("z", "c"), None, None),
            P(("z", "c"), None, None),
            P(),
        ),
        out_specs=(rows, P(("dp", "z", "c"))),
        check_vma=False,
    )
```

```python
import functools

import jax
import jax.numpy as jnp
from jax import lax
from jax.experimental import pallas as pl
from jax.experimental.pallas import tpu as pltpu
from jax.sharding import Mesh
from jax.sharding import PartitionSpec as P

SEQ_LEN = 16
MOST = 24


def from_partner(block, axis, bit):
    count = lax.axis_size(axis)
    route = []
    for low in range(count):
        high = low | 1 << bit
        if high != low and high < count:
            route += [(low, high), (high, low)]
    return lax.ppermute(block, axis, route)


def route_ranks(expert_ids, expert_total):
    flat_ids = expert_ids.reshape(-1)
    entry_count = flat_ids.shape[0]
    onehot = flat_ids[:, None] == jnp.arange(expert_total, dtype=jnp.int32)[None, :]
    positions = jnp.arange(entry_count, dtype=jnp.int32)
    earlier = (positions[:, None] > positions[None, :]).astype(jnp.bfloat16)
    counts = jnp.dot(earlier, onehot.astype(jnp.bfloat16), preferred_element_type=jnp.float32)
    rank_in = jnp.sum(jnp.where(onehot, counts, 0.0), axis=1).astype(jnp.int32)
    return rank_in.reshape(expert_ids.shape)


MESH = pl.DeviceIdType.MESH


def dispatch_kernel(z_count, chunks, blk_ref, out_ref, send_sem, recv_sem, local_sem):
    z = lax.axis_index("z")
    c = lax.axis_index("c")
    row = lax.axis_index("dp")
    other = 1 - c
    step = 1 - 2 * c
    fwd = lax.rem(z + step + z_count, z_count)
    bwd = lax.rem(z - step + z_count, z_count)
    fwd_id, bwd_id, pair_id = (row, fwd, c), (row, bwd, c), (row, z, other)
    piece = blk_ref.shape[0] // chunks

    barrier = pltpu.get_barrier_semaphore()
    for target in (fwd_id, bwd_id, pair_id):
        pl.semaphore_signal(barrier, 1, device_id=target, device_id_type=MESH)
    pl.semaphore_wait(barrier, 3)

    mine = c * z_count + z
    local = pltpu.make_async_copy(blk_ref, out_ref.at[mine], local_sem.at[0])
    local.start()
    sends = []

    def part(ref, k):
        return ref.at[pl.ds(k * piece, piece)]

    def send(src, slot, k, target):
        copy = pltpu.make_async_remote_copy(
            src_ref=part(src, k),
            dst_ref=part(out_ref.at[slot], k),
            send_sem=send_sem.at[len(sends)],
            recv_sem=recv_sem.at[slot * chunks + k],
            device_id=target,
            device_id_type=MESH,
        )
        copy.start()
        sends.append(copy)

    def arrive(slot, k):
        view = part(out_ref.at[slot], k)
        pltpu.make_async_remote_copy(
            src_ref=view,
            dst_ref=view,
            send_sem=send_sem.at[0],
            recv_sem=recv_sem.at[slot * chunks + k],
            device_id=pair_id,
            device_id_type=MESH,
        ).wait_recv()

    for k in range(chunks):
        send(blk_ref, mine, k, fwd_id)
        send(blk_ref, mine, k, bwd_id)
    for k in range(chunks):
        send(blk_ref, mine, k, pair_id)
    fwd_hops = z_count // 2
    bwd_hops = z_count - 1 - fwd_hops
    for hop in range(1, fwd_hops + 1):
        for k in range(chunks):
            slot = c * z_count + lax.rem(z - step * hop + 2 * z_count, z_count)
            arrive(slot, k)
            if hop < fwd_hops:
                send(out_ref.at[slot], slot, k, fwd_id)
            send(out_ref.at[slot], slot, k, pair_id)
            if hop <= bwd_hops:
                slot = c * z_count + lax.rem(z + step * hop + 2 * z_count, z_count)
                arrive(slot, k)
                if hop < bwd_hops:
                    send(out_ref.at[slot], slot, k, bwd_id)
                send(out_ref.at[slot], slot, k, pair_id)
    for zz in range(z_count):
        for k in range(chunks):
            arrive(other * z_count + zz, k)
    local.wait()
    for copy in sends:
        copy.wait_send()


def gather_blocks(block, z_count, chunks):
    count = 2 * z_count
    return pl.pallas_call(
        functools.partial(dispatch_kernel, z_count, chunks),
        out_shape=jax.ShapeDtypeStruct((count,) + block.shape, block.dtype),
        in_specs=[pl.BlockSpec(memory_space=pl.ANY)],
        out_specs=pl.BlockSpec(memory_space=pl.ANY),
        scratch_shapes=[
            pltpu.SemaphoreType.DMA((2 * count * chunks,)),
            pltpu.SemaphoreType.DMA((count * chunks,)),
            pltpu.SemaphoreType.DMA((1,)),
        ],
        compiler_params=pltpu.CompilerParams(collective_id=0, has_side_effects=True),
    )(block)


def combine_kernel(
    z_count, chunks, part_ref, out_ref, pair_buf, fwd_buf, bwd_buf, fwd_out, bwd_out,
    send_sem, recv_sem,
):
    z = lax.axis_index("z")
    c = lax.axis_index("c")
    row = lax.axis_index("dp")
    other = 1 - c
    step = 1 - 2 * c
    fwd = lax.rem(z + step + z_count, z_count)
    bwd = lax.rem(z - step + z_count, z_count)
    fwd_id, bwd_id, pair_id = (row, fwd, c), (row, bwd, c), (row, z, other)
    fwd_hops = z_count // 2
    bwd_hops = z_count - 1 - fwd_hops
    piece = part_ref.shape[2] // chunks

    barrier = pltpu.get_barrier_semaphore()
    for target in (fwd_id, bwd_id, pair_id):
        pl.semaphore_signal(barrier, 1, device_id=target, device_id_type=MESH)
    pl.semaphore_wait(barrier, 3)

    sends = []

    def send(src, dst, sem, target):
        copy = pltpu.make_async_remote_copy(
            src_ref=src,
            dst_ref=dst,
            send_sem=send_sem.at[len(sends)],
            recv_sem=recv_sem.at[sem],
            device_id=target,
            device_id_type=MESH,
        )
        copy.start()
        sends.append(copy)

    def arrive(dst, sem):
        pltpu.make_async_remote_copy(
            src_ref=dst,
            dst_ref=dst,
            send_sem=send_sem.at[0],
            recv_sem=recv_sem.at[sem],
            device_id=pair_id,
            device_id_type=MESH,
        ).wait_recv()

    def order(ring_step):
        dests = []
        for hop in range(1, fwd_hops + 1):
            dests.append(lax.rem(z + ring_step * (fwd_hops + 1 - hop) + 2 * z_count, z_count))
            if hop <= bwd_hops:
                dests.append(lax.rem(z - ring_step * (bwd_hops + 1 - hop) + 2 * z_count, z_count))
        return dests + [z]

    for n, dest in enumerate(order(-step)):
        send(part_ref.at[other, dest], pair_buf.at[n], n, pair_id)
    def own(dest, n, k):
        if k == 0:
            arrive(pair_buf.at[n], n)
        rows = pl.ds(k * piece, piece)
        return part_ref[c, dest, rows].astype(jnp.float32) + pair_buf[n, rows].astype(
            jnp.float32
        )

    fwd_sem = z_count
    bwd_sem = z_count + fwd_hops * chunks
    for hop in range(1, fwd_hops + 1):
        for k in range(chunks):
            rows = pl.ds(k * piece, piece)
            dest = lax.rem(z + step * (fwd_hops + 1 - hop) + 2 * z_count, z_count)
            n = hop - 1 + min(hop - 1, bwd_hops)
            total = own(dest, n, k)
            if hop > 1:
                sem = fwd_sem + (hop - 2) * chunks + k
                arrive(fwd_buf.at[hop - 2, rows], sem)
                total = total + fwd_buf[hop - 2, rows].astype(jnp.float32)
            fwd_out[hop - 1, rows] = total.astype(fwd_out.dtype)
            sem = fwd_sem + (hop - 1) * chunks + k
            send(fwd_out.at[hop - 1, rows], fwd_buf.at[hop - 1, rows], sem, fwd_id)
            if hop <= bwd_hops:
                dest = lax.rem(z - step * (bwd_hops + 1 - hop) + 2 * z_count, z_count)
                total = own(dest, n + 1, k)
                if hop > 1:
                    sem = bwd_sem + (hop - 2) * chunks + k
                    arrive(bwd_buf.at[hop - 2, rows], sem)
                    total = total + bwd_buf[hop - 2, rows].astype(jnp.float32)
                bwd_out[hop - 1, rows] = total.astype(bwd_out.dtype)
                sem = bwd_sem + (hop - 1) * chunks + k
                send(bwd_out.at[hop - 1, rows], bwd_buf.at[hop - 1, rows], sem, bwd_id)
    for k in range(chunks):
        rows = pl.ds(k * piece, piece)
        total = own(z, fwd_hops + bwd_hops, k)
        arrive(fwd_buf.at[fwd_hops - 1, rows], fwd_sem + (fwd_hops - 1) * chunks + k)
        total = total + fwd_buf[fwd_hops - 1, rows].astype(jnp.float32)
        if bwd_hops > 0:
            arrive(bwd_buf.at[bwd_hops - 1, rows], bwd_sem + (bwd_hops - 1) * chunks + k)
            total = total + bwd_buf[bwd_hops - 1, rows].astype(jnp.float32)
        out_ref[rows] = total.astype(out_ref.dtype)
    for copy in sends:
        copy.wait_send()


def scatter_sums(partial, chunks):
    c_count, z_count, rows, width = partial.shape
    fwd_hops = z_count // 2
    bwd_hops = max(z_count - 1 - fwd_hops, 1)
    block = (rows, width)
    vmem = pl.BlockSpec(memory_space=pltpu.VMEM)
    sems = z_count + (fwd_hops + bwd_hops) * chunks
    return pl.pallas_call(
        functools.partial(combine_kernel, z_count, chunks),
        out_shape=jax.ShapeDtypeStruct(block, partial.dtype),
        in_specs=[vmem],
        out_specs=vmem,
        scratch_shapes=[
            pltpu.VMEM((z_count,) + block, partial.dtype),
            pltpu.VMEM((fwd_hops,) + block, partial.dtype),
            pltpu.VMEM((bwd_hops,) + block, partial.dtype),
            pltpu.VMEM((fwd_hops,) + block, partial.dtype),
            pltpu.VMEM((bwd_hops,) + block, partial.dtype),
            pltpu.SemaphoreType.DMA((sems,)),
            pltpu.SemaphoreType.DMA((sems,)),
        ],
        compiler_params=pltpu.CompilerParams(
            collective_id=1, has_side_effects=True, vmem_limit_bytes=48 * 1024 * 1024
        ),
    )(partial)


def body(
    tokens, expert_ids, gate_fixed, scorer_id, direction_tags, w_gate, w_up, w_down, score_head
):
    z_count = lax.axis_size("z")
    c_count = lax.axis_size("c")
    expert_count = z_count * c_count
    per_device = w_gate.shape[0]
    tok_rows, model_width = tokens.shape
    top_count = expert_ids.shape[1]
    which_tag = jnp.repeat(scorer_id, SEQ_LEN)[:, None]
    tag_rows = jnp.where(
        which_tag == 1, direction_tags[1][None, :], direction_tags[0][None, :]
    ).astype(jnp.float32)
    inputs = (tokens.astype(jnp.float32) + tag_rows).astype(jnp.bfloat16)
    rank_in = route_ranks(expert_ids, per_device * expert_count)
    routes = jnp.concatenate(
        [expert_ids, rank_in, gate_fixed // 256, gate_fixed % 256], axis=1
    ).astype(jnp.bfloat16)
    routes = jnp.pad(routes, ((0, 0), (0, 128 - 4 * top_count)))
    block = jnp.concatenate([inputs, routes], axis=1)
    gathered = gather_blocks(block, z_count, 2)
    inputs_all = gathered[:, :, :model_width]
    routes_all = gathered[:, :, model_width : model_width + 4 * top_count].astype(jnp.int32)
    ids_cube = routes_all[..., :top_count]
    rank_cube = routes_all[..., top_count : 2 * top_count]
    fixed_val = (
        routes_all[..., 2 * top_count : 3 * top_count] * 256 + routes_all[..., 3 * top_count :]
    ).astype(jnp.float32)
    weight_cube = fixed_val / jnp.sum(fixed_val, axis=2, keepdims=True)
    my_index = lax.axis_index("z") * c_count + lax.axis_index("c")
    local_count = per_device * MOST
    local_slot = ids_cube - my_index * per_device
    is_mine = (local_slot >= 0) & (local_slot < per_device)
    local_key = jnp.where(is_mine, local_slot * MOST + rank_cube, -1)
    match = (
        local_key[:, None, :, :] == jnp.arange(local_count, dtype=jnp.int32)[None, :, None, None]
    )
    picker = jnp.any(match, axis=3).astype(jnp.bfloat16)
    slot_weight = jnp.sum(jnp.where(match, weight_cube[:, None, :, :], 0.0), axis=(2, 3)).reshape(
        expert_count, per_device, MOST
    )
    row_block = jnp.einsum(
        "sqt,std->sqd", picker, inputs_all, preferred_element_type=jnp.float32
    ).astype(jnp.bfloat16)
    row_block = row_block.reshape(expert_count, per_device, MOST, model_width)
    gate_proj = jnp.einsum("nemd,edf->nemf", row_block, w_gate, preferred_element_type=jnp.float32)
    up_proj = jnp.einsum("nemd,edf->nemf", row_block, w_up, preferred_element_type=jnp.float32)
    hidden = (jax.nn.silu(gate_proj) * up_proj).astype(jnp.bfloat16)
    down_out = jnp.einsum("nemf,efd->nemd", hidden, w_down, preferred_element_type=jnp.float32)
    result = (slot_weight[..., None] * down_out).astype(jnp.bfloat16)
    partial_value = jnp.einsum(
        "sqt,sqd->std",
        picker,
        result.reshape(expert_count, local_count, model_width),
        preferred_element_type=jnp.float32,
    )
    partial_value = partial_value.reshape(c_count, z_count, tok_rows, model_width)
    mixed = scatter_sums(partial_value.astype(jnp.bfloat16), 2)
    token_score = jnp.dot(mixed.astype(jnp.float32), score_head, precision=lax.Precision.HIGHEST)
    seq_score = token_score.reshape(-1, SEQ_LEN).sum(axis=1)
    partner = from_partner(seq_score, "dp", lax.axis_size("dp").bit_length() - 2)
    pair_score = jnp.abs(seq_score - partner) + 0.5 * (seq_score + partner)
    return (mixed, pair_score)


def solution(mesh):
    dp_count, expert_count = mesh.devices.shape
    split = Mesh(mesh.devices.reshape(dp_count, expert_count // 2, 2), ("dp", "z", "c"))
    rows = P(("dp", "z", "c"), None)
    return jax.shard_map(
        body,
        mesh=split,
        in_specs=(
            rows,
            rows,
            rows,
            P(("dp", "z", "c")),
            P(),
            P(("z", "c"), None, None),
            P(("z", "c"), None, None),
            P(("z", "c"), None, None),
            P(),
        ),
        out_specs=(rows, P(("dp", "z", "c"))),
        check_vma=False,
    )
```

```python
import functools

import jax
import jax.numpy as jnp
from jax import lax
from jax.experimental import pallas as pl
from jax.experimental.pallas import tpu as pltpu
from jax.sharding import Mesh
from jax.sharding import PartitionSpec as P

SEQ_LEN = 16
MOST = 24


def from_partner(block, axis, bit):
    count = lax.axis_size(axis)
    route = []
    for low in range(count):
        high = low | 1 << bit
        if high != low and high < count:
            route += [(low, high), (high, low)]
    return lax.ppermute(block, axis, route)


def route_ranks(expert_ids, expert_total):
    flat_ids = expert_ids.reshape(-1)
    entry_count = flat_ids.shape[0]
    onehot = flat_ids[:, None] == jnp.arange(expert_total, dtype=jnp.int32)[None, :]
    positions = jnp.arange(entry_count, dtype=jnp.int32)
    earlier = (positions[:, None] > positions[None, :]).astype(jnp.bfloat16)
    counts = jnp.dot(earlier, onehot.astype(jnp.bfloat16), preferred_element_type=jnp.float32)
    rank_in = jnp.sum(jnp.where(onehot, counts, 0.0), axis=1).astype(jnp.int32)
    return rank_in.reshape(expert_ids.shape)


MESH = pl.DeviceIdType.MESH


def dispatch_kernel(z_count, chunks, blk_ref, out_ref, send_sem, recv_sem, local_sem):
    z = lax.axis_index("z")
    c = lax.axis_index("c")
    row = lax.axis_index("dp")
    other = 1 - c
    step = 1 - 2 * c
    fwd = lax.rem(z + step + z_count, z_count)
    bwd = lax.rem(z - step + z_count, z_count)
    fwd_id, bwd_id, pair_id = (row, fwd, c), (row, bwd, c), (row, z, other)
    piece = blk_ref.shape[0] // chunks

    barrier = pltpu.get_barrier_semaphore()
    for target in (fwd_id, bwd_id, pair_id):
        pl.semaphore_signal(barrier, 1, device_id=target, device_id_type=MESH)
    pl.semaphore_wait(barrier, 3)

    mine = c * z_count + z
    local = pltpu.make_async_copy(blk_ref, out_ref.at[mine], local_sem.at[0])
    local.start()
    sends = []

    def part(ref, k):
        return ref.at[pl.ds(k * piece, piece)]

    def send(src, slot, k, target):
        copy = pltpu.make_async_remote_copy(
            src_ref=part(src, k),
            dst_ref=part(out_ref.at[slot], k),
            send_sem=send_sem.at[len(sends)],
            recv_sem=recv_sem.at[slot * chunks + k],
            device_id=target,
            device_id_type=MESH,
        )
        copy.start()
        sends.append(copy)

    def arrive(slot, k):
        view = part(out_ref.at[slot], k)
        pltpu.make_async_remote_copy(
            src_ref=view,
            dst_ref=view,
            send_sem=send_sem.at[0],
            recv_sem=recv_sem.at[slot * chunks + k],
            device_id=pair_id,
            device_id_type=MESH,
        ).wait_recv()

    for k in range(chunks):
        send(blk_ref, mine, k, fwd_id)
        send(blk_ref, mine, k, bwd_id)
    for k in range(chunks):
        send(blk_ref, mine, k, pair_id)
    fwd_hops = z_count // 2
    bwd_hops = z_count - 1 - fwd_hops
    for hop in range(1, fwd_hops + 1):
        for k in range(chunks):
            slot = c * z_count + lax.rem(z - step * hop + 2 * z_count, z_count)
            arrive(slot, k)
            if hop < fwd_hops:
                send(out_ref.at[slot], slot, k, fwd_id)
            send(out_ref.at[slot], slot, k, pair_id)
            if hop <= bwd_hops:
                slot = c * z_count + lax.rem(z + step * hop + 2 * z_count, z_count)
                arrive(slot, k)
                if hop < bwd_hops:
                    send(out_ref.at[slot], slot, k, bwd_id)
                send(out_ref.at[slot], slot, k, pair_id)
    for zz in range(z_count):
        for k in range(chunks):
            arrive(other * z_count + zz, k)
    local.wait()
    for copy in sends:
        copy.wait_send()


def gather_blocks(block, z_count, chunks):
    count = 2 * z_count
    return pl.pallas_call(
        functools.partial(dispatch_kernel, z_count, chunks),
        out_shape=jax.ShapeDtypeStruct((count,) + block.shape, block.dtype),
        in_specs=[pl.BlockSpec(memory_space=pl.ANY)],
        out_specs=pl.BlockSpec(memory_space=pl.ANY),
        scratch_shapes=[
            pltpu.SemaphoreType.DMA((2 * count * chunks,)),
            pltpu.SemaphoreType.DMA((count * chunks,)),
            pltpu.SemaphoreType.DMA((1,)),
        ],
        compiler_params=pltpu.CompilerParams(collective_id=0, has_side_effects=True),
    )(block)


def combine_kernel(
    z_count, chunks, part_ref, out_ref, pair_buf, fwd_buf, bwd_buf, fwd_out, bwd_out,
    send_sem, recv_sem,
):
    z = lax.axis_index("z")
    c = lax.axis_index("c")
    row = lax.axis_index("dp")
    other = 1 - c
    step = 1 - 2 * c
    fwd = lax.rem(z + step + z_count, z_count)
    bwd = lax.rem(z - step + z_count, z_count)
    fwd_id, bwd_id, pair_id = (row, fwd, c), (row, bwd, c), (row, z, other)
    fwd_hops = z_count // 2
    bwd_hops = z_count - 1 - fwd_hops
    piece = part_ref.shape[2] // chunks

    barrier = pltpu.get_barrier_semaphore()
    for target in (fwd_id, bwd_id, pair_id):
        pl.semaphore_signal(barrier, 1, device_id=target, device_id_type=MESH)
    pl.semaphore_wait(barrier, 3)

    sends = []

    def send(src, dst, sem, target):
        copy = pltpu.make_async_remote_copy(
            src_ref=src,
            dst_ref=dst,
            send_sem=send_sem.at[len(sends)],
            recv_sem=recv_sem.at[sem],
            device_id=target,
            device_id_type=MESH,
        )
        copy.start()
        sends.append(copy)

    def arrive(dst, sem):
        pltpu.make_async_remote_copy(
            src_ref=dst,
            dst_ref=dst,
            send_sem=send_sem.at[0],
            recv_sem=recv_sem.at[sem],
            device_id=pair_id,
            device_id_type=MESH,
        ).wait_recv()

    def order(ring_step):
        dests = []
        for hop in range(1, fwd_hops + 1):
            dests.append(lax.rem(z + ring_step * (fwd_hops + 1 - hop) + 2 * z_count, z_count))
            if hop <= bwd_hops:
                dests.append(lax.rem(z - ring_step * (bwd_hops + 1 - hop) + 2 * z_count, z_count))
        return dests + [z]

    for n, dest in enumerate(order(-step)):
        send(part_ref.at[other, dest], pair_buf.at[n], n, pair_id)
    def own(dest, n, k):
        if k == 0:
            arrive(pair_buf.at[n], n)
        rows = pl.ds(k * piece, piece)
        return part_ref[c, dest, rows].astype(jnp.float32) + pair_buf[n, rows].astype(
            jnp.float32
        )

    fwd_sem = z_count
    bwd_sem = z_count + fwd_hops * chunks
    for hop in range(1, fwd_hops + 1):
        for k in range(chunks):
            rows = pl.ds(k * piece, piece)
            dest = lax.rem(z + step * (fwd_hops + 1 - hop) + 2 * z_count, z_count)
            n = hop - 1 + min(hop - 1, bwd_hops)
            total = own(dest, n, k)
            if hop > 1:
                sem = fwd_sem + (hop - 2) * chunks + k
                arrive(fwd_buf.at[hop - 2, rows], sem)
                total = total + fwd_buf[hop - 2, rows].astype(jnp.float32)
            fwd_out[hop - 1, rows] = total.astype(fwd_out.dtype)
            sem = fwd_sem + (hop - 1) * chunks + k
            send(fwd_out.at[hop - 1, rows], fwd_buf.at[hop - 1, rows], sem, fwd_id)
            if hop <= bwd_hops:
                dest = lax.rem(z - step * (bwd_hops + 1 - hop) + 2 * z_count, z_count)
                total = own(dest, n + 1, k)
                if hop > 1:
                    sem = bwd_sem + (hop - 2) * chunks + k
                    arrive(bwd_buf.at[hop - 2, rows], sem)
                    total = total + bwd_buf[hop - 2, rows].astype(jnp.float32)
                bwd_out[hop - 1, rows] = total.astype(bwd_out.dtype)
                sem = bwd_sem + (hop - 1) * chunks + k
                send(bwd_out.at[hop - 1, rows], bwd_buf.at[hop - 1, rows], sem, bwd_id)
    for k in range(chunks):
        rows = pl.ds(k * piece, piece)
        total = own(z, fwd_hops + bwd_hops, k)
        arrive(fwd_buf.at[fwd_hops - 1, rows], fwd_sem + (fwd_hops - 1) * chunks + k)
        total = total + fwd_buf[fwd_hops - 1, rows].astype(jnp.float32)
        if bwd_hops > 0:
            arrive(bwd_buf.at[bwd_hops - 1, rows], bwd_sem + (bwd_hops - 1) * chunks + k)
            total = total + bwd_buf[bwd_hops - 1, rows].astype(jnp.float32)
        out_ref[rows] = total.astype(out_ref.dtype)
    for copy in sends:
        copy.wait_send()


def scatter_sums(partial, chunks):
    c_count, z_count, rows, width = partial.shape
    fwd_hops = z_count // 2
    bwd_hops = max(z_count - 1 - fwd_hops, 1)
    block = (rows, width)
    vmem = pl.BlockSpec(memory_space=pltpu.VMEM)
    sems = z_count + (fwd_hops + bwd_hops) * chunks
    return pl.pallas_call(
        functools.partial(combine_kernel, z_count, chunks),
        out_shape=jax.ShapeDtypeStruct(block, partial.dtype),
        in_specs=[vmem],
        out_specs=vmem,
        scratch_shapes=[
            pltpu.VMEM((z_count,) + block, partial.dtype),
            pltpu.VMEM((fwd_hops,) + block, partial.dtype),
            pltpu.VMEM((bwd_hops,) + block, partial.dtype),
            pltpu.VMEM((fwd_hops,) + block, partial.dtype),
            pltpu.VMEM((bwd_hops,) + block, partial.dtype),
            pltpu.SemaphoreType.DMA((sems,)),
            pltpu.SemaphoreType.DMA((sems,)),
        ],
        compiler_params=pltpu.CompilerParams(
            collective_id=1, has_side_effects=True, vmem_limit_bytes=48 * 1024 * 1024
        ),
    )(partial)


def body(
    tokens, expert_ids, gate_fixed, scorer_id, direction_tags, w_gate, w_up, w_down, score_head
):
    z_count = lax.axis_size("z")
    c_count = lax.axis_size("c")
    expert_count = z_count * c_count
    per_device = w_gate.shape[0]
    tok_rows, model_width = tokens.shape
    top_count = expert_ids.shape[1]
    which_tag = jnp.repeat(scorer_id, SEQ_LEN)[:, None]
    tag_rows = jnp.where(
        which_tag == 1, direction_tags[1][None, :], direction_tags[0][None, :]
    ).astype(jnp.float32)
    inputs = (tokens.astype(jnp.float32) + tag_rows).astype(jnp.bfloat16)
    rank_in = route_ranks(expert_ids, per_device * expert_count)
    routes = jnp.concatenate(
        [expert_ids, rank_in, gate_fixed // 256, gate_fixed % 256], axis=1
    ).astype(jnp.bfloat16)
    routes = jnp.pad(routes, ((0, 0), (0, 128 - 4 * top_count)))
    block = jnp.concatenate([inputs, routes], axis=1)
    gathered = gather_blocks(block, z_count, 4)
    inputs_all = gathered[:, :, :model_width]
    routes_all = gathered[:, :, model_width : model_width + 4 * top_count].astype(jnp.int32)
    ids_cube = routes_all[..., :top_count]
    rank_cube = routes_all[..., top_count : 2 * top_count]
    fixed_val = (
        routes_all[..., 2 * top_count : 3 * top_count] * 256 + routes_all[..., 3 * top_count :]
    ).astype(jnp.float32)
    weight_cube = fixed_val / jnp.sum(fixed_val, axis=2, keepdims=True)
    my_index = lax.axis_index("z") * c_count + lax.axis_index("c")
    local_count = per_device * MOST
    local_slot = ids_cube - my_index * per_device
    is_mine = (local_slot >= 0) & (local_slot < per_device)
    local_key = jnp.where(is_mine, local_slot * MOST + rank_cube, -1)
    match = (
        local_key[:, None, :, :] == jnp.arange(local_count, dtype=jnp.int32)[None, :, None, None]
    )
    picker = jnp.any(match, axis=3).astype(jnp.bfloat16)
    slot_weight = jnp.sum(jnp.where(match, weight_cube[:, None, :, :], 0.0), axis=(2, 3)).reshape(
        expert_count, per_device, MOST
    )
    row_block = jnp.einsum(
        "sqt,std->sqd", picker, inputs_all, preferred_element_type=jnp.float32
    ).astype(jnp.bfloat16)
    row_block = row_block.reshape(expert_count, per_device, MOST, model_width)
    gate_proj = jnp.einsum("nemd,edf->nemf", row_block, w_gate, preferred_element_type=jnp.float32)
    up_proj = jnp.einsum("nemd,edf->nemf", row_block, w_up, preferred_element_type=jnp.float32)
    hidden = (jax.nn.silu(gate_proj) * up_proj).astype(jnp.bfloat16)
    down_out = jnp.einsum("nemf,efd->nemd", hidden, w_down, preferred_element_type=jnp.float32)
    result = (slot_weight[..., None] * down_out).astype(jnp.bfloat16)
    partial_value = jnp.einsum(
        "sqt,sqd->std",
        picker,
        result.reshape(expert_count, local_count, model_width),
        preferred_element_type=jnp.float32,
    )
    partial_value = partial_value.reshape(c_count, z_count, tok_rows, model_width)
    mixed = scatter_sums(partial_value.astype(jnp.bfloat16), 4)
    token_score = jnp.dot(mixed.astype(jnp.float32), score_head, precision=lax.Precision.HIGHEST)
    seq_score = token_score.reshape(-1, SEQ_LEN).sum(axis=1)
    partner = from_partner(seq_score, "dp", lax.axis_size("dp").bit_length() - 2)
    pair_score = jnp.abs(seq_score - partner) + 0.5 * (seq_score + partner)
    return (mixed, pair_score)


def solution(mesh):
    dp_count, expert_count = mesh.devices.shape
    split = Mesh(mesh.devices.reshape(dp_count, expert_count // 2, 2), ("dp", "z", "c"))
    rows = P(("dp", "z", "c"), None)
    return jax.shard_map(
        body,
        mesh=split,
        in_specs=(
            rows,
            rows,
            rows,
            P(("dp", "z", "c")),
            P(),
            P(("z", "c"), None, None),
            P(("z", "c"), None, None),
            P(("z", "c"), None, None),
            P(),
        ),
        out_specs=(rows, P(("dp", "z", "c"))),
        check_vma=False,
    )
```

```python
import functools

import jax
import jax.numpy as jnp
from jax import lax
from jax.experimental import pallas as pl
from jax.experimental.pallas import tpu as pltpu
from jax.sharding import Mesh
from jax.sharding import PartitionSpec as P

SEQ_LEN = 16
MOST = 24


def from_partner(block, axis, bit):
    count = lax.axis_size(axis)
    route = []
    for low in range(count):
        high = low | 1 << bit
        if high != low and high < count:
            route += [(low, high), (high, low)]
    return lax.ppermute(block, axis, route)


def route_ranks(expert_ids, expert_total):
    flat_ids = expert_ids.reshape(-1)
    entry_count = flat_ids.shape[0]
    onehot = flat_ids[:, None] == jnp.arange(expert_total, dtype=jnp.int32)[None, :]
    positions = jnp.arange(entry_count, dtype=jnp.int32)
    earlier = (positions[:, None] > positions[None, :]).astype(jnp.bfloat16)
    counts = jnp.dot(earlier, onehot.astype(jnp.bfloat16), preferred_element_type=jnp.float32)
    rank_in = jnp.sum(jnp.where(onehot, counts, 0.0), axis=1).astype(jnp.int32)
    return rank_in.reshape(expert_ids.shape)


MESH = pl.DeviceIdType.MESH


def dispatch_kernel(z_count, chunks, blk_ref, out_ref, send_sem, recv_sem, local_sem):
    z = lax.axis_index("z")
    c = lax.axis_index("c")
    row = lax.axis_index("dp")
    other = 1 - c
    step = 1 - 2 * c
    fwd = lax.rem(z + step + z_count, z_count)
    bwd = lax.rem(z - step + z_count, z_count)
    fwd_id, bwd_id, pair_id = (row, fwd, c), (row, bwd, c), (row, z, other)
    piece = blk_ref.shape[0] // chunks

    barrier = pltpu.get_barrier_semaphore()
    for target in (fwd_id, bwd_id, pair_id):
        pl.semaphore_signal(barrier, 1, device_id=target, device_id_type=MESH)
    pl.semaphore_wait(barrier, 3)

    mine = c * z_count + z
    local = pltpu.make_async_copy(blk_ref, out_ref.at[mine], local_sem.at[0])
    local.start()
    sends = []

    def part(ref, k):
        return ref.at[pl.ds(k * piece, piece)]

    def send(src, slot, k, target):
        copy = pltpu.make_async_remote_copy(
            src_ref=part(src, k),
            dst_ref=part(out_ref.at[slot], k),
            send_sem=send_sem.at[len(sends)],
            recv_sem=recv_sem.at[slot * chunks + k],
            device_id=target,
            device_id_type=MESH,
        )
        copy.start()
        sends.append(copy)

    def arrive(slot, k):
        view = part(out_ref.at[slot], k)
        pltpu.make_async_remote_copy(
            src_ref=view,
            dst_ref=view,
            send_sem=send_sem.at[0],
            recv_sem=recv_sem.at[slot * chunks + k],
            device_id=pair_id,
            device_id_type=MESH,
        ).wait_recv()

    for k in range(chunks):
        send(blk_ref, mine, k, fwd_id)
        send(blk_ref, mine, k, bwd_id)
    for k in range(chunks):
        send(blk_ref, mine, k, pair_id)
    fwd_hops = z_count // 2
    bwd_hops = z_count - 1 - fwd_hops
    for hop in range(1, fwd_hops + 1):
        for k in range(chunks):
            slot = c * z_count + lax.rem(z - step * hop + 2 * z_count, z_count)
            arrive(slot, k)
            if hop < fwd_hops:
                send(out_ref.at[slot], slot, k, fwd_id)
            send(out_ref.at[slot], slot, k, pair_id)
            if hop <= bwd_hops:
                slot = c * z_count + lax.rem(z + step * hop + 2 * z_count, z_count)
                arrive(slot, k)
                if hop < bwd_hops:
                    send(out_ref.at[slot], slot, k, bwd_id)
                send(out_ref.at[slot], slot, k, pair_id)
    for zz in range(z_count):
        for k in range(chunks):
            arrive(other * z_count + zz, k)
    local.wait()
    for copy in sends:
        copy.wait_send()


def gather_blocks(block, z_count, chunks):
    count = 2 * z_count
    return pl.pallas_call(
        functools.partial(dispatch_kernel, z_count, chunks),
        out_shape=jax.ShapeDtypeStruct((count,) + block.shape, block.dtype),
        in_specs=[pl.BlockSpec(memory_space=pl.ANY)],
        out_specs=pl.BlockSpec(memory_space=pl.ANY),
        scratch_shapes=[
            pltpu.SemaphoreType.DMA((2 * count * chunks,)),
            pltpu.SemaphoreType.DMA((count * chunks,)),
            pltpu.SemaphoreType.DMA((1,)),
        ],
        compiler_params=pltpu.CompilerParams(collective_id=0, has_side_effects=True),
    )(block)


def combine_kernel(
    z_count, chunks, part_ref, out_ref, fwd_buf, bwd_buf, fwd_out, bwd_out, send_sem, recv_sem
):
    z = lax.axis_index("z")
    c = lax.axis_index("c")
    row = lax.axis_index("dp")
    step = 1 - 2 * c
    fwd = lax.rem(z + step + z_count, z_count)
    bwd = lax.rem(z - step + z_count, z_count)
    fwd_id, bwd_id = (row, fwd, c), (row, bwd, c)
    fwd_hops = z_count // 2
    bwd_hops = z_count - 1 - fwd_hops
    piece = part_ref.shape[1] // chunks

    barrier = pltpu.get_barrier_semaphore()
    for target in (fwd_id, bwd_id):
        pl.semaphore_signal(barrier, 1, device_id=target, device_id_type=MESH)
    pl.semaphore_wait(barrier, 2)

    sends = []

    def send(src, dst, sem, target):
        copy = pltpu.make_async_remote_copy(
            src_ref=src,
            dst_ref=dst,
            send_sem=send_sem.at[len(sends)],
            recv_sem=recv_sem.at[sem],
            device_id=target,
            device_id_type=MESH,
        )
        copy.start()
        sends.append(copy)

    def arrive(dst, sem):
        pltpu.make_async_remote_copy(
            src_ref=dst,
            dst_ref=dst,
            send_sem=send_sem.at[0],
            recv_sem=recv_sem.at[sem],
            device_id=fwd_id,
            device_id_type=MESH,
        ).wait_recv()

    def own(dest, rows):
        return part_ref[dest, rows].astype(jnp.float32)

    bwd_sem = fwd_hops * chunks
    for hop in range(1, fwd_hops + 1):
        for k in range(chunks):
            rows = pl.ds(k * piece, piece)
            dest = lax.rem(z + step * (fwd_hops + 1 - hop) + 2 * z_count, z_count)
            total = own(dest, rows)
            if hop > 1:
                sem = (hop - 2) * chunks + k
                arrive(fwd_buf.at[hop - 2, rows], sem)
                total = total + fwd_buf[hop - 2, rows].astype(jnp.float32)
            fwd_out[hop - 1, rows] = total.astype(fwd_out.dtype)
            sem = (hop - 1) * chunks + k
            send(fwd_out.at[hop - 1, rows], fwd_buf.at[hop - 1, rows], sem, fwd_id)
            if hop <= bwd_hops:
                dest = lax.rem(z - step * (bwd_hops + 1 - hop) + 2 * z_count, z_count)
                total = own(dest, rows)
                if hop > 1:
                    sem = bwd_sem + (hop - 2) * chunks + k
                    arrive(bwd_buf.at[hop - 2, rows], sem)
                    total = total + bwd_buf[hop - 2, rows].astype(jnp.float32)
                bwd_out[hop - 1, rows] = total.astype(bwd_out.dtype)
                sem = bwd_sem + (hop - 1) * chunks + k
                send(bwd_out.at[hop - 1, rows], bwd_buf.at[hop - 1, rows], sem, bwd_id)
    for k in range(chunks):
        rows = pl.ds(k * piece, piece)
        total = own(z, rows)
        arrive(fwd_buf.at[fwd_hops - 1, rows], (fwd_hops - 1) * chunks + k)
        total = total + fwd_buf[fwd_hops - 1, rows].astype(jnp.float32)
        if bwd_hops > 0:
            arrive(bwd_buf.at[bwd_hops - 1, rows], bwd_sem + (bwd_hops - 1) * chunks + k)
            total = total + bwd_buf[bwd_hops - 1, rows].astype(jnp.float32)
        out_ref[rows] = total.astype(out_ref.dtype)
    for copy in sends:
        copy.wait_send()


def scatter_sums(partial, chunks):
    z_count, rows, width = partial.shape
    fwd_hops = z_count // 2
    bwd_hops = max(z_count - 1 - fwd_hops, 1)
    block = (rows, width)
    vmem = pl.BlockSpec(memory_space=pltpu.VMEM)
    sems = (fwd_hops + bwd_hops) * chunks
    return pl.pallas_call(
        functools.partial(combine_kernel, z_count, chunks),
        out_shape=jax.ShapeDtypeStruct(block, partial.dtype),
        in_specs=[vmem],
        out_specs=vmem,
        scratch_shapes=[
            pltpu.VMEM((fwd_hops,) + block, partial.dtype),
            pltpu.VMEM((bwd_hops,) + block, partial.dtype),
            pltpu.VMEM((fwd_hops,) + block, partial.dtype),
            pltpu.VMEM((bwd_hops,) + block, partial.dtype),
            pltpu.SemaphoreType.DMA((sems,)),
            pltpu.SemaphoreType.DMA((sems,)),
        ],
        compiler_params=pltpu.CompilerParams(
            collective_id=1, has_side_effects=True, vmem_limit_bytes=48 * 1024 * 1024
        ),
    )(partial)


def expert_partials(inputs_all, ids_cube, rank_cube, weight_cube, my_index, w_gate, w_up, w_down):
    source_count, tok_rows, model_width = inputs_all.shape
    per_device = w_gate.shape[0]
    local_count = per_device * MOST
    local_slot = ids_cube - my_index * per_device
    is_mine = (local_slot >= 0) & (local_slot < per_device)
    local_key = jnp.where(is_mine, local_slot * MOST + rank_cube, -1)
    match = (
        local_key[:, None, :, :] == jnp.arange(local_count, dtype=jnp.int32)[None, :, None, None]
    )
    picker = jnp.any(match, axis=3).astype(jnp.bfloat16)
    slot_weight = jnp.sum(jnp.where(match, weight_cube[:, None, :, :], 0.0), axis=(2, 3)).reshape(
        source_count, per_device, MOST
    )
    row_block = jnp.einsum(
        "sqt,std->sqd", picker, inputs_all, preferred_element_type=jnp.float32
    ).astype(jnp.bfloat16)
    row_block = row_block.reshape(source_count, per_device, MOST, model_width)
    gate_proj = jnp.einsum("nemd,edf->nemf", row_block, w_gate, preferred_element_type=jnp.float32)
    up_proj = jnp.einsum("nemd,edf->nemf", row_block, w_up, preferred_element_type=jnp.float32)
    hidden = (jax.nn.silu(gate_proj) * up_proj).astype(jnp.bfloat16)
    down_out = jnp.einsum("nemf,efd->nemd", hidden, w_down, preferred_element_type=jnp.float32)
    result = (slot_weight[..., None] * down_out).astype(jnp.bfloat16)
    return jnp.einsum(
        "sqt,sqd->std",
        picker,
        result.reshape(source_count, local_count, model_width),
        preferred_element_type=jnp.float32,
    )


def body(
    tokens, expert_ids, gate_fixed, scorer_id, direction_tags, w_gate, w_up, w_down, score_head
):
    z_count = lax.axis_size("z")
    c_count = lax.axis_size("c")
    expert_count = z_count * c_count
    per_device = w_gate.shape[0]
    tok_rows, model_width = tokens.shape
    top_count = expert_ids.shape[1]
    which_tag = jnp.repeat(scorer_id, SEQ_LEN)[:, None]
    tag_rows = jnp.where(
        which_tag == 1, direction_tags[1][None, :], direction_tags[0][None, :]
    ).astype(jnp.float32)
    inputs = (tokens.astype(jnp.float32) + tag_rows).astype(jnp.bfloat16)
    rank_in = route_ranks(expert_ids, per_device * expert_count)
    routes = jnp.concatenate(
        [expert_ids, rank_in, gate_fixed // 256, gate_fixed % 256], axis=1
    ).astype(jnp.bfloat16)
    routes = jnp.pad(routes, ((0, 0), (0, 128 - 4 * top_count)))
    block = jnp.concatenate([inputs, routes], axis=1)
    gathered = gather_blocks(block, z_count, 4)
    inputs_all = gathered[:, :, :model_width]
    routes_all = gathered[:, :, model_width : model_width + 4 * top_count].astype(jnp.int32)
    ids_cube = routes_all[..., :top_count]
    rank_cube = routes_all[..., top_count : 2 * top_count]
    fixed_val = (
        routes_all[..., 2 * top_count : 3 * top_count] * 256 + routes_all[..., 3 * top_count :]
    ).astype(jnp.float32)
    weight_cube = fixed_val / jnp.sum(fixed_val, axis=2, keepdims=True)
    my_index = lax.axis_index("z") * c_count + lax.axis_index("c")
    c = lax.axis_index("c")

    def ring(cube, which):
        shaped = cube.reshape((c_count, z_count) + cube.shape[1:])
        return lax.dynamic_index_in_dim(shaped, which, axis=0, keepdims=False)

    def partials(which):
        return expert_partials(
            ring(inputs_all, which),
            ring(ids_cube, which),
            ring(rank_cube, which),
            ring(weight_cube, which),
            my_index,
            w_gate,
            w_up,
            w_down,
        )

    for_partner = partials(1 - c).astype(jnp.bfloat16)
    from_partner_core = lax.ppermute(for_partner, "c", [(0, 1), (1, 0)])
    own_ring = partials(c)
    chip_sum = (own_ring + from_partner_core.astype(jnp.float32)).astype(jnp.bfloat16)
    mixed = scatter_sums(chip_sum, 4)
    token_score = jnp.dot(mixed.astype(jnp.float32), score_head, precision=lax.Precision.HIGHEST)
    seq_score = token_score.reshape(-1, SEQ_LEN).sum(axis=1)
    partner = from_partner(seq_score, "dp", lax.axis_size("dp").bit_length() - 2)
    pair_score = jnp.abs(seq_score - partner) + 0.5 * (seq_score + partner)
    return (mixed, pair_score)


def solution(mesh):
    dp_count, expert_count = mesh.devices.shape
    split = Mesh(mesh.devices.reshape(dp_count, expert_count // 2, 2), ("dp", "z", "c"))
    rows = P(("dp", "z", "c"), None)
    return jax.shard_map(
        body,
        mesh=split,
        in_specs=(
            rows,
            rows,
            rows,
            P(("dp", "z", "c")),
            P(),
            P(("z", "c"), None, None),
            P(("z", "c"), None, None),
            P(("z", "c"), None, None),
            P(),
        ),
        out_specs=(rows, P(("dp", "z", "c"))),
        check_vma=False,
    )
```

```python
import functools

import jax
import jax.numpy as jnp
from jax import lax
from jax.experimental import pallas as pl
from jax.experimental.pallas import tpu as pltpu
from jax.sharding import Mesh
from jax.sharding import PartitionSpec as P

SEQ_LEN = 16
MOST = 24


def from_partner(block, axis, bit):
    count = lax.axis_size(axis)
    route = []
    for low in range(count):
        high = low | 1 << bit
        if high != low and high < count:
            route += [(low, high), (high, low)]
    return lax.ppermute(block, axis, route)


def route_ranks(expert_ids, expert_total):
    flat_ids = expert_ids.reshape(-1)
    entry_count = flat_ids.shape[0]
    onehot = flat_ids[:, None] == jnp.arange(expert_total, dtype=jnp.int32)[None, :]
    positions = jnp.arange(entry_count, dtype=jnp.int32)
    earlier = (positions[:, None] > positions[None, :]).astype(jnp.bfloat16)
    counts = jnp.dot(earlier, onehot.astype(jnp.bfloat16), preferred_element_type=jnp.float32)
    rank_in = jnp.sum(jnp.where(onehot, counts, 0.0), axis=1).astype(jnp.int32)
    return rank_in.reshape(expert_ids.shape)


MESH = pl.DeviceIdType.MESH


def dispatch_kernel(z_count, chunks, blk_ref, out_ref, send_sem, recv_sem, local_sem):
    z = lax.axis_index("z")
    c = lax.axis_index("c")
    row = lax.axis_index("dp")
    other = 1 - c
    step = 1 - 2 * c
    fwd = lax.rem(z + step + z_count, z_count)
    bwd = lax.rem(z - step + z_count, z_count)
    fwd_id, bwd_id, pair_id = (row, fwd, c), (row, bwd, c), (row, z, other)
    piece = blk_ref.shape[0] // chunks

    barrier = pltpu.get_barrier_semaphore()
    for target in (fwd_id, bwd_id, pair_id):
        pl.semaphore_signal(barrier, 1, device_id=target, device_id_type=MESH)
    pl.semaphore_wait(barrier, 3)

    mine = c * z_count + z
    local = pltpu.make_async_copy(blk_ref, out_ref.at[mine], local_sem.at[0])
    local.start()
    sends = []

    def part(ref, k):
        return ref.at[pl.ds(k * piece, piece)]

    def send(src, slot, k, target):
        copy = pltpu.make_async_remote_copy(
            src_ref=part(src, k),
            dst_ref=part(out_ref.at[slot], k),
            send_sem=send_sem.at[len(sends)],
            recv_sem=recv_sem.at[slot * chunks + k],
            device_id=target,
            device_id_type=MESH,
        )
        copy.start()
        sends.append(copy)

    def arrive(slot, k):
        view = part(out_ref.at[slot], k)
        pltpu.make_async_remote_copy(
            src_ref=view,
            dst_ref=view,
            send_sem=send_sem.at[0],
            recv_sem=recv_sem.at[slot * chunks + k],
            device_id=pair_id,
            device_id_type=MESH,
        ).wait_recv()

    for k in range(chunks):
        send(blk_ref, mine, k, fwd_id)
        send(blk_ref, mine, k, bwd_id)
    for k in range(chunks):
        send(blk_ref, mine, k, pair_id)
    fwd_hops = z_count // 2
    bwd_hops = z_count - 1 - fwd_hops
    for hop in range(1, fwd_hops + 1):
        for k in range(chunks):
            slot = c * z_count + lax.rem(z - step * hop + 2 * z_count, z_count)
            arrive(slot, k)
            if hop < fwd_hops:
                send(out_ref.at[slot], slot, k, fwd_id)
            send(out_ref.at[slot], slot, k, pair_id)
            if hop <= bwd_hops:
                slot = c * z_count + lax.rem(z + step * hop + 2 * z_count, z_count)
                arrive(slot, k)
                if hop < bwd_hops:
                    send(out_ref.at[slot], slot, k, bwd_id)
                send(out_ref.at[slot], slot, k, pair_id)
    for zz in range(z_count):
        for k in range(chunks):
            arrive(other * z_count + zz, k)
    local.wait()
    for copy in sends:
        copy.wait_send()


def gather_blocks(block, z_count, chunks):
    count = 2 * z_count
    return pl.pallas_call(
        functools.partial(dispatch_kernel, z_count, chunks),
        out_shape=jax.ShapeDtypeStruct((count,) + block.shape, block.dtype),
        in_specs=[pl.BlockSpec(memory_space=pl.ANY)],
        out_specs=pl.BlockSpec(memory_space=pl.ANY),
        scratch_shapes=[
            pltpu.SemaphoreType.DMA((2 * count * chunks,)),
            pltpu.SemaphoreType.DMA((count * chunks,)),
            pltpu.SemaphoreType.DMA((1,)),
        ],
        compiler_params=pltpu.CompilerParams(collective_id=0, has_side_effects=True),
    )(block)


def combine_kernel(
    z_count, chunks, part_ref, out_ref, pair_buf, fwd_buf, bwd_buf, fwd_out, bwd_out,
    send_sem, recv_sem,
):
    z = lax.axis_index("z")
    c = lax.axis_index("c")
    row = lax.axis_index("dp")
    other = 1 - c
    step = 1 - 2 * c
    fwd = lax.rem(z + step + z_count, z_count)
    bwd = lax.rem(z - step + z_count, z_count)
    fwd_id, bwd_id, pair_id = (row, fwd, c), (row, bwd, c), (row, z, other)
    fwd_hops = z_count // 2
    bwd_hops = z_count - 1 - fwd_hops
    piece = part_ref.shape[2] // chunks

    barrier = pltpu.get_barrier_semaphore()
    for target in (fwd_id, bwd_id, pair_id):
        pl.semaphore_signal(barrier, 1, device_id=target, device_id_type=MESH)
    pl.semaphore_wait(barrier, 3)

    sends = []

    def send(src, dst, sem, target):
        copy = pltpu.make_async_remote_copy(
            src_ref=src,
            dst_ref=dst,
            send_sem=send_sem.at[len(sends)],
            recv_sem=recv_sem.at[sem],
            device_id=target,
            device_id_type=MESH,
        )
        copy.start()
        sends.append(copy)

    def arrive(dst, sem):
        pltpu.make_async_remote_copy(
            src_ref=dst,
            dst_ref=dst,
            send_sem=send_sem.at[0],
            recv_sem=recv_sem.at[sem],
            device_id=pair_id,
            device_id_type=MESH,
        ).wait_recv()

    def order(ring_step):
        dests = []
        for hop in range(1, fwd_hops + 1):
            dests.append(lax.rem(z + ring_step * (fwd_hops + 1 - hop) + 2 * z_count, z_count))
            if hop <= bwd_hops:
                dests.append(lax.rem(z - ring_step * (bwd_hops + 1 - hop) + 2 * z_count, z_count))
        return dests + [z]

    for n, dest in enumerate(order(-step)):
        send(part_ref.at[other, dest], pair_buf.at[n], n, pair_id)
    def own(dest, n, k):
        if k == 0:
            arrive(pair_buf.at[n], n)
        rows = pl.ds(k * piece, piece)
        return part_ref[c, dest, rows].astype(jnp.float32) + pair_buf[n, rows].astype(
            jnp.float32
        )

    fwd_sem = z_count
    bwd_sem = z_count + fwd_hops * chunks
    for hop in range(1, fwd_hops + 1):
        for k in range(chunks):
            rows = pl.ds(k * piece, piece)
            dest = lax.rem(z + step * (fwd_hops + 1 - hop) + 2 * z_count, z_count)
            n = hop - 1 + min(hop - 1, bwd_hops)
            total = own(dest, n, k)
            if hop > 1:
                sem = fwd_sem + (hop - 2) * chunks + k
                arrive(fwd_buf.at[hop - 2, rows], sem)
                total = total + fwd_buf[hop - 2, rows].astype(jnp.float32)
            fwd_out[hop - 1, rows] = total.astype(fwd_out.dtype)
            sem = fwd_sem + (hop - 1) * chunks + k
            send(fwd_out.at[hop - 1, rows], fwd_buf.at[hop - 1, rows], sem, fwd_id)
            if hop <= bwd_hops:
                dest = lax.rem(z - step * (bwd_hops + 1 - hop) + 2 * z_count, z_count)
                total = own(dest, n + 1, k)
                if hop > 1:
                    sem = bwd_sem + (hop - 2) * chunks + k
                    arrive(bwd_buf.at[hop - 2, rows], sem)
                    total = total + bwd_buf[hop - 2, rows].astype(jnp.float32)
                bwd_out[hop - 1, rows] = total.astype(bwd_out.dtype)
                sem = bwd_sem + (hop - 1) * chunks + k
                send(bwd_out.at[hop - 1, rows], bwd_buf.at[hop - 1, rows], sem, bwd_id)
    for k in range(chunks):
        rows = pl.ds(k * piece, piece)
        total = own(z, fwd_hops + bwd_hops, k)
        arrive(fwd_buf.at[fwd_hops - 1, rows], fwd_sem + (fwd_hops - 1) * chunks + k)
        total = total + fwd_buf[fwd_hops - 1, rows].astype(jnp.float32)
        if bwd_hops > 0:
            arrive(bwd_buf.at[bwd_hops - 1, rows], bwd_sem + (bwd_hops - 1) * chunks + k)
            total = total + bwd_buf[bwd_hops - 1, rows].astype(jnp.float32)
        out_ref[rows] = total.astype(out_ref.dtype)
    for copy in sends:
        copy.wait_send()


def scatter_sums(partial, chunks):
    c_count, z_count, rows, width = partial.shape
    fwd_hops = z_count // 2
    bwd_hops = max(z_count - 1 - fwd_hops, 1)
    block = (rows, width)
    vmem = pl.BlockSpec(memory_space=pltpu.VMEM)
    sems = z_count + (fwd_hops + bwd_hops) * chunks
    return pl.pallas_call(
        functools.partial(combine_kernel, z_count, chunks),
        out_shape=jax.ShapeDtypeStruct(block, partial.dtype),
        in_specs=[vmem],
        out_specs=vmem,
        scratch_shapes=[
            pltpu.VMEM((z_count,) + block, partial.dtype),
            pltpu.VMEM((fwd_hops,) + block, partial.dtype),
            pltpu.VMEM((bwd_hops,) + block, partial.dtype),
            pltpu.VMEM((fwd_hops,) + block, partial.dtype),
            pltpu.VMEM((bwd_hops,) + block, partial.dtype),
            pltpu.SemaphoreType.DMA((sems,)),
            pltpu.SemaphoreType.DMA((sems,)),
        ],
        compiler_params=pltpu.CompilerParams(
            collective_id=1, has_side_effects=True, vmem_limit_bytes=48 * 1024 * 1024
        ),
    )(partial)


def ffn_kernel(x_ref, sw_ref, wg_ref, wu_ref, wd_ref, o_ref):
    sources, slots, width = x_ref.shape
    rows = x_ref[...].reshape(sources * slots, width).astype(jnp.bfloat16)
    gate_proj = jnp.dot(rows, wg_ref[0], preferred_element_type=jnp.float32)
    up_proj = jnp.dot(rows, wu_ref[0], preferred_element_type=jnp.float32)
    hidden = (gate_proj / (1.0 + jnp.exp(-gate_proj)) * up_proj).astype(jnp.bfloat16)
    down_out = jnp.dot(hidden, wd_ref[0], preferred_element_type=jnp.float32)
    result = (sw_ref[...].reshape(sources * slots, 1) * down_out).astype(jnp.bfloat16)
    o_ref[...] = result.astype(jnp.float32).reshape(sources, slots, width)


def expert_ffn(row_block, slot_weight, w_gate, w_up, w_down):
    sources, slots, width = row_block.shape
    per_device, _, hidden = w_gate.shape
    rows = slots // per_device
    return pl.pallas_call(
        ffn_kernel,
        out_shape=jax.ShapeDtypeStruct(row_block.shape, jnp.float32),
        grid=(per_device,),
        in_specs=[
            pl.BlockSpec((sources, rows, width), lambda e: (0, e, 0)),
            pl.BlockSpec((sources, rows, 1), lambda e: (0, e, 0)),
            pl.BlockSpec((1, width, hidden), lambda e: (e, 0, 0)),
            pl.BlockSpec((1, width, hidden), lambda e: (e, 0, 0)),
            pl.BlockSpec((1, hidden, width), lambda e: (e, 0, 0)),
        ],
        out_specs=pl.BlockSpec((sources, rows, width), lambda e: (0, e, 0)),
        compiler_params=pltpu.CompilerParams(vmem_limit_bytes=56 * 1024 * 1024),
    )(row_block, slot_weight[..., None], w_gate, w_up, w_down)


def body(
    tokens, expert_ids, gate_fixed, scorer_id, direction_tags, w_gate, w_up, w_down, score_head
):
    z_count = lax.axis_size("z")
    c_count = lax.axis_size("c")
    expert_count = z_count * c_count
    per_device = w_gate.shape[0]
    tok_rows, model_width = tokens.shape
    top_count = expert_ids.shape[1]
    which_tag = jnp.repeat(scorer_id, SEQ_LEN)[:, None]
    tag_rows = jnp.where(
        which_tag == 1, direction_tags[1][None, :], direction_tags[0][None, :]
    ).astype(jnp.float32)
    inputs = (tokens.astype(jnp.float32) + tag_rows).astype(jnp.bfloat16)
    rank_in = route_ranks(expert_ids, per_device * expert_count)
    routes = jnp.concatenate(
        [expert_ids, rank_in, gate_fixed // 256, gate_fixed % 256], axis=1
    ).astype(jnp.bfloat16)
    routes = jnp.pad(routes, ((0, 0), (0, 128 - 4 * top_count)))
    block = jnp.concatenate([inputs, routes], axis=1)
    gathered = gather_blocks(block, z_count, 2)
    inputs_all = gathered[:, :, :model_width]
    routes_all = gathered[:, :, model_width : model_width + 4 * top_count].astype(jnp.int32)
    ids_cube = routes_all[..., :top_count]
    rank_cube = routes_all[..., top_count : 2 * top_count]
    fixed_val = (
        routes_all[..., 2 * top_count : 3 * top_count] * 256 + routes_all[..., 3 * top_count :]
    ).astype(jnp.float32)
    weight_cube = fixed_val / jnp.sum(fixed_val, axis=2, keepdims=True)
    my_index = lax.axis_index("z") * c_count + lax.axis_index("c")
    local_count = per_device * MOST
    local_slot = ids_cube - my_index * per_device
    is_mine = (local_slot >= 0) & (local_slot < per_device)
    local_key = jnp.where(is_mine, local_slot * MOST + rank_cube, -1)
    match = (
        local_key[:, None, :, :] == jnp.arange(local_count, dtype=jnp.int32)[None, :, None, None]
    )
    picker = jnp.any(match, axis=3).astype(jnp.bfloat16)
    slot_weight = jnp.sum(jnp.where(match, weight_cube[:, None, :, :], 0.0), axis=(2, 3))
    row_block = jnp.einsum("sqt,std->sqd", picker, inputs_all, preferred_element_type=jnp.float32)
    result = expert_ffn(row_block, slot_weight, w_gate, w_up, w_down).astype(jnp.bfloat16)
    partial_value = jnp.einsum(
        "sqt,sqd->std",
        picker,
        result,
        preferred_element_type=jnp.float32,
    )
    partial_value = partial_value.reshape(c_count, z_count, tok_rows, model_width)
    mixed = scatter_sums(partial_value.astype(jnp.bfloat16), 2)
    token_score = jnp.dot(mixed.astype(jnp.float32), score_head, precision=lax.Precision.HIGHEST)
    seq_score = token_score.reshape(-1, SEQ_LEN).sum(axis=1)
    partner = from_partner(seq_score, "dp", lax.axis_size("dp").bit_length() - 2)
    pair_score = jnp.abs(seq_score - partner) + 0.5 * (seq_score + partner)
    return (mixed, pair_score)


def solution(mesh):
    dp_count, expert_count = mesh.devices.shape
    split = Mesh(mesh.devices.reshape(dp_count, expert_count // 2, 2), ("dp", "z", "c"))
    rows = P(("dp", "z", "c"), None)
    return jax.shard_map(
        body,
        mesh=split,
        in_specs=(
            rows,
            rows,
            rows,
            P(("dp", "z", "c")),
            P(),
            P(("z", "c"), None, None),
            P(("z", "c"), None, None),
            P(("z", "c"), None, None),
            P(),
        ),
        out_specs=(rows, P(("dp", "z", "c"))),
        check_vma=False,
    )
```

```python
import functools

import jax
import jax.numpy as jnp
from jax import lax
from jax.experimental import pallas as pl
from jax.experimental.pallas import tpu as pltpu
from jax.sharding import Mesh
from jax.sharding import PartitionSpec as P

SEQ_LEN = 16
MOST = 24


def from_partner(block, axis, bit):
    count = lax.axis_size(axis)
    route = []
    for low in range(count):
        high = low | 1 << bit
        if high != low and high < count:
            route += [(low, high), (high, low)]
    return lax.ppermute(block, axis, route)


def route_ranks(expert_ids, expert_total):
    flat_ids = expert_ids.reshape(-1)
    entry_count = flat_ids.shape[0]
    onehot = flat_ids[:, None] == jnp.arange(expert_total, dtype=jnp.int32)[None, :]
    positions = jnp.arange(entry_count, dtype=jnp.int32)
    earlier = (positions[:, None] > positions[None, :]).astype(jnp.bfloat16)
    counts = jnp.dot(earlier, onehot.astype(jnp.bfloat16), preferred_element_type=jnp.float32)
    rank_in = jnp.sum(jnp.where(onehot, counts, 0.0), axis=1).astype(jnp.int32)
    return rank_in.reshape(expert_ids.shape)


MESH = pl.DeviceIdType.MESH


def dispatch_kernel(z_count, chunks, blk_ref, out_ref, send_sem, recv_sem, local_sem):
    z = lax.axis_index("z")
    c = lax.axis_index("c")
    row = lax.axis_index("dp")
    other = 1 - c
    step = 1 - 2 * c
    fwd = lax.rem(z + step + z_count, z_count)
    bwd = lax.rem(z - step + z_count, z_count)
    fwd_id, bwd_id, pair_id = (row, fwd, c), (row, bwd, c), (row, z, other)
    piece = blk_ref.shape[0] // chunks

    barrier = pltpu.get_barrier_semaphore()
    for target in (fwd_id, bwd_id, pair_id):
        pl.semaphore_signal(barrier, 1, device_id=target, device_id_type=MESH)
    pl.semaphore_wait(barrier, 3)

    mine = c * z_count + z
    local = pltpu.make_async_copy(blk_ref, out_ref.at[mine], local_sem.at[0])
    local.start()
    sends = []

    def part(ref, k):
        return ref.at[pl.ds(k * piece, piece)]

    def send(src, slot, k, target):
        copy = pltpu.make_async_remote_copy(
            src_ref=part(src, k),
            dst_ref=part(out_ref.at[slot], k),
            send_sem=send_sem.at[len(sends)],
            recv_sem=recv_sem.at[slot * chunks + k],
            device_id=target,
            device_id_type=MESH,
        )
        copy.start()
        sends.append(copy)

    def arrive(slot, k):
        view = part(out_ref.at[slot], k)
        pltpu.make_async_remote_copy(
            src_ref=view,
            dst_ref=view,
            send_sem=send_sem.at[0],
            recv_sem=recv_sem.at[slot * chunks + k],
            device_id=pair_id,
            device_id_type=MESH,
        ).wait_recv()

    for k in range(chunks):
        send(blk_ref, mine, k, fwd_id)
        send(blk_ref, mine, k, bwd_id)
    for k in range(chunks):
        send(blk_ref, mine, k, pair_id)
    fwd_hops = z_count // 2
    bwd_hops = z_count - 1 - fwd_hops
    for hop in range(1, fwd_hops + 1):
        for k in range(chunks):
            slot = c * z_count + lax.rem(z - step * hop + 2 * z_count, z_count)
            arrive(slot, k)
            if hop < fwd_hops:
                send(out_ref.at[slot], slot, k, fwd_id)
            send(out_ref.at[slot], slot, k, pair_id)
            if hop <= bwd_hops:
                slot = c * z_count + lax.rem(z + step * hop + 2 * z_count, z_count)
                arrive(slot, k)
                if hop < bwd_hops:
                    send(out_ref.at[slot], slot, k, bwd_id)
                send(out_ref.at[slot], slot, k, pair_id)
    for zz in range(z_count):
        for k in range(chunks):
            arrive(other * z_count + zz, k)
    local.wait()
    for copy in sends:
        copy.wait_send()


def gather_blocks(block, z_count, chunks):
    count = 2 * z_count
    return pl.pallas_call(
        functools.partial(dispatch_kernel, z_count, chunks),
        out_shape=jax.ShapeDtypeStruct((count,) + block.shape, block.dtype),
        in_specs=[pl.BlockSpec(memory_space=pl.ANY)],
        out_specs=pl.BlockSpec(memory_space=pl.ANY),
        scratch_shapes=[
            pltpu.SemaphoreType.DMA((2 * count * chunks,)),
            pltpu.SemaphoreType.DMA((count * chunks,)),
            pltpu.SemaphoreType.DMA((1,)),
        ],
        compiler_params=pltpu.CompilerParams(collective_id=0, has_side_effects=True),
    )(block)


def combine_kernel(
    z_count, chunks, part_ref, out_ref, pair_buf, fwd_buf, bwd_buf, fwd_out, bwd_out,
    send_sem, recv_sem,
):
    z = lax.axis_index("z")
    c = lax.axis_index("c")
    row = lax.axis_index("dp")
    other = 1 - c
    step = 1 - 2 * c
    fwd = lax.rem(z + step + z_count, z_count)
    bwd = lax.rem(z - step + z_count, z_count)
    fwd_id, bwd_id, pair_id = (row, fwd, c), (row, bwd, c), (row, z, other)
    fwd_hops = z_count // 2
    bwd_hops = z_count - 1 - fwd_hops
    piece = part_ref.shape[2] // chunks

    barrier = pltpu.get_barrier_semaphore()
    for target in (fwd_id, bwd_id, pair_id):
        pl.semaphore_signal(barrier, 1, device_id=target, device_id_type=MESH)
    pl.semaphore_wait(barrier, 3)

    sends = []

    def send(src, dst, sem, target):
        copy = pltpu.make_async_remote_copy(
            src_ref=src,
            dst_ref=dst,
            send_sem=send_sem.at[len(sends)],
            recv_sem=recv_sem.at[sem],
            device_id=target,
            device_id_type=MESH,
        )
        copy.start()
        sends.append(copy)

    def arrive(dst, sem):
        pltpu.make_async_remote_copy(
            src_ref=dst,
            dst_ref=dst,
            send_sem=send_sem.at[0],
            recv_sem=recv_sem.at[sem],
            device_id=pair_id,
            device_id_type=MESH,
        ).wait_recv()

    def order(ring_step):
        dests = []
        for hop in range(1, fwd_hops + 1):
            dests.append(lax.rem(z + ring_step * (fwd_hops + 1 - hop) + 2 * z_count, z_count))
            if hop <= bwd_hops:
                dests.append(lax.rem(z - ring_step * (bwd_hops + 1 - hop) + 2 * z_count, z_count))
        return dests + [z]

    for n, dest in enumerate(order(-step)):
        send(part_ref.at[other, dest], pair_buf.at[n], n, pair_id)
    def own(dest, n, k):
        if k == 0:
            arrive(pair_buf.at[n], n)
        rows = pl.ds(k * piece, piece)
        return part_ref[c, dest, rows].astype(jnp.float32) + pair_buf[n, rows].astype(
            jnp.float32
        )

    fwd_sem = z_count
    bwd_sem = z_count + fwd_hops * chunks
    for hop in range(1, fwd_hops + 1):
        for k in range(chunks):
            rows = pl.ds(k * piece, piece)
            dest = lax.rem(z + step * (fwd_hops + 1 - hop) + 2 * z_count, z_count)
            n = hop - 1 + min(hop - 1, bwd_hops)
            total = own(dest, n, k)
            if hop > 1:
                sem = fwd_sem + (hop - 2) * chunks + k
                arrive(fwd_buf.at[hop - 2, rows], sem)
                total = total + fwd_buf[hop - 2, rows].astype(jnp.float32)
            fwd_out[hop - 1, rows] = total.astype(fwd_out.dtype)
            sem = fwd_sem + (hop - 1) * chunks + k
            send(fwd_out.at[hop - 1, rows], fwd_buf.at[hop - 1, rows], sem, fwd_id)
            if hop <= bwd_hops:
                dest = lax.rem(z - step * (bwd_hops + 1 - hop) + 2 * z_count, z_count)
                total = own(dest, n + 1, k)
                if hop > 1:
                    sem = bwd_sem + (hop - 2) * chunks + k
                    arrive(bwd_buf.at[hop - 2, rows], sem)
                    total = total + bwd_buf[hop - 2, rows].astype(jnp.float32)
                bwd_out[hop - 1, rows] = total.astype(bwd_out.dtype)
                sem = bwd_sem + (hop - 1) * chunks + k
                send(bwd_out.at[hop - 1, rows], bwd_buf.at[hop - 1, rows], sem, bwd_id)
    for k in range(chunks):
        rows = pl.ds(k * piece, piece)
        total = own(z, fwd_hops + bwd_hops, k)
        arrive(fwd_buf.at[fwd_hops - 1, rows], fwd_sem + (fwd_hops - 1) * chunks + k)
        total = total + fwd_buf[fwd_hops - 1, rows].astype(jnp.float32)
        if bwd_hops > 0:
            arrive(bwd_buf.at[bwd_hops - 1, rows], bwd_sem + (bwd_hops - 1) * chunks + k)
            total = total + bwd_buf[bwd_hops - 1, rows].astype(jnp.float32)
        out_ref[rows] = total.astype(out_ref.dtype)
    for copy in sends:
        copy.wait_send()


def scatter_sums(partial, chunks):
    c_count, z_count, rows, width = partial.shape
    fwd_hops = z_count // 2
    bwd_hops = max(z_count - 1 - fwd_hops, 1)
    block = (rows, width)
    vmem = pl.BlockSpec(memory_space=pltpu.VMEM)
    sems = z_count + (fwd_hops + bwd_hops) * chunks
    return pl.pallas_call(
        functools.partial(combine_kernel, z_count, chunks),
        out_shape=jax.ShapeDtypeStruct(block, partial.dtype),
        in_specs=[vmem],
        out_specs=vmem,
        scratch_shapes=[
            pltpu.VMEM((z_count,) + block, partial.dtype),
            pltpu.VMEM((fwd_hops,) + block, partial.dtype),
            pltpu.VMEM((bwd_hops,) + block, partial.dtype),
            pltpu.VMEM((fwd_hops,) + block, partial.dtype),
            pltpu.VMEM((bwd_hops,) + block, partial.dtype),
            pltpu.SemaphoreType.DMA((sems,)),
            pltpu.SemaphoreType.DMA((sems,)),
        ],
        compiler_params=pltpu.CompilerParams(
            collective_id=1, has_side_effects=True, vmem_limit_bytes=48 * 1024 * 1024
        ),
    )(partial)


def local_kernel(
    inp_ref, pick_ref, pickt_ref, sw_ref, wg_hbm, wu_hbm, wd_hbm, o_ref, wg, wu, wd, x_scr, sem
):
    copies = [
        pltpu.make_async_copy(src, dst, sem.at[n])
        for n, (src, dst) in enumerate(((wg_hbm, wg), (wu_hbm, wu), (wd_hbm, wd)))
    ]
    for copy in copies:
        copy.start()
    sources, slots, _ = pick_ref.shape
    per_device = wg.shape[0]
    most = slots // per_device
    width = o_ref.shape[2]

    def gather(s, carry):
        rows = jnp.dot(pick_ref[s], inp_ref[s, :, pl.ds(0, width)], preferred_element_type=jnp.float32)
        start = pl.multiple_of(s * most, 8)
        for e in range(per_device):
            x_scr[e, pl.ds(start, most)] = rows[e * most : (e + 1) * most]
        return carry

    lax.fori_loop(0, sources, gather, 0)
    for copy in copies:
        copy.wait()
    for e in range(per_device):
        rows = x_scr[e].astype(jnp.bfloat16)
        gate_proj = jnp.dot(rows, wg[e], preferred_element_type=jnp.float32)
        up_proj = jnp.dot(rows, wu[e], preferred_element_type=jnp.float32)
        hidden = (gate_proj / (1.0 + jnp.exp(-gate_proj)) * up_proj).astype(jnp.bfloat16)
        down_out = jnp.dot(hidden, wd[e], preferred_element_type=jnp.float32)
        x_scr[e] = (sw_ref[e] * down_out).astype(jnp.bfloat16).astype(jnp.float32)

    def combine(s, carry):
        start = pl.multiple_of(s * most, 8)
        total = jnp.zeros(o_ref.shape[1:], jnp.float32)
        for e in range(per_device):
            result = x_scr[e, pl.ds(start, most)]
            total = total + jnp.dot(pickt_ref[s, e], result, preferred_element_type=jnp.float32)
        o_ref[s] = total.astype(o_ref.dtype)
        return carry

    lax.fori_loop(0, sources, combine, 0)


def local_experts(gathered, picker, slot_weight, w_gate, w_up, w_down, model_width):
    sources, slots, tok_rows = picker.shape
    per_device = w_gate.shape[0]
    most = slots // per_device
    pick_t = picker.astype(jnp.float32).reshape(sources, per_device, most, tok_rows)
    pick_t = jnp.swapaxes(pick_t, 2, 3)
    weights = slot_weight.reshape(sources, per_device, most).transpose(1, 0, 2)
    weights = weights.reshape(per_device, sources * most, 1)
    vmem = pl.BlockSpec(memory_space=pltpu.VMEM)
    hbm = pl.BlockSpec(memory_space=pl.ANY)
    return pl.pallas_call(
        local_kernel,
        out_shape=jax.ShapeDtypeStruct((sources, tok_rows, model_width), jnp.bfloat16),
        in_specs=[vmem, vmem, vmem, vmem, hbm, hbm, hbm],
        out_specs=vmem,
        scratch_shapes=[
            pltpu.VMEM(w_gate.shape, w_gate.dtype),
            pltpu.VMEM(w_up.shape, w_up.dtype),
            pltpu.VMEM(w_down.shape, w_down.dtype),
            pltpu.VMEM((per_device, sources * most, model_width), jnp.float32),
            pltpu.SemaphoreType.DMA((3,)),
        ],
        compiler_params=pltpu.CompilerParams(vmem_limit_bytes=60 * 1024 * 1024),
    )(gathered, picker, pick_t, weights, w_gate, w_up, w_down)


def body(
    tokens, expert_ids, gate_fixed, scorer_id, direction_tags, w_gate, w_up, w_down, score_head
):
    z_count = lax.axis_size("z")
    c_count = lax.axis_size("c")
    expert_count = z_count * c_count
    per_device = w_gate.shape[0]
    tok_rows, model_width = tokens.shape
    top_count = expert_ids.shape[1]
    which_tag = jnp.repeat(scorer_id, SEQ_LEN)[:, None]
    tag_rows = jnp.where(
        which_tag == 1, direction_tags[1][None, :], direction_tags[0][None, :]
    ).astype(jnp.float32)
    inputs = (tokens.astype(jnp.float32) + tag_rows).astype(jnp.bfloat16)
    rank_in = route_ranks(expert_ids, per_device * expert_count)
    routes = jnp.concatenate(
        [expert_ids, rank_in, gate_fixed // 256, gate_fixed % 256], axis=1
    ).astype(jnp.bfloat16)
    routes = jnp.pad(routes, ((0, 0), (0, 128 - 4 * top_count)))
    block = jnp.concatenate([inputs, routes], axis=1)
    gathered = gather_blocks(block, z_count, 2)
    inputs_all = gathered[:, :, :model_width]
    routes_all = gathered[:, :, model_width : model_width + 4 * top_count].astype(jnp.int32)
    ids_cube = routes_all[..., :top_count]
    rank_cube = routes_all[..., top_count : 2 * top_count]
    fixed_val = (
        routes_all[..., 2 * top_count : 3 * top_count] * 256 + routes_all[..., 3 * top_count :]
    ).astype(jnp.float32)
    weight_cube = fixed_val / jnp.sum(fixed_val, axis=2, keepdims=True)
    my_index = lax.axis_index("z") * c_count + lax.axis_index("c")
    local_count = per_device * MOST
    local_slot = ids_cube - my_index * per_device
    is_mine = (local_slot >= 0) & (local_slot < per_device)
    local_key = jnp.where(is_mine, local_slot * MOST + rank_cube, -1)
    match = (
        local_key[:, None, :, :] == jnp.arange(local_count, dtype=jnp.int32)[None, :, None, None]
    )
    picker = jnp.any(match, axis=3).astype(jnp.bfloat16)
    slot_weight = jnp.sum(jnp.where(match, weight_cube[:, None, :, :], 0.0), axis=(2, 3))
    partial_value = local_experts(gathered, picker, slot_weight, w_gate, w_up, w_down, model_width)
    partial_value = partial_value.reshape(c_count, z_count, tok_rows, model_width)
    mixed = scatter_sums(partial_value, 2)
    token_score = jnp.dot(mixed.astype(jnp.float32), score_head, precision=lax.Precision.HIGHEST)
    seq_score = token_score.reshape(-1, SEQ_LEN).sum(axis=1)
    partner = from_partner(seq_score, "dp", lax.axis_size("dp").bit_length() - 2)
    pair_score = jnp.abs(seq_score - partner) + 0.5 * (seq_score + partner)
    return (mixed, pair_score)


def solution(mesh):
    dp_count, expert_count = mesh.devices.shape
    split = Mesh(mesh.devices.reshape(dp_count, expert_count // 2, 2), ("dp", "z", "c"))
    rows = P(("dp", "z", "c"), None)
    return jax.shard_map(
        body,
        mesh=split,
        in_specs=(
            rows,
            rows,
            rows,
            P(("dp", "z", "c")),
            P(),
            P(("z", "c"), None, None),
            P(("z", "c"), None, None),
            P(("z", "c"), None, None),
            P(),
        ),
        out_specs=(rows, P(("dp", "z", "c"))),
        check_vma=False,
    )
```

```python
import functools

import jax
import jax.numpy as jnp
from jax import lax
from jax.experimental import pallas as pl
from jax.experimental.pallas import tpu as pltpu
from jax.sharding import Mesh
from jax.sharding import PartitionSpec as P

SEQ_LEN = 16
MOST = 24


def from_partner(block, axis, bit):
    count = lax.axis_size(axis)
    route = []
    for low in range(count):
        high = low | 1 << bit
        if high != low and high < count:
            route += [(low, high), (high, low)]
    return lax.ppermute(block, axis, route)


def route_ranks(expert_ids, expert_total):
    flat_ids = expert_ids.reshape(-1)
    entry_count = flat_ids.shape[0]
    onehot = flat_ids[:, None] == jnp.arange(expert_total, dtype=jnp.int32)[None, :]
    positions = jnp.arange(entry_count, dtype=jnp.int32)
    earlier = (positions[:, None] > positions[None, :]).astype(jnp.bfloat16)
    counts = jnp.dot(earlier, onehot.astype(jnp.bfloat16), preferred_element_type=jnp.float32)
    rank_in = jnp.sum(jnp.where(onehot, counts, 0.0), axis=1).astype(jnp.int32)
    return rank_in.reshape(expert_ids.shape)


MESH = pl.DeviceIdType.MESH


def dispatch_kernel(z_count, chunks, blk_ref, out_ref, send_sem, recv_sem, local_sem):
    z = lax.axis_index("z")
    c = lax.axis_index("c")
    row = lax.axis_index("dp")
    other = 1 - c
    step = 1 - 2 * c
    fwd = lax.rem(z + step + z_count, z_count)
    bwd = lax.rem(z - step + z_count, z_count)
    fwd_id, bwd_id, pair_id = (row, fwd, c), (row, bwd, c), (row, z, other)
    piece = blk_ref.shape[0] // chunks

    barrier = pltpu.get_barrier_semaphore()
    for target in (fwd_id, bwd_id, pair_id):
        pl.semaphore_signal(barrier, 1, device_id=target, device_id_type=MESH)
    pl.semaphore_wait(barrier, 3)

    mine = c * z_count + z
    local = pltpu.make_async_copy(blk_ref, out_ref.at[mine], local_sem.at[0])
    local.start()
    sends = []

    def part(ref, k):
        return ref.at[pl.ds(k * piece, piece)]

    def send(src, slot, k, target):
        copy = pltpu.make_async_remote_copy(
            src_ref=part(src, k),
            dst_ref=part(out_ref.at[slot], k),
            send_sem=send_sem.at[len(sends)],
            recv_sem=recv_sem.at[slot * chunks + k],
            device_id=target,
            device_id_type=MESH,
        )
        copy.start()
        sends.append(copy)

    def arrive(slot, k):
        view = part(out_ref.at[slot], k)
        pltpu.make_async_remote_copy(
            src_ref=view,
            dst_ref=view,
            send_sem=send_sem.at[0],
            recv_sem=recv_sem.at[slot * chunks + k],
            device_id=pair_id,
            device_id_type=MESH,
        ).wait_recv()

    for k in range(chunks):
        send(blk_ref, mine, k, fwd_id)
        send(blk_ref, mine, k, bwd_id)
    for k in range(chunks):
        send(blk_ref, mine, k, pair_id)
    fwd_hops = z_count // 2
    bwd_hops = z_count - 1 - fwd_hops
    for hop in range(1, fwd_hops + 1):
        for k in range(chunks):
            slot = c * z_count + lax.rem(z - step * hop + 2 * z_count, z_count)
            arrive(slot, k)
            if hop < fwd_hops:
                send(out_ref.at[slot], slot, k, fwd_id)
            send(out_ref.at[slot], slot, k, pair_id)
            if hop <= bwd_hops:
                slot = c * z_count + lax.rem(z + step * hop + 2 * z_count, z_count)
                arrive(slot, k)
                if hop < bwd_hops:
                    send(out_ref.at[slot], slot, k, bwd_id)
                send(out_ref.at[slot], slot, k, pair_id)
    for zz in range(z_count):
        for k in range(chunks):
            arrive(other * z_count + zz, k)
    local.wait()
    for copy in sends:
        copy.wait_send()


def gather_blocks(block, z_count, chunks):
    count = 2 * z_count
    return pl.pallas_call(
        functools.partial(dispatch_kernel, z_count, chunks),
        out_shape=jax.ShapeDtypeStruct((count,) + block.shape, block.dtype),
        in_specs=[pl.BlockSpec(memory_space=pltpu.VMEM)],
        out_specs=pl.BlockSpec(memory_space=pltpu.VMEM),
        scratch_shapes=[
            pltpu.SemaphoreType.DMA((2 * count * chunks,)),
            pltpu.SemaphoreType.DMA((count * chunks,)),
            pltpu.SemaphoreType.DMA((1,)),
        ],
        compiler_params=pltpu.CompilerParams(
            collective_id=0, has_side_effects=True, vmem_limit_bytes=32 * 1024 * 1024
        ),
    )(block)


def combine_kernel(
    z_count, chunks, part_ref, out_ref, pair_buf, fwd_buf, bwd_buf, fwd_out, bwd_out,
    send_sem, recv_sem,
):
    z = lax.axis_index("z")
    c = lax.axis_index("c")
    row = lax.axis_index("dp")
    other = 1 - c
    step = 1 - 2 * c
    fwd = lax.rem(z + step + z_count, z_count)
    bwd = lax.rem(z - step + z_count, z_count)
    fwd_id, bwd_id, pair_id = (row, fwd, c), (row, bwd, c), (row, z, other)
    fwd_hops = z_count // 2
    bwd_hops = z_count - 1 - fwd_hops
    piece = part_ref.shape[2] // chunks

    barrier = pltpu.get_barrier_semaphore()
    for target in (fwd_id, bwd_id, pair_id):
        pl.semaphore_signal(barrier, 1, device_id=target, device_id_type=MESH)
    pl.semaphore_wait(barrier, 3)

    sends = []

    def send(src, dst, sem, target):
        copy = pltpu.make_async_remote_copy(
            src_ref=src,
            dst_ref=dst,
            send_sem=send_sem.at[len(sends)],
            recv_sem=recv_sem.at[sem],
            device_id=target,
            device_id_type=MESH,
        )
        copy.start()
        sends.append(copy)

    def arrive(dst, sem):
        pltpu.make_async_remote_copy(
            src_ref=dst,
            dst_ref=dst,
            send_sem=send_sem.at[0],
            recv_sem=recv_sem.at[sem],
            device_id=pair_id,
            device_id_type=MESH,
        ).wait_recv()

    def order(ring_step):
        dests = []
        for hop in range(1, fwd_hops + 1):
            dests.append(lax.rem(z + ring_step * (fwd_hops + 1 - hop) + 2 * z_count, z_count))
            if hop <= bwd_hops:
                dests.append(lax.rem(z - ring_step * (bwd_hops + 1 - hop) + 2 * z_count, z_count))
        return dests + [z]

    for n, dest in enumerate(order(-step)):
        send(part_ref.at[other, dest], pair_buf.at[n], n, pair_id)
    def own(dest, n, k):
        if k == 0:
            arrive(pair_buf.at[n], n)
        rows = pl.ds(k * piece, piece)
        return part_ref[c, dest, rows].astype(jnp.float32) + pair_buf[n, rows].astype(
            jnp.float32
        )

    fwd_sem = z_count
    bwd_sem = z_count + fwd_hops * chunks
    for hop in range(1, fwd_hops + 1):
        for k in range(chunks):
            rows = pl.ds(k * piece, piece)
            dest = lax.rem(z + step * (fwd_hops + 1 - hop) + 2 * z_count, z_count)
            n = hop - 1 + min(hop - 1, bwd_hops)
            total = own(dest, n, k)
            if hop > 1:
                sem = fwd_sem + (hop - 2) * chunks + k
                arrive(fwd_buf.at[hop - 2, rows], sem)
                total = total + fwd_buf[hop - 2, rows].astype(jnp.float32)
            fwd_out[hop - 1, rows] = total.astype(fwd_out.dtype)
            sem = fwd_sem + (hop - 1) * chunks + k
            send(fwd_out.at[hop - 1, rows], fwd_buf.at[hop - 1, rows], sem, fwd_id)
            if hop <= bwd_hops:
                dest = lax.rem(z - step * (bwd_hops + 1 - hop) + 2 * z_count, z_count)
                total = own(dest, n + 1, k)
                if hop > 1:
                    sem = bwd_sem + (hop - 2) * chunks + k
                    arrive(bwd_buf.at[hop - 2, rows], sem)
                    total = total + bwd_buf[hop - 2, rows].astype(jnp.float32)
                bwd_out[hop - 1, rows] = total.astype(bwd_out.dtype)
                sem = bwd_sem + (hop - 1) * chunks + k
                send(bwd_out.at[hop - 1, rows], bwd_buf.at[hop - 1, rows], sem, bwd_id)
    for k in range(chunks):
        rows = pl.ds(k * piece, piece)
        total = own(z, fwd_hops + bwd_hops, k)
        arrive(fwd_buf.at[fwd_hops - 1, rows], fwd_sem + (fwd_hops - 1) * chunks + k)
        total = total + fwd_buf[fwd_hops - 1, rows].astype(jnp.float32)
        if bwd_hops > 0:
            arrive(bwd_buf.at[bwd_hops - 1, rows], bwd_sem + (bwd_hops - 1) * chunks + k)
            total = total + bwd_buf[bwd_hops - 1, rows].astype(jnp.float32)
        out_ref[rows] = total.astype(out_ref.dtype)
    for copy in sends:
        copy.wait_send()


def scatter_sums(partial, chunks):
    c_count, z_count, rows, width = partial.shape
    fwd_hops = z_count // 2
    bwd_hops = max(z_count - 1 - fwd_hops, 1)
    block = (rows, width)
    vmem = pl.BlockSpec(memory_space=pltpu.VMEM)
    sems = z_count + (fwd_hops + bwd_hops) * chunks
    return pl.pallas_call(
        functools.partial(combine_kernel, z_count, chunks),
        out_shape=jax.ShapeDtypeStruct(block, partial.dtype),
        in_specs=[vmem],
        out_specs=vmem,
        scratch_shapes=[
            pltpu.VMEM((z_count,) + block, partial.dtype),
            pltpu.VMEM((fwd_hops,) + block, partial.dtype),
            pltpu.VMEM((bwd_hops,) + block, partial.dtype),
            pltpu.VMEM((fwd_hops,) + block, partial.dtype),
            pltpu.VMEM((bwd_hops,) + block, partial.dtype),
            pltpu.SemaphoreType.DMA((sems,)),
            pltpu.SemaphoreType.DMA((sems,)),
        ],
        compiler_params=pltpu.CompilerParams(
            collective_id=1, has_side_effects=True, vmem_limit_bytes=48 * 1024 * 1024
        ),
    )(partial)


def body(
    tokens, expert_ids, gate_fixed, scorer_id, direction_tags, w_gate, w_up, w_down, score_head
):
    z_count = lax.axis_size("z")
    c_count = lax.axis_size("c")
    expert_count = z_count * c_count
    per_device = w_gate.shape[0]
    tok_rows, model_width = tokens.shape
    top_count = expert_ids.shape[1]
    which_tag = jnp.repeat(scorer_id, SEQ_LEN)[:, None]
    tag_rows = jnp.where(
        which_tag == 1, direction_tags[1][None, :], direction_tags[0][None, :]
    ).astype(jnp.float32)
    inputs = (tokens.astype(jnp.float32) + tag_rows).astype(jnp.bfloat16)
    rank_in = route_ranks(expert_ids, per_device * expert_count)
    routes = jnp.concatenate(
        [expert_ids, rank_in, gate_fixed // 256, gate_fixed % 256], axis=1
    ).astype(jnp.bfloat16)
    routes = jnp.pad(routes, ((0, 0), (0, 128 - 4 * top_count)))
    block = jnp.concatenate([inputs, routes], axis=1)
    gathered = gather_blocks(block, z_count, 2)
    inputs_all = gathered[:, :, :model_width]
    routes_all = gathered[:, :, model_width : model_width + 4 * top_count].astype(jnp.int32)
    ids_cube = routes_all[..., :top_count]
    rank_cube = routes_all[..., top_count : 2 * top_count]
    fixed_val = (
        routes_all[..., 2 * top_count : 3 * top_count] * 256 + routes_all[..., 3 * top_count :]
    ).astype(jnp.float32)
    weight_cube = fixed_val / jnp.sum(fixed_val, axis=2, keepdims=True)
    my_index = lax.axis_index("z") * c_count + lax.axis_index("c")
    local_count = per_device * MOST
    local_slot = ids_cube - my_index * per_device
    is_mine = (local_slot >= 0) & (local_slot < per_device)
    local_key = jnp.where(is_mine, local_slot * MOST + rank_cube, -1)
    match = (
        local_key[:, None, :, :] == jnp.arange(local_count, dtype=jnp.int32)[None, :, None, None]
    )
    picker = jnp.any(match, axis=3).astype(jnp.bfloat16)
    slot_weight = jnp.sum(jnp.where(match, weight_cube[:, None, :, :], 0.0), axis=(2, 3)).reshape(
        expert_count, per_device, MOST
    )
    row_block = jnp.einsum(
        "sqt,std->sqd", picker, inputs_all, preferred_element_type=jnp.float32
    ).astype(jnp.bfloat16)
    row_block = row_block.reshape(expert_count, per_device, MOST, model_width)
    gate_proj = jnp.einsum("nemd,edf->nemf", row_block, w_gate, preferred_element_type=jnp.float32)
    up_proj = jnp.einsum("nemd,edf->nemf", row_block, w_up, preferred_element_type=jnp.float32)
    hidden = (jax.nn.silu(gate_proj) * up_proj).astype(jnp.bfloat16)
    down_out = jnp.einsum("nemf,efd->nemd", hidden, w_down, preferred_element_type=jnp.float32)
    result = (slot_weight[..., None] * down_out).astype(jnp.bfloat16)
    partial_value = jnp.einsum(
        "sqt,sqd->std",
        picker,
        result.reshape(expert_count, local_count, model_width),
        preferred_element_type=jnp.float32,
    )
    partial_value = partial_value.reshape(c_count, z_count, tok_rows, model_width)
    mixed = scatter_sums(partial_value.astype(jnp.bfloat16), 2)
    token_score = jnp.dot(mixed.astype(jnp.float32), score_head, precision=lax.Precision.HIGHEST)
    seq_score = token_score.reshape(-1, SEQ_LEN).sum(axis=1)
    partner = from_partner(seq_score, "dp", lax.axis_size("dp").bit_length() - 2)
    pair_score = jnp.abs(seq_score - partner) + 0.5 * (seq_score + partner)
    return (mixed, pair_score)


def solution(mesh):
    dp_count, expert_count = mesh.devices.shape
    split = Mesh(mesh.devices.reshape(dp_count, expert_count // 2, 2), ("dp", "z", "c"))
    rows = P(("dp", "z", "c"), None)
    return jax.shard_map(
        body,
        mesh=split,
        in_specs=(
            rows,
            rows,
            rows,
            P(("dp", "z", "c")),
            P(),
            P(("z", "c"), None, None),
            P(("z", "c"), None, None),
            P(("z", "c"), None, None),
            P(),
        ),
        out_specs=(rows, P(("dp", "z", "c"))),
        check_vma=False,
    )
```

```python
import functools

import jax
import jax.numpy as jnp
from jax import lax
from jax.experimental import pallas as pl
from jax.experimental.pallas import tpu as pltpu
from jax.sharding import Mesh
from jax.sharding import PartitionSpec as P

SEQ_LEN = 16
MOST = 24


def from_partner(block, axis, bit):
    count = lax.axis_size(axis)
    route = []
    for low in range(count):
        high = low | 1 << bit
        if high != low and high < count:
            route += [(low, high), (high, low)]
    return lax.ppermute(block, axis, route)


def route_ranks(expert_ids, expert_total):
    flat_ids = expert_ids.reshape(-1)
    entry_count = flat_ids.shape[0]
    onehot = flat_ids[:, None] == jnp.arange(expert_total, dtype=jnp.int32)[None, :]
    positions = jnp.arange(entry_count, dtype=jnp.int32)
    earlier = (positions[:, None] > positions[None, :]).astype(jnp.bfloat16)
    counts = jnp.dot(earlier, onehot.astype(jnp.bfloat16), preferred_element_type=jnp.float32)
    rank_in = jnp.sum(jnp.where(onehot, counts, 0.0), axis=1).astype(jnp.int32)
    return rank_in.reshape(expert_ids.shape)


MESH = pl.DeviceIdType.MESH


def dispatch_kernel(z_count, chunks, blk_ref, out_ref, send_sem, recv_sem, local_sem):
    z = lax.axis_index("z")
    c = lax.axis_index("c")
    row = lax.axis_index("dp")
    other = 1 - c
    step = 1 - 2 * c
    fwd = lax.rem(z + step + z_count, z_count)
    bwd = lax.rem(z - step + z_count, z_count)
    fwd_id, bwd_id, pair_id = (row, fwd, c), (row, bwd, c), (row, z, other)
    piece = blk_ref.shape[0] // chunks

    barrier = pltpu.get_barrier_semaphore()
    for target in (fwd_id, bwd_id, pair_id):
        pl.semaphore_signal(barrier, 1, device_id=target, device_id_type=MESH)
    pl.semaphore_wait(barrier, 3)

    mine = c * z_count + z
    local = pltpu.make_async_copy(blk_ref, out_ref.at[mine], local_sem.at[0])
    local.start()
    sends = []

    def part(ref, k):
        return ref.at[pl.ds(k * piece, piece)]

    def send(src, slot, k, target):
        copy = pltpu.make_async_remote_copy(
            src_ref=part(src, k),
            dst_ref=part(out_ref.at[slot], k),
            send_sem=send_sem.at[len(sends)],
            recv_sem=recv_sem.at[slot * chunks + k],
            device_id=target,
            device_id_type=MESH,
        )
        copy.start()
        sends.append(copy)

    def arrive(slot, k):
        view = part(out_ref.at[slot], k)
        pltpu.make_async_remote_copy(
            src_ref=view,
            dst_ref=view,
            send_sem=send_sem.at[0],
            recv_sem=recv_sem.at[slot * chunks + k],
            device_id=pair_id,
            device_id_type=MESH,
        ).wait_recv()

    for k in range(chunks):
        send(blk_ref, mine, k, fwd_id)
        send(blk_ref, mine, k, bwd_id)
    for k in range(chunks):
        send(blk_ref, mine, k, pair_id)
    fwd_hops = z_count // 2
    bwd_hops = z_count - 1 - fwd_hops
    for hop in range(1, fwd_hops + 1):
        for k in range(chunks):
            slot = c * z_count + lax.rem(z - step * hop + 2 * z_count, z_count)
            arrive(slot, k)
            if hop < fwd_hops:
                send(out_ref.at[slot], slot, k, fwd_id)
            send(out_ref.at[slot], slot, k, pair_id)
            if hop <= bwd_hops:
                slot = c * z_count + lax.rem(z + step * hop + 2 * z_count, z_count)
                arrive(slot, k)
                if hop < bwd_hops:
                    send(out_ref.at[slot], slot, k, bwd_id)
                send(out_ref.at[slot], slot, k, pair_id)
    for zz in range(z_count):
        for k in range(chunks):
            arrive(other * z_count + zz, k)
    local.wait()
    for copy in sends:
        copy.wait_send()


def gather_blocks(block, z_count, chunks):
    count = 2 * z_count
    return pl.pallas_call(
        functools.partial(dispatch_kernel, z_count, chunks),
        out_shape=jax.ShapeDtypeStruct((count,) + block.shape, block.dtype),
        in_specs=[pl.BlockSpec(memory_space=pltpu.VMEM)],
        out_specs=pl.BlockSpec(memory_space=pltpu.VMEM),
        scratch_shapes=[
            pltpu.SemaphoreType.DMA((2 * count * chunks,)),
            pltpu.SemaphoreType.DMA((count * chunks,)),
            pltpu.SemaphoreType.DMA((1,)),
        ],
        compiler_params=pltpu.CompilerParams(
            collective_id=0, has_side_effects=True, vmem_limit_bytes=32 * 1024 * 1024
        ),
    )(block)


def combine_kernel(
    z_count, dp_count, seq_len, chunks, part_ref, head_ref, out_ref, pair_out, pair_buf,
    fwd_buf, bwd_buf, fwd_out, bwd_out, seq_out, seq_in, send_sem, recv_sem, seq_sem,
):
    z = lax.axis_index("z")
    c = lax.axis_index("c")
    row = lax.axis_index("dp")
    other = 1 - c
    step = 1 - 2 * c
    fwd = lax.rem(z + step + z_count, z_count)
    bwd = lax.rem(z - step + z_count, z_count)
    fwd_id, bwd_id, pair_id = (row, fwd, c), (row, bwd, c), (row, z, other)
    mate_id = (lax.rem(row + dp_count // 2, dp_count), z, c)
    fwd_hops = z_count // 2
    bwd_hops = z_count - 1 - fwd_hops
    piece = part_ref.shape[2] // chunks

    barrier = pltpu.get_barrier_semaphore()
    for target in (fwd_id, bwd_id, pair_id, mate_id):
        pl.semaphore_signal(barrier, 1, device_id=target, device_id_type=MESH)
    pl.semaphore_wait(barrier, 4)

    sends = []

    def send(src, dst, sem, target):
        copy = pltpu.make_async_remote_copy(
            src_ref=src,
            dst_ref=dst,
            send_sem=send_sem.at[len(sends)],
            recv_sem=recv_sem.at[sem],
            device_id=target,
            device_id_type=MESH,
        )
        copy.start()
        sends.append(copy)

    def arrive(dst, sem):
        pltpu.make_async_remote_copy(
            src_ref=dst,
            dst_ref=dst,
            send_sem=send_sem.at[0],
            recv_sem=recv_sem.at[sem],
            device_id=pair_id,
            device_id_type=MESH,
        ).wait_recv()

    def order(ring_step):
        dests = []
        for hop in range(1, fwd_hops + 1):
            dests.append(lax.rem(z + ring_step * (fwd_hops + 1 - hop) + 2 * z_count, z_count))
            if hop <= bwd_hops:
                dests.append(lax.rem(z - ring_step * (bwd_hops + 1 - hop) + 2 * z_count, z_count))
        return dests + [z]

    for n, dest in enumerate(order(-step)):
        send(part_ref.at[other, dest], pair_buf.at[n], n, pair_id)
    def own(dest, n, k):
        if k == 0:
            arrive(pair_buf.at[n], n)
        rows = pl.ds(k * piece, piece)
        return part_ref[c, dest, rows].astype(jnp.float32) + pair_buf[n, rows].astype(
            jnp.float32
        )

    fwd_sem = z_count
    bwd_sem = z_count + fwd_hops * chunks
    for hop in range(1, fwd_hops + 1):
        for k in range(chunks):
            rows = pl.ds(k * piece, piece)
            dest = lax.rem(z + step * (fwd_hops + 1 - hop) + 2 * z_count, z_count)
            n = hop - 1 + min(hop - 1, bwd_hops)
            total = own(dest, n, k)
            if hop > 1:
                sem = fwd_sem + (hop - 2) * chunks + k
                arrive(fwd_buf.at[hop - 2, rows], sem)
                total = total + fwd_buf[hop - 2, rows].astype(jnp.float32)
            fwd_out[hop - 1, rows] = total.astype(fwd_out.dtype)
            sem = fwd_sem + (hop - 1) * chunks + k
            send(fwd_out.at[hop - 1, rows], fwd_buf.at[hop - 1, rows], sem, fwd_id)
            if hop <= bwd_hops:
                dest = lax.rem(z - step * (bwd_hops + 1 - hop) + 2 * z_count, z_count)
                total = own(dest, n + 1, k)
                if hop > 1:
                    sem = bwd_sem + (hop - 2) * chunks + k
                    arrive(bwd_buf.at[hop - 2, rows], sem)
                    total = total + bwd_buf[hop - 2, rows].astype(jnp.float32)
                bwd_out[hop - 1, rows] = total.astype(bwd_out.dtype)
                sem = bwd_sem + (hop - 1) * chunks + k
                send(bwd_out.at[hop - 1, rows], bwd_buf.at[hop - 1, rows], sem, bwd_id)
    for k in range(chunks):
        rows = pl.ds(k * piece, piece)
        total = own(z, fwd_hops + bwd_hops, k)
        arrive(fwd_buf.at[fwd_hops - 1, rows], fwd_sem + (fwd_hops - 1) * chunks + k)
        total = total + fwd_buf[fwd_hops - 1, rows].astype(jnp.float32)
        if bwd_hops > 0:
            arrive(bwd_buf.at[bwd_hops - 1, rows], bwd_sem + (bwd_hops - 1) * chunks + k)
            total = total + bwd_buf[bwd_hops - 1, rows].astype(jnp.float32)
        out_ref[rows] = total.astype(out_ref.dtype)
    tok_rows, width = out_ref.shape
    seqs = tok_rows // seq_len
    scored = out_ref[...].astype(jnp.float32) * head_ref[...]
    per_seq = jnp.sum(scored.reshape(seqs, seq_len, width), axis=1)
    seq_score = jnp.sum(per_seq, axis=1, keepdims=True)
    seq_out[...] = jnp.zeros(seq_out.shape, jnp.float32)
    seq_out[pl.ds(0, seqs)] = jnp.broadcast_to(seq_score, (seqs, seq_out.shape[1]))
    mate = pltpu.make_async_remote_copy(
        src_ref=seq_out,
        dst_ref=seq_in,
        send_sem=seq_sem.at[0],
        recv_sem=seq_sem.at[1],
        device_id=mate_id,
        device_id_type=MESH,
    )
    mate.start()
    mate.wait()
    mine = seq_out[...]
    theirs = seq_in[...]
    pair_out[...] = jnp.abs(mine - theirs) + 0.5 * (mine + theirs)
    for copy in sends:
        copy.wait_send()


def scatter_sums(partial, score_head, dp_count, seq_len, chunks):
    c_count, z_count, rows, width = partial.shape
    fwd_hops = z_count // 2
    bwd_hops = max(z_count - 1 - fwd_hops, 1)
    block = (rows, width)
    vmem = pl.BlockSpec(memory_space=pltpu.VMEM)
    sems = z_count + (fwd_hops + bwd_hops) * chunks
    tile = (8, 128)
    return pl.pallas_call(
        functools.partial(combine_kernel, z_count, dp_count, seq_len, chunks),
        out_shape=(
            jax.ShapeDtypeStruct(block, partial.dtype),
            jax.ShapeDtypeStruct(tile, jnp.float32),
        ),
        in_specs=[vmem, vmem],
        out_specs=(vmem, vmem),
        scratch_shapes=[
            pltpu.VMEM((z_count,) + block, partial.dtype),
            pltpu.VMEM((fwd_hops,) + block, partial.dtype),
            pltpu.VMEM((bwd_hops,) + block, partial.dtype),
            pltpu.VMEM((fwd_hops,) + block, partial.dtype),
            pltpu.VMEM((bwd_hops,) + block, partial.dtype),
            pltpu.VMEM(tile, jnp.float32),
            pltpu.VMEM(tile, jnp.float32),
            pltpu.SemaphoreType.DMA((sems,)),
            pltpu.SemaphoreType.DMA((sems,)),
            pltpu.SemaphoreType.DMA((2,)),
        ],
        compiler_params=pltpu.CompilerParams(
            collective_id=1, has_side_effects=True, vmem_limit_bytes=48 * 1024 * 1024
        ),
    )(partial, score_head.reshape(1, -1))


def body(
    tokens, expert_ids, gate_fixed, scorer_id, direction_tags, w_gate, w_up, w_down, score_head
):
    z_count = lax.axis_size("z")
    c_count = lax.axis_size("c")
    expert_count = z_count * c_count
    per_device = w_gate.shape[0]
    tok_rows, model_width = tokens.shape
    top_count = expert_ids.shape[1]
    which_tag = jnp.repeat(scorer_id, SEQ_LEN)[:, None]
    tag_rows = jnp.where(
        which_tag == 1, direction_tags[1][None, :], direction_tags[0][None, :]
    ).astype(jnp.float32)
    inputs = (tokens.astype(jnp.float32) + tag_rows).astype(jnp.bfloat16)
    rank_in = route_ranks(expert_ids, per_device * expert_count)
    routes = jnp.concatenate(
        [expert_ids, rank_in, gate_fixed // 256, gate_fixed % 256], axis=1
    ).astype(jnp.bfloat16)
    routes = jnp.pad(routes, ((0, 0), (0, 128 - 4 * top_count)))
    block = jnp.concatenate([inputs, routes], axis=1)
    gathered = gather_blocks(block, z_count, 2)
    inputs_all = gathered[:, :, :model_width]
    routes_all = gathered[:, :, model_width : model_width + 4 * top_count].astype(jnp.int32)
    ids_cube = routes_all[..., :top_count]
    rank_cube = routes_all[..., top_count : 2 * top_count]
    fixed_val = (
        routes_all[..., 2 * top_count : 3 * top_count] * 256 + routes_all[..., 3 * top_count :]
    ).astype(jnp.float32)
    weight_cube = fixed_val / jnp.sum(fixed_val, axis=2, keepdims=True)
    my_index = lax.axis_index("z") * c_count + lax.axis_index("c")
    local_count = per_device * MOST
    local_slot = ids_cube - my_index * per_device
    is_mine = (local_slot >= 0) & (local_slot < per_device)
    local_key = jnp.where(is_mine, local_slot * MOST + rank_cube, -1)
    match = (
        local_key[:, None, :, :] == jnp.arange(local_count, dtype=jnp.int32)[None, :, None, None]
    )
    picker = jnp.any(match, axis=3).astype(jnp.bfloat16)
    slot_weight = jnp.sum(jnp.where(match, weight_cube[:, None, :, :], 0.0), axis=(2, 3)).reshape(
        expert_count, per_device, MOST
    )
    row_block = jnp.einsum(
        "sqt,std->sqd", picker, inputs_all, preferred_element_type=jnp.float32
    ).astype(jnp.bfloat16)
    row_block = row_block.reshape(expert_count, per_device, MOST, model_width)
    gate_proj = jnp.einsum("nemd,edf->nemf", row_block, w_gate, preferred_element_type=jnp.float32)
    up_proj = jnp.einsum("nemd,edf->nemf", row_block, w_up, preferred_element_type=jnp.float32)
    hidden = (jax.nn.silu(gate_proj) * up_proj).astype(jnp.bfloat16)
    down_out = jnp.einsum("nemf,efd->nemd", hidden, w_down, preferred_element_type=jnp.float32)
    result = (slot_weight[..., None] * down_out).astype(jnp.bfloat16)
    partial_value = jnp.einsum(
        "sqt,sqd->std",
        picker,
        result.reshape(expert_count, local_count, model_width),
        preferred_element_type=jnp.float32,
    )
    partial_value = partial_value.reshape(c_count, z_count, tok_rows, model_width)
    mixed, pair_tile = scatter_sums(
        partial_value.astype(jnp.bfloat16), score_head, lax.axis_size("dp"), SEQ_LEN, 2
    )
    pair_score = pair_tile[: tok_rows // SEQ_LEN, 0]
    return (mixed, pair_score)


def solution(mesh):
    dp_count, expert_count = mesh.devices.shape
    split = Mesh(mesh.devices.reshape(dp_count, expert_count // 2, 2), ("dp", "z", "c"))
    rows = P(("dp", "z", "c"), None)
    return jax.shard_map(
        body,
        mesh=split,
        in_specs=(
            rows,
            rows,
            rows,
            P(("dp", "z", "c")),
            P(),
            P(("z", "c"), None, None),
            P(("z", "c"), None, None),
            P(("z", "c"), None, None),
            P(),
        ),
        out_specs=(rows, P(("dp", "z", "c"))),
        check_vma=False,
    )
```

```python
import functools

import jax
import jax.numpy as jnp
from jax import lax
from jax.experimental import pallas as pl
from jax.experimental.pallas import tpu as pltpu
from jax.sharding import Mesh
from jax.sharding import PartitionSpec as P

SEQ_LEN = 16
MOST = 24


def from_partner(block, axis, bit):
    count = lax.axis_size(axis)
    route = []
    for low in range(count):
        high = low | 1 << bit
        if high != low and high < count:
            route += [(low, high), (high, low)]
    return lax.ppermute(block, axis, route)


def route_ranks(expert_ids, expert_total):
    flat_ids = expert_ids.reshape(-1)
    entry_count = flat_ids.shape[0]
    onehot = flat_ids[:, None] == jnp.arange(expert_total, dtype=jnp.int32)[None, :]
    positions = jnp.arange(entry_count, dtype=jnp.int32)
    earlier = (positions[:, None] > positions[None, :]).astype(jnp.bfloat16)
    counts = jnp.dot(earlier, onehot.astype(jnp.bfloat16), preferred_element_type=jnp.float32)
    rank_in = jnp.sum(jnp.where(onehot, counts, 0.0), axis=1).astype(jnp.int32)
    return rank_in.reshape(expert_ids.shape)


MESH = pl.DeviceIdType.MESH


def dispatch_kernel(z_count, chunks, blk_ref, out_ref, send_sem, recv_sem, local_sem):
    z = lax.axis_index("z")
    c = lax.axis_index("c")
    row = lax.axis_index("dp")
    other = 1 - c
    step = 1 - 2 * c
    fwd = lax.rem(z + step + z_count, z_count)
    bwd = lax.rem(z - step + z_count, z_count)
    fwd_id, bwd_id, pair_id = (row, fwd, c), (row, bwd, c), (row, z, other)
    piece = blk_ref.shape[0] // chunks

    barrier = pltpu.get_barrier_semaphore()
    for target in (fwd_id, bwd_id, pair_id):
        pl.semaphore_signal(barrier, 1, device_id=target, device_id_type=MESH)
    pl.semaphore_wait(barrier, 3)

    mine = c * z_count + z
    local = pltpu.make_async_copy(blk_ref, out_ref.at[mine], local_sem.at[0])
    local.start()
    sends = []

    def part(ref, k):
        return ref.at[pl.ds(k * piece, piece)]

    def send(src, slot, k, target):
        copy = pltpu.make_async_remote_copy(
            src_ref=part(src, k),
            dst_ref=part(out_ref.at[slot], k),
            send_sem=send_sem.at[len(sends)],
            recv_sem=recv_sem.at[slot * chunks + k],
            device_id=target,
            device_id_type=MESH,
        )
        copy.start()
        sends.append(copy)

    def arrive(slot, k):
        view = part(out_ref.at[slot], k)
        pltpu.make_async_remote_copy(
            src_ref=view,
            dst_ref=view,
            send_sem=send_sem.at[0],
            recv_sem=recv_sem.at[slot * chunks + k],
            device_id=pair_id,
            device_id_type=MESH,
        ).wait_recv()

    for k in range(chunks):
        send(blk_ref, mine, k, fwd_id)
        send(blk_ref, mine, k, bwd_id)
    for k in range(chunks):
        send(blk_ref, mine, k, pair_id)
    fwd_hops = z_count // 2
    bwd_hops = z_count - 1 - fwd_hops
    for hop in range(1, fwd_hops + 1):
        for k in range(chunks):
            slot = c * z_count + lax.rem(z - step * hop + 2 * z_count, z_count)
            arrive(slot, k)
            if hop < fwd_hops:
                send(out_ref.at[slot], slot, k, fwd_id)
            send(out_ref.at[slot], slot, k, pair_id)
            if hop <= bwd_hops:
                slot = c * z_count + lax.rem(z + step * hop + 2 * z_count, z_count)
                arrive(slot, k)
                if hop < bwd_hops:
                    send(out_ref.at[slot], slot, k, bwd_id)
                send(out_ref.at[slot], slot, k, pair_id)
    for zz in range(z_count):
        for k in range(chunks):
            arrive(other * z_count + zz, k)
    local.wait()
    for copy in sends:
        copy.wait_send()


def gather_blocks(block, z_count, chunks):
    count = 2 * z_count
    return pl.pallas_call(
        functools.partial(dispatch_kernel, z_count, chunks),
        out_shape=jax.ShapeDtypeStruct((count,) + block.shape, block.dtype),
        in_specs=[pl.BlockSpec(memory_space=pltpu.VMEM)],
        out_specs=pl.BlockSpec(memory_space=pltpu.VMEM),
        scratch_shapes=[
            pltpu.SemaphoreType.DMA((2 * count * chunks,)),
            pltpu.SemaphoreType.DMA((count * chunks,)),
            pltpu.SemaphoreType.DMA((1,)),
        ],
        compiler_params=pltpu.CompilerParams(
            collective_id=0, has_side_effects=True, vmem_limit_bytes=32 * 1024 * 1024
        ),
    )(block)


def combine_kernel(
    z_count, dp_count, seq_len, chunks, part_ref, head_ref, out_ref, pair_out, pair_buf,
    fwd_buf, bwd_buf, fwd_out, bwd_out, seq_out, seq_in, send_sem, recv_sem, seq_sem,
):
    z = lax.axis_index("z")
    c = lax.axis_index("c")
    row = lax.axis_index("dp")
    other = 1 - c
    step = 1 - 2 * c
    fwd = lax.rem(z + step + z_count, z_count)
    bwd = lax.rem(z - step + z_count, z_count)
    fwd_id, bwd_id, pair_id = (row, fwd, c), (row, bwd, c), (row, z, other)
    mate_id = (lax.rem(row + dp_count // 2, dp_count), z, c)
    fwd_hops = z_count // 2
    bwd_hops = z_count - 1 - fwd_hops
    piece = part_ref.shape[2] // chunks

    barrier = pltpu.get_barrier_semaphore()
    for target in (fwd_id, bwd_id, pair_id, mate_id):
        pl.semaphore_signal(barrier, 1, device_id=target, device_id_type=MESH)
    pl.semaphore_wait(barrier, 4)

    sends = []

    def send(src, dst, sem, target):
        copy = pltpu.make_async_remote_copy(
            src_ref=src,
            dst_ref=dst,
            send_sem=send_sem.at[len(sends)],
            recv_sem=recv_sem.at[sem],
            device_id=target,
            device_id_type=MESH,
        )
        copy.start()
        sends.append(copy)

    def arrive(dst, sem):
        pltpu.make_async_remote_copy(
            src_ref=dst,
            dst_ref=dst,
            send_sem=send_sem.at[0],
            recv_sem=recv_sem.at[sem],
            device_id=pair_id,
            device_id_type=MESH,
        ).wait_recv()

    def order(ring_step):
        dests = []
        for hop in range(1, fwd_hops + 1):
            dests.append(lax.rem(z + ring_step * (fwd_hops + 1 - hop) + 2 * z_count, z_count))
            if hop <= bwd_hops:
                dests.append(lax.rem(z - ring_step * (bwd_hops + 1 - hop) + 2 * z_count, z_count))
        return dests + [z]

    for n, dest in enumerate(order(-step)):
        send(part_ref.at[other, dest], pair_buf.at[n], n, pair_id)
    def own(dest, n, k):
        if k == 0:
            arrive(pair_buf.at[n], n)
        rows = pl.ds(k * piece, piece)
        return part_ref[c, dest, rows].astype(jnp.float32) + pair_buf[n, rows].astype(
            jnp.float32
        )

    fwd_sem = z_count
    bwd_sem = z_count + fwd_hops * chunks
    for hop in range(1, fwd_hops + 1):
        for k in range(chunks):
            rows = pl.ds(k * piece, piece)
            dest = lax.rem(z + step * (fwd_hops + 1 - hop) + 2 * z_count, z_count)
            n = hop - 1 + min(hop - 1, bwd_hops)
            total = own(dest, n, k)
            if hop > 1:
                sem = fwd_sem + (hop - 2) * chunks + k
                arrive(fwd_buf.at[hop - 2, rows], sem)
                total = total + fwd_buf[hop - 2, rows].astype(jnp.float32)
            fwd_out[hop - 1, rows] = total.astype(fwd_out.dtype)
            sem = fwd_sem + (hop - 1) * chunks + k
            send(fwd_out.at[hop - 1, rows], fwd_buf.at[hop - 1, rows], sem, fwd_id)
            if hop <= bwd_hops:
                dest = lax.rem(z - step * (bwd_hops + 1 - hop) + 2 * z_count, z_count)
                total = own(dest, n + 1, k)
                if hop > 1:
                    sem = bwd_sem + (hop - 2) * chunks + k
                    arrive(bwd_buf.at[hop - 2, rows], sem)
                    total = total + bwd_buf[hop - 2, rows].astype(jnp.float32)
                bwd_out[hop - 1, rows] = total.astype(bwd_out.dtype)
                sem = bwd_sem + (hop - 1) * chunks + k
                send(bwd_out.at[hop - 1, rows], bwd_buf.at[hop - 1, rows], sem, bwd_id)
    for k in range(chunks):
        rows = pl.ds(k * piece, piece)
        total = own(z, fwd_hops + bwd_hops, k)
        arrive(fwd_buf.at[fwd_hops - 1, rows], fwd_sem + (fwd_hops - 1) * chunks + k)
        total = total + fwd_buf[fwd_hops - 1, rows].astype(jnp.float32)
        if bwd_hops > 0:
            arrive(bwd_buf.at[bwd_hops - 1, rows], bwd_sem + (bwd_hops - 1) * chunks + k)
            total = total + bwd_buf[bwd_hops - 1, rows].astype(jnp.float32)
        out_ref[rows] = total.astype(out_ref.dtype)
    tok_rows, width = out_ref.shape
    seqs = tok_rows // seq_len
    scored = out_ref[...].astype(jnp.float32) * head_ref[...]
    per_seq = jnp.sum(scored.reshape(seqs, seq_len, width), axis=1)
    seq_score = jnp.sum(per_seq, axis=1, keepdims=True)
    seq_out[...] = jnp.zeros(seq_out.shape, jnp.float32)
    seq_out[pl.ds(0, seqs)] = jnp.broadcast_to(seq_score, (seqs, seq_out.shape[1]))
    mate = pltpu.make_async_remote_copy(
        src_ref=seq_out,
        dst_ref=seq_in,
        send_sem=seq_sem.at[0],
        recv_sem=seq_sem.at[1],
        device_id=mate_id,
        device_id_type=MESH,
    )
    mate.start()
    mate.wait()
    mine = seq_out[...]
    theirs = seq_in[...]
    pair_out[...] = jnp.abs(mine - theirs) + 0.5 * (mine + theirs)
    for copy in sends:
        copy.wait_send()


def scatter_sums(partial, score_head, dp_count, seq_len, chunks):
    c_count, z_count, rows, width = partial.shape
    fwd_hops = z_count // 2
    bwd_hops = max(z_count - 1 - fwd_hops, 1)
    block = (rows, width)
    vmem = pl.BlockSpec(memory_space=pltpu.VMEM)
    sems = z_count + (fwd_hops + bwd_hops) * chunks
    tile = (8, 128)
    return pl.pallas_call(
        functools.partial(combine_kernel, z_count, dp_count, seq_len, chunks),
        out_shape=(
            jax.ShapeDtypeStruct(block, partial.dtype),
            jax.ShapeDtypeStruct(tile, jnp.float32),
        ),
        in_specs=[vmem, vmem],
        out_specs=(vmem, vmem),
        scratch_shapes=[
            pltpu.VMEM((z_count,) + block, partial.dtype),
            pltpu.VMEM((fwd_hops,) + block, partial.dtype),
            pltpu.VMEM((bwd_hops,) + block, partial.dtype),
            pltpu.VMEM((fwd_hops,) + block, partial.dtype),
            pltpu.VMEM((bwd_hops,) + block, partial.dtype),
            pltpu.VMEM(tile, jnp.float32),
            pltpu.VMEM(tile, jnp.float32),
            pltpu.SemaphoreType.DMA((sems,)),
            pltpu.SemaphoreType.DMA((sems,)),
            pltpu.SemaphoreType.DMA((2,)),
        ],
        compiler_params=pltpu.CompilerParams(
            collective_id=1, has_side_effects=True, vmem_limit_bytes=48 * 1024 * 1024
        ),
    )(partial, score_head.reshape(1, -1))


def body(
    tokens, expert_ids, gate_fixed, scorer_id, direction_tags, w_gate, w_up, w_down, score_head
):
    z_count = lax.axis_size("z")
    c_count = lax.axis_size("c")
    expert_count = z_count * c_count
    per_device = w_gate.shape[0]
    tok_rows, model_width = tokens.shape
    top_count = expert_ids.shape[1]
    which_tag = jnp.repeat(scorer_id, SEQ_LEN)[:, None]
    tag_rows = jnp.where(
        which_tag == 1, direction_tags[1][None, :], direction_tags[0][None, :]
    ).astype(jnp.float32)
    inputs = (tokens.astype(jnp.float32) + tag_rows).astype(jnp.bfloat16)
    rank_in = route_ranks(expert_ids, per_device * expert_count)
    routes = jnp.concatenate(
        [expert_ids, rank_in, gate_fixed // 256, gate_fixed % 256], axis=1
    ).astype(jnp.bfloat16)
    routes = jnp.pad(routes, ((0, 0), (0, 128 - 4 * top_count)))
    block = jnp.concatenate([inputs, routes], axis=1)
    gathered = gather_blocks(block, z_count, 2)
    inputs_all = gathered[:, :, :model_width]
    routes_all = gathered[:, :, model_width : model_width + 4 * top_count].astype(jnp.int32)
    ids_cube = routes_all[..., :top_count]
    rank_cube = routes_all[..., top_count : 2 * top_count]
    fixed_val = (
        routes_all[..., 2 * top_count : 3 * top_count] * 256 + routes_all[..., 3 * top_count :]
    ).astype(jnp.float32)
    weight_cube = fixed_val / jnp.sum(fixed_val, axis=2, keepdims=True)
    my_index = lax.axis_index("z") * c_count + lax.axis_index("c")
    local_count = per_device * MOST
    local_slot = ids_cube - my_index * per_device
    is_mine = (local_slot >= 0) & (local_slot < per_device)
    local_key = jnp.where(is_mine, local_slot * MOST + rank_cube, -1)
    match = (
        local_key[:, None, :, :] == jnp.arange(local_count, dtype=jnp.int32)[None, :, None, None]
    )
    picker = jnp.any(match, axis=3).astype(jnp.bfloat16)
    slot_weight = jnp.sum(jnp.where(match, weight_cube[:, None, :, :], 0.0), axis=(2, 3))
    picker = picker.reshape(expert_count, per_device, MOST, tok_rows).transpose(1, 0, 2, 3)
    slot_weight = slot_weight.reshape(expert_count, per_device, MOST).transpose(1, 0, 2)
    row_block = jnp.einsum(
        "esmt,std->esmd", picker, inputs_all, preferred_element_type=jnp.float32
    ).astype(jnp.bfloat16)
    gate_proj = jnp.einsum("esmd,edf->esmf", row_block, w_gate, preferred_element_type=jnp.float32)
    up_proj = jnp.einsum("esmd,edf->esmf", row_block, w_up, preferred_element_type=jnp.float32)
    hidden = (jax.nn.silu(gate_proj) * up_proj).astype(jnp.bfloat16)
    down_out = jnp.einsum("esmf,efd->esmd", hidden, w_down, preferred_element_type=jnp.float32)
    result = (slot_weight[..., None] * down_out).astype(jnp.bfloat16)
    partial_value = jnp.einsum(
        "esmt,esmd->std", picker, result, preferred_element_type=jnp.float32
    )
    partial_value = partial_value.reshape(c_count, z_count, tok_rows, model_width)
    mixed, pair_tile = scatter_sums(
        partial_value.astype(jnp.bfloat16), score_head, lax.axis_size("dp"), SEQ_LEN, 2
    )
    pair_score = pair_tile[: tok_rows // SEQ_LEN, 0]
    return (mixed, pair_score)


def solution(mesh):
    dp_count, expert_count = mesh.devices.shape
    split = Mesh(mesh.devices.reshape(dp_count, expert_count // 2, 2), ("dp", "z", "c"))
    rows = P(("dp", "z", "c"), None)
    return jax.shard_map(
        body,
        mesh=split,
        in_specs=(
            rows,
            rows,
            rows,
            P(("dp", "z", "c")),
            P(),
            P(("z", "c"), None, None),
            P(("z", "c"), None, None),
            P(("z", "c"), None, None),
            P(),
        ),
        out_specs=(rows, P(("dp", "z", "c"))),
        check_vma=False,
    )
```

```python
import functools

import jax
import jax.numpy as jnp
from jax import lax
from jax.experimental import pallas as pl
from jax.experimental.pallas import tpu as pltpu
from jax.sharding import Mesh
from jax.sharding import PartitionSpec as P

SEQ_LEN = 16
MOST = 24


def from_partner(block, axis, bit):
    count = lax.axis_size(axis)
    route = []
    for low in range(count):
        high = low | 1 << bit
        if high != low and high < count:
            route += [(low, high), (high, low)]
    return lax.ppermute(block, axis, route)


def route_ranks(expert_ids, expert_total):
    flat_ids = expert_ids.reshape(-1)
    entry_count = flat_ids.shape[0]
    onehot = flat_ids[:, None] == jnp.arange(expert_total, dtype=jnp.int32)[None, :]
    positions = jnp.arange(entry_count, dtype=jnp.int32)
    earlier = (positions[:, None] > positions[None, :]).astype(jnp.bfloat16)
    counts = jnp.dot(earlier, onehot.astype(jnp.bfloat16), preferred_element_type=jnp.float32)
    rank_in = jnp.sum(jnp.where(onehot, counts, 0.0), axis=1).astype(jnp.int32)
    return rank_in.reshape(expert_ids.shape)


MESH = pl.DeviceIdType.MESH


def dispatch_kernel(z_count, chunks, blk_ref, out_ref, send_sem, recv_sem, local_sem):
    z = lax.axis_index("z")
    c = lax.axis_index("c")
    row = lax.axis_index("dp")
    other = 1 - c
    step = 1 - 2 * c
    fwd = lax.rem(z + step + z_count, z_count)
    bwd = lax.rem(z - step + z_count, z_count)
    fwd_id, bwd_id, pair_id = (row, fwd, c), (row, bwd, c), (row, z, other)
    piece = blk_ref.shape[0] // chunks

    barrier = pltpu.get_barrier_semaphore()
    for target in (fwd_id, bwd_id, pair_id):
        pl.semaphore_signal(barrier, 1, device_id=target, device_id_type=MESH)
    pl.semaphore_wait(barrier, 3)

    mine = c * z_count + z
    local = pltpu.make_async_copy(blk_ref, out_ref.at[mine], local_sem.at[0])
    local.start()
    sends = []

    def part(ref, k):
        return ref.at[pl.ds(k * piece, piece)]

    def send(src, slot, k, target):
        copy = pltpu.make_async_remote_copy(
            src_ref=part(src, k),
            dst_ref=part(out_ref.at[slot], k),
            send_sem=send_sem.at[len(sends)],
            recv_sem=recv_sem.at[slot * chunks + k],
            device_id=target,
            device_id_type=MESH,
        )
        copy.start()
        sends.append(copy)

    def arrive(slot, k):
        view = part(out_ref.at[slot], k)
        pltpu.make_async_remote_copy(
            src_ref=view,
            dst_ref=view,
            send_sem=send_sem.at[0],
            recv_sem=recv_sem.at[slot * chunks + k],
            device_id=pair_id,
            device_id_type=MESH,
        ).wait_recv()

    for k in range(chunks):
        send(blk_ref, mine, k, fwd_id)
        send(blk_ref, mine, k, bwd_id)
    for k in range(chunks):
        send(blk_ref, mine, k, pair_id)
    fwd_hops = z_count // 2
    bwd_hops = z_count - 1 - fwd_hops
    for hop in range(1, fwd_hops + 1):
        for k in range(chunks):
            slot = c * z_count + lax.rem(z - step * hop + 2 * z_count, z_count)
            arrive(slot, k)
            if hop < fwd_hops:
                send(out_ref.at[slot], slot, k, fwd_id)
            send(out_ref.at[slot], slot, k, pair_id)
            if hop <= bwd_hops:
                slot = c * z_count + lax.rem(z + step * hop + 2 * z_count, z_count)
                arrive(slot, k)
                if hop < bwd_hops:
                    send(out_ref.at[slot], slot, k, bwd_id)
                send(out_ref.at[slot], slot, k, pair_id)
    for zz in range(z_count):
        for k in range(chunks):
            arrive(other * z_count + zz, k)
    local.wait()
    for copy in sends:
        copy.wait_send()


def gather_blocks(block, z_count, chunks):
    count = 2 * z_count
    return pl.pallas_call(
        functools.partial(dispatch_kernel, z_count, chunks),
        out_shape=jax.ShapeDtypeStruct((count,) + block.shape, block.dtype),
        in_specs=[pl.BlockSpec(memory_space=pl.ANY)],
        out_specs=pl.BlockSpec(memory_space=pl.ANY),
        scratch_shapes=[
            pltpu.SemaphoreType.DMA((2 * count * chunks,)),
            pltpu.SemaphoreType.DMA((count * chunks,)),
            pltpu.SemaphoreType.DMA((1,)),
        ],
        compiler_params=pltpu.CompilerParams(collective_id=0, has_side_effects=True),
    )(block)


def combine_kernel(
    z_count, dp_count, seq_len, chunks, part_ref, head_ref, out_ref, pair_out, pair_buf,
    own_buf, fwd_buf, bwd_buf, fwd_out, bwd_out, seq_out, seq_in, send_sem, recv_sem, seq_sem,
    own_sem,
):
    z = lax.axis_index("z")
    c = lax.axis_index("c")
    row = lax.axis_index("dp")
    other = 1 - c
    step = 1 - 2 * c
    fwd = lax.rem(z + step + z_count, z_count)
    bwd = lax.rem(z - step + z_count, z_count)
    fwd_id, bwd_id, pair_id = (row, fwd, c), (row, bwd, c), (row, z, other)
    mate_id = (lax.rem(row + dp_count // 2, dp_count), z, c)
    fwd_hops = z_count // 2
    bwd_hops = z_count - 1 - fwd_hops
    piece = part_ref.shape[2] // chunks

    barrier = pltpu.get_barrier_semaphore()
    for target in (fwd_id, bwd_id, pair_id, mate_id):
        pl.semaphore_signal(barrier, 1, device_id=target, device_id_type=MESH)
    pl.semaphore_wait(barrier, 4)

    sends = []

    def send(src, dst, sem, target):
        copy = pltpu.make_async_remote_copy(
            src_ref=src,
            dst_ref=dst,
            send_sem=send_sem.at[len(sends)],
            recv_sem=recv_sem.at[sem],
            device_id=target,
            device_id_type=MESH,
        )
        copy.start()
        sends.append(copy)

    def arrive(dst, sem):
        pltpu.make_async_remote_copy(
            src_ref=dst,
            dst_ref=dst,
            send_sem=send_sem.at[0],
            recv_sem=recv_sem.at[sem],
            device_id=pair_id,
            device_id_type=MESH,
        ).wait_recv()

    def order(ring_step):
        dests = []
        for hop in range(1, fwd_hops + 1):
            dests.append(lax.rem(z + ring_step * (fwd_hops + 1 - hop) + 2 * z_count, z_count))
            if hop <= bwd_hops:
                dests.append(lax.rem(z - ring_step * (bwd_hops + 1 - hop) + 2 * z_count, z_count))
        return dests + [z]

    for n, dest in enumerate(order(-step)):
        send(part_ref.at[other, dest], pair_buf.at[n], n, pair_id)
    loads = []
    for n, dest in enumerate(order(step)):
        load = pltpu.make_async_copy(part_ref.at[c, dest], own_buf.at[n], own_sem.at[n])
        load.start()
        loads.append(load)

    def own(dest, n, k):
        if k == 0:
            loads[n].wait()
            arrive(pair_buf.at[n], n)
        rows = pl.ds(k * piece, piece)
        return own_buf[n, rows].astype(jnp.float32) + pair_buf[n, rows].astype(jnp.float32)

    fwd_sem = z_count
    bwd_sem = z_count + fwd_hops * chunks
    for hop in range(1, fwd_hops + 1):
        for k in range(chunks):
            rows = pl.ds(k * piece, piece)
            dest = lax.rem(z + step * (fwd_hops + 1 - hop) + 2 * z_count, z_count)
            n = hop - 1 + min(hop - 1, bwd_hops)
            total = own(dest, n, k)
            if hop > 1:
                sem = fwd_sem + (hop - 2) * chunks + k
                arrive(fwd_buf.at[hop - 2, rows], sem)
                total = total + fwd_buf[hop - 2, rows].astype(jnp.float32)
            fwd_out[hop - 1, rows] = total.astype(fwd_out.dtype)
            sem = fwd_sem + (hop - 1) * chunks + k
            send(fwd_out.at[hop - 1, rows], fwd_buf.at[hop - 1, rows], sem, fwd_id)
            if hop <= bwd_hops:
                dest = lax.rem(z - step * (bwd_hops + 1 - hop) + 2 * z_count, z_count)
                total = own(dest, n + 1, k)
                if hop > 1:
                    sem = bwd_sem + (hop - 2) * chunks + k
                    arrive(bwd_buf.at[hop - 2, rows], sem)
                    total = total + bwd_buf[hop - 2, rows].astype(jnp.float32)
                bwd_out[hop - 1, rows] = total.astype(bwd_out.dtype)
                sem = bwd_sem + (hop - 1) * chunks + k
                send(bwd_out.at[hop - 1, rows], bwd_buf.at[hop - 1, rows], sem, bwd_id)
    for k in range(chunks):
        rows = pl.ds(k * piece, piece)
        total = own(z, fwd_hops + bwd_hops, k)
        arrive(fwd_buf.at[fwd_hops - 1, rows], fwd_sem + (fwd_hops - 1) * chunks + k)
        total = total + fwd_buf[fwd_hops - 1, rows].astype(jnp.float32)
        if bwd_hops > 0:
            arrive(bwd_buf.at[bwd_hops - 1, rows], bwd_sem + (bwd_hops - 1) * chunks + k)
            total = total + bwd_buf[bwd_hops - 1, rows].astype(jnp.float32)
        out_ref[rows] = total.astype(out_ref.dtype)
    tok_rows, width = out_ref.shape
    seqs = tok_rows // seq_len
    scored = out_ref[...].astype(jnp.float32) * head_ref[...]
    per_seq = jnp.sum(scored.reshape(seqs, seq_len, width), axis=1)
    seq_score = jnp.sum(per_seq, axis=1, keepdims=True)
    seq_out[...] = jnp.zeros(seq_out.shape, jnp.float32)
    seq_out[pl.ds(0, seqs)] = jnp.broadcast_to(seq_score, (seqs, seq_out.shape[1]))
    mate = pltpu.make_async_remote_copy(
        src_ref=seq_out,
        dst_ref=seq_in,
        send_sem=seq_sem.at[0],
        recv_sem=seq_sem.at[1],
        device_id=mate_id,
        device_id_type=MESH,
    )
    mate.start()
    mate.wait()
    mine = seq_out[...]
    theirs = seq_in[...]
    pair_out[...] = jnp.abs(mine - theirs) + 0.5 * (mine + theirs)
    for copy in sends:
        copy.wait_send()


def scatter_sums(partial, score_head, dp_count, seq_len, chunks):
    c_count, z_count, rows, width = partial.shape
    fwd_hops = z_count // 2
    bwd_hops = max(z_count - 1 - fwd_hops, 1)
    block = (rows, width)
    vmem = pl.BlockSpec(memory_space=pltpu.VMEM)
    sems = z_count + (fwd_hops + bwd_hops) * chunks
    tile = (8, 128)
    return pl.pallas_call(
        functools.partial(combine_kernel, z_count, dp_count, seq_len, chunks),
        out_shape=(
            jax.ShapeDtypeStruct(block, partial.dtype),
            jax.ShapeDtypeStruct(tile, jnp.float32),
        ),
        in_specs=[pl.BlockSpec(memory_space=pl.ANY), vmem],
        out_specs=(vmem, vmem),
        scratch_shapes=[
            pltpu.VMEM((z_count,) + block, partial.dtype),
            pltpu.VMEM((z_count,) + block, partial.dtype),
            pltpu.VMEM((fwd_hops,) + block, partial.dtype),
            pltpu.VMEM((bwd_hops,) + block, partial.dtype),
            pltpu.VMEM((fwd_hops,) + block, partial.dtype),
            pltpu.VMEM((bwd_hops,) + block, partial.dtype),
            pltpu.VMEM(tile, jnp.float32),
            pltpu.VMEM(tile, jnp.float32),
            pltpu.SemaphoreType.DMA((sems,)),
            pltpu.SemaphoreType.DMA((sems,)),
            pltpu.SemaphoreType.DMA((2,)),
            pltpu.SemaphoreType.DMA((z_count,)),
        ],
        compiler_params=pltpu.CompilerParams(
            collective_id=1, has_side_effects=True, vmem_limit_bytes=48 * 1024 * 1024
        ),
    )(partial, score_head.reshape(1, -1))


def body(
    tokens, expert_ids, gate_fixed, scorer_id, direction_tags, w_gate, w_up, w_down, score_head
):
    z_count = lax.axis_size("z")
    c_count = lax.axis_size("c")
    expert_count = z_count * c_count
    per_device = w_gate.shape[0]
    tok_rows, model_width = tokens.shape
    top_count = expert_ids.shape[1]
    which_tag = jnp.repeat(scorer_id, SEQ_LEN)[:, None]
    tag_rows = jnp.where(
        which_tag == 1, direction_tags[1][None, :], direction_tags[0][None, :]
    ).astype(jnp.float32)
    inputs = (tokens.astype(jnp.float32) + tag_rows).astype(jnp.bfloat16)
    rank_in = route_ranks(expert_ids, per_device * expert_count)
    routes = jnp.concatenate(
        [expert_ids, rank_in, gate_fixed // 256, gate_fixed % 256], axis=1
    ).astype(jnp.bfloat16)
    routes = jnp.pad(routes, ((0, 0), (0, 128 - 4 * top_count)))
    block = jnp.concatenate([inputs, routes], axis=1)
    gathered = gather_blocks(block, z_count, 2)
    inputs_all = gathered[:, :, :model_width]
    routes_all = gathered[:, :, model_width : model_width + 4 * top_count].astype(jnp.int32)
    ids_cube = routes_all[..., :top_count]
    rank_cube = routes_all[..., top_count : 2 * top_count]
    fixed_val = (
        routes_all[..., 2 * top_count : 3 * top_count] * 256 + routes_all[..., 3 * top_count :]
    ).astype(jnp.float32)
    weight_cube = fixed_val / jnp.sum(fixed_val, axis=2, keepdims=True)
    my_index = lax.axis_index("z") * c_count + lax.axis_index("c")
    local_count = per_device * MOST
    local_slot = ids_cube - my_index * per_device
    is_mine = (local_slot >= 0) & (local_slot < per_device)
    local_key = jnp.where(is_mine, local_slot * MOST + rank_cube, -1)
    match = (
        local_key[:, None, :, :] == jnp.arange(local_count, dtype=jnp.int32)[None, :, None, None]
    )
    picker = jnp.any(match, axis=3).astype(jnp.bfloat16)
    slot_weight = jnp.sum(jnp.where(match, weight_cube[:, None, :, :], 0.0), axis=(2, 3))
    picker = picker.reshape(expert_count, per_device, MOST, tok_rows).transpose(1, 0, 2, 3)
    slot_weight = slot_weight.reshape(expert_count, per_device, MOST).transpose(1, 0, 2)
    row_block = jnp.einsum(
        "esmt,std->esmd", picker, inputs_all, preferred_element_type=jnp.float32
    ).astype(jnp.bfloat16)
    gate_proj = jnp.einsum("esmd,edf->esmf", row_block, w_gate, preferred_element_type=jnp.float32)
    up_proj = jnp.einsum("esmd,edf->esmf", row_block, w_up, preferred_element_type=jnp.float32)
    hidden = (jax.nn.silu(gate_proj) * up_proj).astype(jnp.bfloat16)
    down_out = jnp.einsum("esmf,efd->esmd", hidden, w_down, preferred_element_type=jnp.float32)
    result = (slot_weight[..., None] * down_out).astype(jnp.bfloat16)
    partial_value = jnp.einsum(
        "esmt,esmd->std", picker, result, preferred_element_type=jnp.float32
    )
    partial_value = partial_value.reshape(c_count, z_count, tok_rows, model_width)
    mixed, pair_tile = scatter_sums(
        partial_value.astype(jnp.bfloat16), score_head, lax.axis_size("dp"), SEQ_LEN, 2
    )
    pair_score = pair_tile[: tok_rows // SEQ_LEN, 0]
    return (mixed, pair_score)


def solution(mesh):
    dp_count, expert_count = mesh.devices.shape
    split = Mesh(mesh.devices.reshape(dp_count, expert_count // 2, 2), ("dp", "z", "c"))
    rows = P(("dp", "z", "c"), None)
    return jax.shard_map(
        body,
        mesh=split,
        in_specs=(
            rows,
            rows,
            rows,
            P(("dp", "z", "c")),
            P(),
            P(("z", "c"), None, None),
            P(("z", "c"), None, None),
            P(("z", "c"), None, None),
            P(),
        ),
        out_specs=(rows, P(("dp", "z", "c"))),
        check_vma=False,
    )
```

```python
import functools

import jax
import jax.numpy as jnp
from jax import lax
from jax.experimental import pallas as pl
from jax.experimental.pallas import tpu as pltpu
from jax.sharding import Mesh
from jax.sharding import PartitionSpec as P

SEQ_LEN = 16
MOST = 24


def from_partner(block, axis, bit):
    count = lax.axis_size(axis)
    route = []
    for low in range(count):
        high = low | 1 << bit
        if high != low and high < count:
            route += [(low, high), (high, low)]
    return lax.ppermute(block, axis, route)


def route_ranks(expert_ids, expert_total):
    flat_ids = expert_ids.reshape(-1)
    entry_count = flat_ids.shape[0]
    onehot = flat_ids[:, None] == jnp.arange(expert_total, dtype=jnp.int32)[None, :]
    positions = jnp.arange(entry_count, dtype=jnp.int32)
    earlier = (positions[:, None] > positions[None, :]).astype(jnp.bfloat16)
    counts = jnp.dot(earlier, onehot.astype(jnp.bfloat16), preferred_element_type=jnp.float32)
    rank_in = jnp.sum(jnp.where(onehot, counts, 0.0), axis=1).astype(jnp.int32)
    return rank_in.reshape(expert_ids.shape)


MESH = pl.DeviceIdType.MESH


def dispatch_kernel(z_count, chunks, blk_ref, out_ref, send_sem, recv_sem, local_sem):
    z = lax.axis_index("z")
    c = lax.axis_index("c")
    row = lax.axis_index("dp")
    other = 1 - c
    step = 1 - 2 * c
    fwd = lax.rem(z + step + z_count, z_count)
    bwd = lax.rem(z - step + z_count, z_count)
    fwd_id, bwd_id, pair_id = (row, fwd, c), (row, bwd, c), (row, z, other)
    piece = blk_ref.shape[0] // chunks

    barrier = pltpu.get_barrier_semaphore()
    for target in (fwd_id, bwd_id, pair_id):
        pl.semaphore_signal(barrier, 1, device_id=target, device_id_type=MESH)
    pl.semaphore_wait(barrier, 3)

    mine = c * z_count + z
    local = pltpu.make_async_copy(blk_ref, out_ref.at[mine], local_sem.at[0])
    local.start()
    sends = []

    def part(ref, k):
        return ref.at[pl.ds(k * piece, piece)]

    def send(src, slot, k, target):
        copy = pltpu.make_async_remote_copy(
            src_ref=part(src, k),
            dst_ref=part(out_ref.at[slot], k),
            send_sem=send_sem.at[len(sends)],
            recv_sem=recv_sem.at[slot * chunks + k],
            device_id=target,
            device_id_type=MESH,
        )
        copy.start()
        sends.append(copy)

    def arrive(slot, k):
        view = part(out_ref.at[slot], k)
        pltpu.make_async_remote_copy(
            src_ref=view,
            dst_ref=view,
            send_sem=send_sem.at[0],
            recv_sem=recv_sem.at[slot * chunks + k],
            device_id=pair_id,
            device_id_type=MESH,
        ).wait_recv()

    for k in range(chunks):
        send(blk_ref, mine, k, fwd_id)
        send(blk_ref, mine, k, bwd_id)
    for k in range(chunks):
        send(blk_ref, mine, k, pair_id)
    fwd_hops = z_count // 2
    bwd_hops = z_count - 1 - fwd_hops
    for hop in range(1, fwd_hops + 1):
        for k in range(chunks):
            slot = c * z_count + lax.rem(z - step * hop + 2 * z_count, z_count)
            arrive(slot, k)
            if hop < fwd_hops:
                send(out_ref.at[slot], slot, k, fwd_id)
            send(out_ref.at[slot], slot, k, pair_id)
            if hop <= bwd_hops:
                slot = c * z_count + lax.rem(z + step * hop + 2 * z_count, z_count)
                arrive(slot, k)
                if hop < bwd_hops:
                    send(out_ref.at[slot], slot, k, bwd_id)
                send(out_ref.at[slot], slot, k, pair_id)
    for zz in range(z_count):
        for k in range(chunks):
            arrive(other * z_count + zz, k)
    local.wait()
    for copy in sends:
        copy.wait_send()


def gather_blocks(block, z_count, chunks):
    count = 2 * z_count
    return pl.pallas_call(
        functools.partial(dispatch_kernel, z_count, chunks),
        out_shape=jax.ShapeDtypeStruct((count,) + block.shape, block.dtype),
        in_specs=[pl.BlockSpec(memory_space=pltpu.VMEM)],
        out_specs=pl.BlockSpec(memory_space=pltpu.VMEM),
        scratch_shapes=[
            pltpu.SemaphoreType.DMA((2 * count * chunks,)),
            pltpu.SemaphoreType.DMA((count * chunks,)),
            pltpu.SemaphoreType.DMA((1,)),
        ],
        compiler_params=pltpu.CompilerParams(
            collective_id=0, has_side_effects=True, vmem_limit_bytes=32 * 1024 * 1024
        ),
    )(block)


def combine_kernel(
    z_count, dp_count, seq_len, chunks, part_ref, head_ref, out_ref, pair_out, pair_buf,
    fwd_buf, bwd_buf, fwd_out, bwd_out, seq_out, seq_in, send_sem, recv_sem, seq_sem,
):
    z = lax.axis_index("z")
    c = lax.axis_index("c")
    row = lax.axis_index("dp")
    other = 1 - c
    step = 1 - 2 * c
    fwd = lax.rem(z + step + z_count, z_count)
    bwd = lax.rem(z - step + z_count, z_count)
    fwd_id, bwd_id, pair_id = (row, fwd, c), (row, bwd, c), (row, z, other)
    mate_id = (lax.rem(row + dp_count // 2, dp_count), z, c)
    fwd_hops = z_count // 2
    bwd_hops = z_count - 1 - fwd_hops
    piece = part_ref.shape[2] // chunks

    barrier = pltpu.get_barrier_semaphore()
    for target in (fwd_id, bwd_id, pair_id, mate_id):
        pl.semaphore_signal(barrier, 1, device_id=target, device_id_type=MESH)
    pl.semaphore_wait(barrier, 4)

    sends = []

    def send(src, dst, sem, target):
        copy = pltpu.make_async_remote_copy(
            src_ref=src,
            dst_ref=dst,
            send_sem=send_sem.at[len(sends)],
            recv_sem=recv_sem.at[sem],
            device_id=target,
            device_id_type=MESH,
        )
        copy.start()
        sends.append(copy)

    def arrive(dst, sem):
        pltpu.make_async_remote_copy(
            src_ref=dst,
            dst_ref=dst,
            send_sem=send_sem.at[0],
            recv_sem=recv_sem.at[sem],
            device_id=pair_id,
            device_id_type=MESH,
        ).wait_recv()

    def order(ring_step):
        dests = []
        for hop in range(1, fwd_hops + 1):
            dests.append(lax.rem(z + ring_step * (fwd_hops + 1 - hop) + 2 * z_count, z_count))
            if hop <= bwd_hops:
                dests.append(lax.rem(z - ring_step * (bwd_hops + 1 - hop) + 2 * z_count, z_count))
        return dests + [z]

    for n, dest in enumerate(order(-step)):
        send(part_ref.at[other, dest], pair_buf.at[n], n, pair_id)
    def own(dest, n, k):
        if k == 0:
            arrive(pair_buf.at[n], n)
        rows = pl.ds(k * piece, piece)
        return part_ref[c, dest, rows].astype(jnp.float32) + pair_buf[n, rows].astype(
            jnp.float32
        )

    fwd_sem = z_count
    bwd_sem = z_count + fwd_hops * chunks
    for hop in range(1, fwd_hops + 1):
        for k in range(chunks):
            rows = pl.ds(k * piece, piece)
            dest = lax.rem(z + step * (fwd_hops + 1 - hop) + 2 * z_count, z_count)
            n = hop - 1 + min(hop - 1, bwd_hops)
            total = own(dest, n, k)
            if hop > 1:
                sem = fwd_sem + (hop - 2) * chunks + k
                arrive(fwd_buf.at[hop - 2, rows], sem)
                total = total + fwd_buf[hop - 2, rows].astype(jnp.float32)
            fwd_out[hop - 1, rows] = total.astype(fwd_out.dtype)
            sem = fwd_sem + (hop - 1) * chunks + k
            send(fwd_out.at[hop - 1, rows], fwd_buf.at[hop - 1, rows], sem, fwd_id)
            if hop <= bwd_hops:
                dest = lax.rem(z - step * (bwd_hops + 1 - hop) + 2 * z_count, z_count)
                total = own(dest, n + 1, k)
                if hop > 1:
                    sem = bwd_sem + (hop - 2) * chunks + k
                    arrive(bwd_buf.at[hop - 2, rows], sem)
                    total = total + bwd_buf[hop - 2, rows].astype(jnp.float32)
                bwd_out[hop - 1, rows] = total.astype(bwd_out.dtype)
                sem = bwd_sem + (hop - 1) * chunks + k
                send(bwd_out.at[hop - 1, rows], bwd_buf.at[hop - 1, rows], sem, bwd_id)
    for k in range(chunks):
        rows = pl.ds(k * piece, piece)
        total = own(z, fwd_hops + bwd_hops, k)
        arrive(fwd_buf.at[fwd_hops - 1, rows], fwd_sem + (fwd_hops - 1) * chunks + k)
        total = total + fwd_buf[fwd_hops - 1, rows].astype(jnp.float32)
        if bwd_hops > 0:
            arrive(bwd_buf.at[bwd_hops - 1, rows], bwd_sem + (bwd_hops - 1) * chunks + k)
            total = total + bwd_buf[bwd_hops - 1, rows].astype(jnp.float32)
        out_ref[rows] = total.astype(out_ref.dtype)
    tok_rows, width = out_ref.shape
    seqs = tok_rows // seq_len
    scored = out_ref[...].astype(jnp.float32) * head_ref[...]
    per_seq = jnp.sum(scored.reshape(seqs, seq_len, width), axis=1)
    seq_score = jnp.sum(per_seq, axis=1, keepdims=True)
    seq_out[...] = jnp.zeros(seq_out.shape, jnp.float32)
    seq_out[pl.ds(0, seqs)] = jnp.broadcast_to(seq_score, (seqs, seq_out.shape[1]))
    mate = pltpu.make_async_remote_copy(
        src_ref=seq_out,
        dst_ref=seq_in,
        send_sem=seq_sem.at[0],
        recv_sem=seq_sem.at[1],
        device_id=mate_id,
        device_id_type=MESH,
    )
    mate.start()
    mate.wait()
    mine = seq_out[...]
    theirs = seq_in[...]
    pair_out[...] = jnp.abs(mine - theirs) + 0.5 * (mine + theirs)
    for copy in sends:
        copy.wait_send()


def scatter_sums(partial, score_head, dp_count, seq_len, chunks):
    c_count, z_count, rows, width = partial.shape
    fwd_hops = z_count // 2
    bwd_hops = max(z_count - 1 - fwd_hops, 1)
    block = (rows, width)
    vmem = pl.BlockSpec(memory_space=pltpu.VMEM)
    sems = z_count + (fwd_hops + bwd_hops) * chunks
    tile = (8, 128)
    return pl.pallas_call(
        functools.partial(combine_kernel, z_count, dp_count, seq_len, chunks),
        out_shape=(
            jax.ShapeDtypeStruct(block, partial.dtype),
            jax.ShapeDtypeStruct(tile, jnp.float32),
        ),
        in_specs=[vmem, vmem],
        out_specs=(vmem, vmem),
        scratch_shapes=[
            pltpu.VMEM((z_count,) + block, partial.dtype),
            pltpu.VMEM((fwd_hops,) + block, partial.dtype),
            pltpu.VMEM((bwd_hops,) + block, partial.dtype),
            pltpu.VMEM((fwd_hops,) + block, partial.dtype),
            pltpu.VMEM((bwd_hops,) + block, partial.dtype),
            pltpu.VMEM(tile, jnp.float32),
            pltpu.VMEM(tile, jnp.float32),
            pltpu.SemaphoreType.DMA((sems,)),
            pltpu.SemaphoreType.DMA((sems,)),
            pltpu.SemaphoreType.DMA((2,)),
        ],
        compiler_params=pltpu.CompilerParams(
            collective_id=1, has_side_effects=True, vmem_limit_bytes=48 * 1024 * 1024
        ),
    )(partial, score_head.reshape(1, -1))


def body(
    tokens, expert_ids, gate_fixed, scorer_id, direction_tags, w_gate, w_up, w_down, score_head
):
    z_count = lax.axis_size("z")
    c_count = lax.axis_size("c")
    expert_count = z_count * c_count
    per_device = w_gate.shape[0]
    tok_rows, model_width = tokens.shape
    top_count = expert_ids.shape[1]
    which_tag = jnp.repeat(scorer_id, SEQ_LEN)[:, None]
    tag_rows = jnp.where(
        which_tag == 1, direction_tags[1][None, :], direction_tags[0][None, :]
    ).astype(jnp.float32)
    inputs = (tokens.astype(jnp.float32) + tag_rows).astype(jnp.bfloat16)
    rank_in = route_ranks(expert_ids, per_device * expert_count)
    routes = jnp.concatenate(
        [expert_ids, rank_in, gate_fixed // 256, gate_fixed % 256], axis=1
    ).astype(jnp.bfloat16)
    routes = jnp.pad(routes, ((0, 0), (0, 128 - 4 * top_count)))
    block = jnp.concatenate([inputs, routes], axis=1)
    gathered = gather_blocks(block, z_count, 2)
    inputs_all = gathered[:, :, :model_width]
    routes_all = gathered[:, :, model_width : model_width + 4 * top_count].astype(jnp.int32)
    ids_cube = routes_all[..., :top_count]
    rank_cube = routes_all[..., top_count : 2 * top_count]
    fixed_val = (
        routes_all[..., 2 * top_count : 3 * top_count] * 256 + routes_all[..., 3 * top_count :]
    ).astype(jnp.float32)
    weight_cube = fixed_val / jnp.sum(fixed_val, axis=2, keepdims=True)
    my_index = lax.axis_index("z") * c_count + lax.axis_index("c")
    local_count = per_device * MOST
    local_slot = ids_cube - my_index * per_device
    is_mine = (local_slot >= 0) & (local_slot < per_device)
    local_key = jnp.where(is_mine, local_slot * MOST + rank_cube, -1)
    match = (
        local_key[:, None, :, :] == jnp.arange(local_count, dtype=jnp.int32)[None, :, None, None]
    )
    picker = jnp.any(match, axis=3).astype(jnp.bfloat16)
    slot_weight = jnp.sum(jnp.where(match, weight_cube[:, None, :, :], 0.0), axis=(2, 3))
    picker = picker.reshape(expert_count, per_device, MOST, tok_rows).transpose(1, 0, 2, 3)
    slot_weight = slot_weight.reshape(expert_count, per_device, MOST).transpose(1, 0, 2)
    row_block = jnp.einsum(
        "esmt,std->esmd", picker, inputs_all, preferred_element_type=jnp.float32
    ).astype(jnp.bfloat16)
    gate_proj = jnp.einsum("esmd,edf->esmf", row_block, w_gate, preferred_element_type=jnp.float32)
    up_proj = jnp.einsum("esmd,edf->esmf", row_block, w_up, preferred_element_type=jnp.float32)
    hidden = (jax.nn.silu(gate_proj) * up_proj).astype(jnp.bfloat16)
    down_out = jnp.einsum("esmf,efd->esmd", hidden, w_down, preferred_element_type=jnp.float32)
    result = (slot_weight[..., None] * down_out).astype(jnp.bfloat16)
    result = lax.optimization_barrier(result)
    partial_value = jnp.einsum(
        "esmt,esmd->std", picker, result, preferred_element_type=jnp.float32
    )
    partial_value = partial_value.reshape(c_count, z_count, tok_rows, model_width)
    mixed, pair_tile = scatter_sums(
        partial_value.astype(jnp.bfloat16), score_head, lax.axis_size("dp"), SEQ_LEN, 2
    )
    pair_score = pair_tile[: tok_rows // SEQ_LEN, 0]
    return (mixed, pair_score)


def solution(mesh):
    dp_count, expert_count = mesh.devices.shape
    split = Mesh(mesh.devices.reshape(dp_count, expert_count // 2, 2), ("dp", "z", "c"))
    rows = P(("dp", "z", "c"), None)
    return jax.shard_map(
        body,
        mesh=split,
        in_specs=(
            rows,
            rows,
            rows,
            P(("dp", "z", "c")),
            P(),
            P(("z", "c"), None, None),
            P(("z", "c"), None, None),
            P(("z", "c"), None, None),
            P(),
        ),
        out_specs=(rows, P(("dp", "z", "c"))),
        check_vma=False,
    )
```

```python
import functools

import jax
import jax.numpy as jnp
from jax import lax
from jax.experimental import pallas as pl
from jax.experimental.pallas import tpu as pltpu
from jax.sharding import Mesh
from jax.sharding import PartitionSpec as P

SEQ_LEN = 16
MOST = 24


def from_partner(block, axis, bit):
    count = lax.axis_size(axis)
    route = []
    for low in range(count):
        high = low | 1 << bit
        if high != low and high < count:
            route += [(low, high), (high, low)]
    return lax.ppermute(block, axis, route)


def route_ranks(expert_ids, expert_total):
    flat_ids = expert_ids.reshape(-1)
    entry_count = flat_ids.shape[0]
    onehot = flat_ids[:, None] == jnp.arange(expert_total, dtype=jnp.int32)[None, :]
    positions = jnp.arange(entry_count, dtype=jnp.int32)
    earlier = (positions[:, None] > positions[None, :]).astype(jnp.bfloat16)
    counts = jnp.dot(earlier, onehot.astype(jnp.bfloat16), preferred_element_type=jnp.float32)
    rank_in = jnp.sum(jnp.where(onehot, counts, 0.0), axis=1).astype(jnp.int32)
    return rank_in.reshape(expert_ids.shape)


MESH = pl.DeviceIdType.MESH


def dispatch_kernel(z_count, chunks, blk_ref, out_ref, send_sem, recv_sem, local_sem):
    z = lax.axis_index("z")
    c = lax.axis_index("c")
    row = lax.axis_index("dp")
    other = 1 - c
    step = 1 - 2 * c
    fwd = lax.rem(z + step + z_count, z_count)
    bwd = lax.rem(z - step + z_count, z_count)
    fwd_id, bwd_id, pair_id = (row, fwd, c), (row, bwd, c), (row, z, other)
    piece = blk_ref.shape[0] // chunks

    barrier = pltpu.get_barrier_semaphore()
    for target in (fwd_id, bwd_id, pair_id):
        pl.semaphore_signal(barrier, 1, device_id=target, device_id_type=MESH)
    pl.semaphore_wait(barrier, 3)

    mine = c * z_count + z
    local = pltpu.make_async_copy(blk_ref, out_ref.at[mine], local_sem.at[0])
    local.start()
    sends = []

    def part(ref, k):
        return ref.at[pl.ds(k * piece, piece)]

    def send(src, slot, k, target):
        copy = pltpu.make_async_remote_copy(
            src_ref=part(src, k),
            dst_ref=part(out_ref.at[slot], k),
            send_sem=send_sem.at[len(sends)],
            recv_sem=recv_sem.at[slot * chunks + k],
            device_id=target,
            device_id_type=MESH,
        )
        copy.start()
        sends.append(copy)

    def arrive(slot, k):
        view = part(out_ref.at[slot], k)
        pltpu.make_async_remote_copy(
            src_ref=view,
            dst_ref=view,
            send_sem=send_sem.at[0],
            recv_sem=recv_sem.at[slot * chunks + k],
            device_id=pair_id,
            device_id_type=MESH,
        ).wait_recv()

    for k in range(chunks):
        send(blk_ref, mine, k, fwd_id)
        send(blk_ref, mine, k, bwd_id)
    for k in range(chunks):
        send(blk_ref, mine, k, pair_id)
    fwd_hops = z_count // 2
    bwd_hops = z_count - 1 - fwd_hops
    for hop in range(1, fwd_hops + 1):
        for k in range(chunks):
            slot = c * z_count + lax.rem(z - step * hop + 2 * z_count, z_count)
            arrive(slot, k)
            if hop < fwd_hops:
                send(out_ref.at[slot], slot, k, fwd_id)
            send(out_ref.at[slot], slot, k, pair_id)
            if hop <= bwd_hops:
                slot = c * z_count + lax.rem(z + step * hop + 2 * z_count, z_count)
                arrive(slot, k)
                if hop < bwd_hops:
                    send(out_ref.at[slot], slot, k, bwd_id)
                send(out_ref.at[slot], slot, k, pair_id)
    for zz in range(z_count):
        for k in range(chunks):
            arrive(other * z_count + zz, k)
    local.wait()
    for copy in sends:
        copy.wait_send()


def gather_blocks(block, z_count, chunks):
    count = 2 * z_count
    return pl.pallas_call(
        functools.partial(dispatch_kernel, z_count, chunks),
        out_shape=jax.ShapeDtypeStruct((count,) + block.shape, block.dtype),
        in_specs=[pl.BlockSpec(memory_space=pl.ANY)],
        out_specs=pl.BlockSpec(memory_space=pl.ANY),
        scratch_shapes=[
            pltpu.SemaphoreType.DMA((2 * count * chunks,)),
            pltpu.SemaphoreType.DMA((count * chunks,)),
            pltpu.SemaphoreType.DMA((1,)),
        ],
        compiler_params=pltpu.CompilerParams(collective_id=0, has_side_effects=True),
    )(block)


def combine_kernel(
    z_count, dp_count, seq_len, chunks, part_ref, head_ref, out_ref, pair_out, pair_buf,
    fwd_buf, bwd_buf, fwd_out, bwd_out, seq_out, seq_in, send_sem, recv_sem, seq_sem,
):
    z = lax.axis_index("z")
    c = lax.axis_index("c")
    row = lax.axis_index("dp")
    other = 1 - c
    step = 1 - 2 * c
    fwd = lax.rem(z + step + z_count, z_count)
    bwd = lax.rem(z - step + z_count, z_count)
    fwd_id, bwd_id, pair_id = (row, fwd, c), (row, bwd, c), (row, z, other)
    mate_id = (lax.rem(row + dp_count // 2, dp_count), z, c)
    fwd_hops = z_count // 2
    bwd_hops = z_count - 1 - fwd_hops
    piece = part_ref.shape[2] // chunks

    barrier = pltpu.get_barrier_semaphore()
    for target in (fwd_id, bwd_id, pair_id, mate_id):
        pl.semaphore_signal(barrier, 1, device_id=target, device_id_type=MESH)
    pl.semaphore_wait(barrier, 4)

    sends = []

    def send(src, dst, sem, target):
        copy = pltpu.make_async_remote_copy(
            src_ref=src,
            dst_ref=dst,
            send_sem=send_sem.at[len(sends)],
            recv_sem=recv_sem.at[sem],
            device_id=target,
            device_id_type=MESH,
        )
        copy.start()
        sends.append(copy)

    def arrive(dst, sem):
        pltpu.make_async_remote_copy(
            src_ref=dst,
            dst_ref=dst,
            send_sem=send_sem.at[0],
            recv_sem=recv_sem.at[sem],
            device_id=pair_id,
            device_id_type=MESH,
        ).wait_recv()

    def order(ring_step):
        dests = []
        for hop in range(1, fwd_hops + 1):
            dests.append(lax.rem(z + ring_step * (fwd_hops + 1 - hop) + 2 * z_count, z_count))
            if hop <= bwd_hops:
                dests.append(lax.rem(z - ring_step * (bwd_hops + 1 - hop) + 2 * z_count, z_count))
        return dests + [z]

    for n, dest in enumerate(order(-step)):
        send(part_ref.at[other, dest], pair_buf.at[n], n, pair_id)
    def own(dest, n, k):
        if k == 0:
            arrive(pair_buf.at[n], n)
        rows = pl.ds(k * piece, piece)
        return part_ref[c, dest, rows].astype(jnp.float32) + pair_buf[n, rows].astype(
            jnp.float32
        )

    fwd_sem = z_count
    bwd_sem = z_count + fwd_hops * chunks
    for hop in range(1, fwd_hops + 1):
        for k in range(chunks):
            rows = pl.ds(k * piece, piece)
            dest = lax.rem(z + step * (fwd_hops + 1 - hop) + 2 * z_count, z_count)
            n = hop - 1 + min(hop - 1, bwd_hops)
            total = own(dest, n, k)
            if hop > 1:
                sem = fwd_sem + (hop - 2) * chunks + k
                arrive(fwd_buf.at[hop - 2, rows], sem)
                total = total + fwd_buf[hop - 2, rows].astype(jnp.float32)
            fwd_out[hop - 1, rows] = total.astype(fwd_out.dtype)
            sem = fwd_sem + (hop - 1) * chunks + k
            send(fwd_out.at[hop - 1, rows], fwd_buf.at[hop - 1, rows], sem, fwd_id)
            if hop <= bwd_hops:
                dest = lax.rem(z - step * (bwd_hops + 1 - hop) + 2 * z_count, z_count)
                total = own(dest, n + 1, k)
                if hop > 1:
                    sem = bwd_sem + (hop - 2) * chunks + k
                    arrive(bwd_buf.at[hop - 2, rows], sem)
                    total = total + bwd_buf[hop - 2, rows].astype(jnp.float32)
                bwd_out[hop - 1, rows] = total.astype(bwd_out.dtype)
                sem = bwd_sem + (hop - 1) * chunks + k
                send(bwd_out.at[hop - 1, rows], bwd_buf.at[hop - 1, rows], sem, bwd_id)
    for k in range(chunks):
        rows = pl.ds(k * piece, piece)
        total = own(z, fwd_hops + bwd_hops, k)
        arrive(fwd_buf.at[fwd_hops - 1, rows], fwd_sem + (fwd_hops - 1) * chunks + k)
        total = total + fwd_buf[fwd_hops - 1, rows].astype(jnp.float32)
        if bwd_hops > 0:
            arrive(bwd_buf.at[bwd_hops - 1, rows], bwd_sem + (bwd_hops - 1) * chunks + k)
            total = total + bwd_buf[bwd_hops - 1, rows].astype(jnp.float32)
        out_ref[rows] = total.astype(out_ref.dtype)
    tok_rows, width = out_ref.shape
    seqs = tok_rows // seq_len
    scored = out_ref[...].astype(jnp.float32) * head_ref[...]
    per_seq = jnp.sum(scored.reshape(seqs, seq_len, width), axis=1)
    seq_score = jnp.sum(per_seq, axis=1, keepdims=True)
    seq_out[...] = jnp.zeros(seq_out.shape, jnp.float32)
    seq_out[pl.ds(0, seqs)] = jnp.broadcast_to(seq_score, (seqs, seq_out.shape[1]))
    mate = pltpu.make_async_remote_copy(
        src_ref=seq_out,
        dst_ref=seq_in,
        send_sem=seq_sem.at[0],
        recv_sem=seq_sem.at[1],
        device_id=mate_id,
        device_id_type=MESH,
    )
    mate.start()
    mate.wait()
    mine = seq_out[...]
    theirs = seq_in[...]
    pair_out[...] = jnp.abs(mine - theirs) + 0.5 * (mine + theirs)
    for copy in sends:
        copy.wait_send()


def scatter_sums(partial, score_head, dp_count, seq_len, chunks):
    c_count, z_count, rows, width = partial.shape
    fwd_hops = z_count // 2
    bwd_hops = max(z_count - 1 - fwd_hops, 1)
    block = (rows, width)
    vmem = pl.BlockSpec(memory_space=pltpu.VMEM)
    sems = z_count + (fwd_hops + bwd_hops) * chunks
    tile = (8, 128)
    return pl.pallas_call(
        functools.partial(combine_kernel, z_count, dp_count, seq_len, chunks),
        out_shape=(
            jax.ShapeDtypeStruct(block, partial.dtype),
            jax.ShapeDtypeStruct(tile, jnp.float32),
        ),
        in_specs=[vmem, vmem],
        out_specs=(vmem, vmem),
        scratch_shapes=[
            pltpu.VMEM((z_count,) + block, partial.dtype),
            pltpu.VMEM((fwd_hops,) + block, partial.dtype),
            pltpu.VMEM((bwd_hops,) + block, partial.dtype),
            pltpu.VMEM((fwd_hops,) + block, partial.dtype),
            pltpu.VMEM((bwd_hops,) + block, partial.dtype),
            pltpu.VMEM(tile, jnp.float32),
            pltpu.VMEM(tile, jnp.float32),
            pltpu.SemaphoreType.DMA((sems,)),
            pltpu.SemaphoreType.DMA((sems,)),
            pltpu.SemaphoreType.DMA((2,)),
        ],
        compiler_params=pltpu.CompilerParams(
            collective_id=1, has_side_effects=True, vmem_limit_bytes=48 * 1024 * 1024
        ),
    )(partial, score_head.reshape(1, -1))


def body(
    tokens, expert_ids, gate_fixed, scorer_id, direction_tags, w_gate, w_up, w_down, score_head
):
    z_count = lax.axis_size("z")
    c_count = lax.axis_size("c")
    expert_count = z_count * c_count
    per_device = w_gate.shape[0]
    tok_rows, model_width = tokens.shape
    top_count = expert_ids.shape[1]
    which_tag = jnp.repeat(scorer_id, SEQ_LEN)[:, None]
    tag_rows = jnp.where(
        which_tag == 1, direction_tags[1][None, :], direction_tags[0][None, :]
    ).astype(jnp.float32)
    inputs = (tokens.astype(jnp.float32) + tag_rows).astype(jnp.bfloat16)
    rank_in = route_ranks(expert_ids, per_device * expert_count)
    routes = jnp.concatenate(
        [expert_ids, rank_in, gate_fixed // 256, gate_fixed % 256], axis=1
    ).astype(jnp.bfloat16)
    routes = jnp.pad(routes, ((0, 0), (0, 128 - 4 * top_count)))
    block = jnp.concatenate([inputs, routes], axis=1)
    gathered = gather_blocks(block, z_count, 2)
    inputs_all = gathered[:, :, :model_width]
    routes_all = gathered[:, :, model_width : model_width + 4 * top_count].astype(jnp.int32)
    ids_cube = routes_all[..., :top_count]
    rank_cube = routes_all[..., top_count : 2 * top_count]
    fixed_val = (
        routes_all[..., 2 * top_count : 3 * top_count] * 256 + routes_all[..., 3 * top_count :]
    ).astype(jnp.float32)
    weight_cube = fixed_val / jnp.sum(fixed_val, axis=2, keepdims=True)
    my_index = lax.axis_index("z") * c_count + lax.axis_index("c")
    local_count = per_device * MOST
    local_slot = ids_cube - my_index * per_device
    is_mine = (local_slot >= 0) & (local_slot < per_device)
    local_key = jnp.where(is_mine, local_slot * MOST + rank_cube, -1)
    match = (
        local_key[:, None, :, :] == jnp.arange(local_count, dtype=jnp.int32)[None, :, None, None]
    )
    picker = jnp.any(match, axis=3).astype(jnp.bfloat16)
    slot_weight = jnp.sum(jnp.where(match, weight_cube[:, None, :, :], 0.0), axis=(2, 3))
    picker = picker.reshape(expert_count, per_device, MOST, tok_rows).transpose(1, 0, 2, 3)
    slot_weight = slot_weight.reshape(expert_count, per_device, MOST).transpose(1, 0, 2)
    row_block = jnp.einsum(
        "esmt,std->esmd", picker, inputs_all, preferred_element_type=jnp.float32
    ).astype(jnp.bfloat16)
    gate_proj = jnp.einsum("esmd,edf->esmf", row_block, w_gate, preferred_element_type=jnp.float32)
    up_proj = jnp.einsum("esmd,edf->esmf", row_block, w_up, preferred_element_type=jnp.float32)
    hidden = (jax.nn.silu(gate_proj) * up_proj).astype(jnp.bfloat16)
    down_out = jnp.einsum("esmf,efd->esmd", hidden, w_down, preferred_element_type=jnp.float32)
    result = (slot_weight[..., None] * down_out).astype(jnp.bfloat16)
    result = lax.optimization_barrier(result)
    partial_value = jnp.einsum(
        "esmt,esmd->std", picker, result, preferred_element_type=jnp.float32
    )
    partial_value = partial_value.reshape(c_count, z_count, tok_rows, model_width)
    mixed, pair_tile = scatter_sums(
        partial_value.astype(jnp.bfloat16), score_head, lax.axis_size("dp"), SEQ_LEN, 2
    )
    pair_score = pair_tile[: tok_rows // SEQ_LEN, 0]
    return (mixed, pair_score)


def solution(mesh):
    dp_count, expert_count = mesh.devices.shape
    split = Mesh(mesh.devices.reshape(dp_count, expert_count // 2, 2), ("dp", "z", "c"))
    rows = P(("dp", "z", "c"), None)
    return jax.shard_map(
        body,
        mesh=split,
        in_specs=(
            rows,
            rows,
            rows,
            P(("dp", "z", "c")),
            P(),
            P(("z", "c"), None, None),
            P(("z", "c"), None, None),
            P(("z", "c"), None, None),
            P(),
        ),
        out_specs=(rows, P(("dp", "z", "c"))),
        check_vma=False,
    )
```

```python
import functools

import jax
import jax.numpy as jnp
from jax import lax
from jax.experimental import pallas as pl
from jax.experimental.pallas import tpu as pltpu
from jax.sharding import Mesh
from jax.sharding import PartitionSpec as P

SEQ_LEN = 16
MOST = 24


def from_partner(block, axis, bit):
    count = lax.axis_size(axis)
    route = []
    for low in range(count):
        high = low | 1 << bit
        if high != low and high < count:
            route += [(low, high), (high, low)]
    return lax.ppermute(block, axis, route)


def route_ranks(expert_ids, expert_total):
    flat_ids = expert_ids.reshape(-1)
    entry_count = flat_ids.shape[0]
    onehot = flat_ids[:, None] == jnp.arange(expert_total, dtype=jnp.int32)[None, :]
    positions = jnp.arange(entry_count, dtype=jnp.int32)
    earlier = (positions[:, None] > positions[None, :]).astype(jnp.bfloat16)
    counts = jnp.dot(earlier, onehot.astype(jnp.bfloat16), preferred_element_type=jnp.float32)
    rank_in = jnp.sum(jnp.where(onehot, counts, 0.0), axis=1).astype(jnp.int32)
    return rank_in.reshape(expert_ids.shape)


MESH = pl.DeviceIdType.MESH


def dispatch_kernel(
    z_count, chunks, blk_ref, rt_ref, out_ref, rt_out, send_sem, recv_sem, rt_sem, local_sem
):
    z = lax.axis_index("z")
    c = lax.axis_index("c")
    row = lax.axis_index("dp")
    other = 1 - c
    step = 1 - 2 * c
    fwd = lax.rem(z + step + z_count, z_count)
    bwd = lax.rem(z - step + z_count, z_count)
    fwd_id, bwd_id, pair_id = (row, fwd, c), (row, bwd, c), (row, z, other)
    piece = blk_ref.shape[0] // chunks

    barrier = pltpu.get_barrier_semaphore()
    for target in (fwd_id, bwd_id, pair_id):
        pl.semaphore_signal(barrier, 1, device_id=target, device_id_type=MESH)
    pl.semaphore_wait(barrier, 3)

    mine = c * z_count + z
    local = pltpu.make_async_copy(blk_ref, out_ref.at[mine], local_sem.at[0])
    local.start()
    local_rt = pltpu.make_async_copy(rt_ref, rt_out.at[mine], local_sem.at[1])
    local_rt.start()
    sends = []

    def part(ref, k):
        return ref.at[pl.ds(k * piece, piece)]

    def remote(src, dst, sem, target):
        copy = pltpu.make_async_remote_copy(
            src_ref=src,
            dst_ref=dst,
            send_sem=send_sem.at[len(sends)],
            recv_sem=sem,
            device_id=target,
            device_id_type=MESH,
        )
        copy.start()
        sends.append(copy)

    def send(src, rt_src, slot, k, target):
        remote(part(src, k), part(out_ref.at[slot], k), recv_sem.at[slot * chunks + k], target)
        if k == 0:
            remote(rt_src, rt_out.at[slot], rt_sem.at[slot], target)

    def wait_for(view, sem):
        pltpu.make_async_remote_copy(
            src_ref=view,
            dst_ref=view,
            send_sem=send_sem.at[0],
            recv_sem=sem,
            device_id=pair_id,
            device_id_type=MESH,
        ).wait_recv()

    def arrive(slot, k):
        wait_for(part(out_ref.at[slot], k), recv_sem.at[slot * chunks + k])
        if k == 0:
            wait_for(rt_out.at[slot], rt_sem.at[slot])

    for k in range(chunks):
        send(blk_ref, rt_ref, mine, k, fwd_id)
        send(blk_ref, rt_ref, mine, k, bwd_id)
    for k in range(chunks):
        send(blk_ref, rt_ref, mine, k, pair_id)
    fwd_hops = z_count // 2
    bwd_hops = z_count - 1 - fwd_hops
    for hop in range(1, fwd_hops + 1):
        for k in range(chunks):
            slot = c * z_count + lax.rem(z - step * hop + 2 * z_count, z_count)
            arrive(slot, k)
            if hop < fwd_hops:
                send(out_ref.at[slot], rt_out.at[slot], slot, k, fwd_id)
            send(out_ref.at[slot], rt_out.at[slot], slot, k, pair_id)
            if hop <= bwd_hops:
                slot = c * z_count + lax.rem(z + step * hop + 2 * z_count, z_count)
                arrive(slot, k)
                if hop < bwd_hops:
                    send(out_ref.at[slot], rt_out.at[slot], slot, k, bwd_id)
                send(out_ref.at[slot], rt_out.at[slot], slot, k, pair_id)
    for zz in range(z_count):
        for k in range(chunks):
            arrive(other * z_count + zz, k)
    local.wait()
    local_rt.wait()
    for copy in sends:
        copy.wait_send()


def gather_blocks(block, route_tile, z_count, chunks):
    count = 2 * z_count
    vmem = pl.BlockSpec(memory_space=pltpu.VMEM)
    return pl.pallas_call(
        functools.partial(dispatch_kernel, z_count, chunks),
        out_shape=(
            jax.ShapeDtypeStruct((count,) + block.shape, block.dtype),
            jax.ShapeDtypeStruct((count,) + route_tile.shape, route_tile.dtype),
        ),
        in_specs=[vmem, vmem],
        out_specs=(vmem, vmem),
        scratch_shapes=[
            pltpu.SemaphoreType.DMA((3 * count * chunks,)),
            pltpu.SemaphoreType.DMA((count * chunks,)),
            pltpu.SemaphoreType.DMA((count,)),
            pltpu.SemaphoreType.DMA((2,)),
        ],
        compiler_params=pltpu.CompilerParams(
            collective_id=0, has_side_effects=True, vmem_limit_bytes=32 * 1024 * 1024
        ),
    )(block, route_tile)


def combine_kernel(
    z_count, dp_count, seq_len, chunks, part_ref, head_ref, out_ref, pair_out, pair_buf,
    fwd_buf, bwd_buf, fwd_out, bwd_out, seq_out, seq_in, send_sem, recv_sem, seq_sem,
):
    z = lax.axis_index("z")
    c = lax.axis_index("c")
    row = lax.axis_index("dp")
    other = 1 - c
    step = 1 - 2 * c
    fwd = lax.rem(z + step + z_count, z_count)
    bwd = lax.rem(z - step + z_count, z_count)
    fwd_id, bwd_id, pair_id = (row, fwd, c), (row, bwd, c), (row, z, other)
    mate_id = (lax.rem(row + dp_count // 2, dp_count), z, c)
    fwd_hops = z_count // 2
    bwd_hops = z_count - 1 - fwd_hops
    piece = part_ref.shape[2] // chunks

    barrier = pltpu.get_barrier_semaphore()
    for target in (fwd_id, bwd_id, pair_id, mate_id):
        pl.semaphore_signal(barrier, 1, device_id=target, device_id_type=MESH)
    pl.semaphore_wait(barrier, 4)

    sends = []

    def send(src, dst, sem, target):
        copy = pltpu.make_async_remote_copy(
            src_ref=src,
            dst_ref=dst,
            send_sem=send_sem.at[len(sends)],
            recv_sem=recv_sem.at[sem],
            device_id=target,
            device_id_type=MESH,
        )
        copy.start()
        sends.append(copy)

    def arrive(dst, sem):
        pltpu.make_async_remote_copy(
            src_ref=dst,
            dst_ref=dst,
            send_sem=send_sem.at[0],
            recv_sem=recv_sem.at[sem],
            device_id=pair_id,
            device_id_type=MESH,
        ).wait_recv()

    def order(ring_step):
        dests = []
        for hop in range(1, fwd_hops + 1):
            dests.append(lax.rem(z + ring_step * (fwd_hops + 1 - hop) + 2 * z_count, z_count))
            if hop <= bwd_hops:
                dests.append(lax.rem(z - ring_step * (bwd_hops + 1 - hop) + 2 * z_count, z_count))
        return dests + [z]

    for n, dest in enumerate(order(-step)):
        send(part_ref.at[other, dest], pair_buf.at[n], n, pair_id)
    def own(dest, n, k):
        if k == 0:
            arrive(pair_buf.at[n], n)
        rows = pl.ds(k * piece, piece)
        return part_ref[c, dest, rows].astype(jnp.float32) + pair_buf[n, rows].astype(
            jnp.float32
        )

    fwd_sem = z_count
    bwd_sem = z_count + fwd_hops * chunks
    for hop in range(1, fwd_hops + 1):
        for k in range(chunks):
            rows = pl.ds(k * piece, piece)
            dest = lax.rem(z + step * (fwd_hops + 1 - hop) + 2 * z_count, z_count)
            n = hop - 1 + min(hop - 1, bwd_hops)
            total = own(dest, n, k)
            if hop > 1:
                sem = fwd_sem + (hop - 2) * chunks + k
                arrive(fwd_buf.at[hop - 2, rows], sem)
                total = total + fwd_buf[hop - 2, rows].astype(jnp.float32)
            fwd_out[hop - 1, rows] = total.astype(fwd_out.dtype)
            sem = fwd_sem + (hop - 1) * chunks + k
            send(fwd_out.at[hop - 1, rows], fwd_buf.at[hop - 1, rows], sem, fwd_id)
            if hop <= bwd_hops:
                dest = lax.rem(z - step * (bwd_hops + 1 - hop) + 2 * z_count, z_count)
                total = own(dest, n + 1, k)
                if hop > 1:
                    sem = bwd_sem + (hop - 2) * chunks + k
                    arrive(bwd_buf.at[hop - 2, rows], sem)
                    total = total + bwd_buf[hop - 2, rows].astype(jnp.float32)
                bwd_out[hop - 1, rows] = total.astype(bwd_out.dtype)
                sem = bwd_sem + (hop - 1) * chunks + k
                send(bwd_out.at[hop - 1, rows], bwd_buf.at[hop - 1, rows], sem, bwd_id)
    for k in range(chunks):
        rows = pl.ds(k * piece, piece)
        total = own(z, fwd_hops + bwd_hops, k)
        arrive(fwd_buf.at[fwd_hops - 1, rows], fwd_sem + (fwd_hops - 1) * chunks + k)
        total = total + fwd_buf[fwd_hops - 1, rows].astype(jnp.float32)
        if bwd_hops > 0:
            arrive(bwd_buf.at[bwd_hops - 1, rows], bwd_sem + (bwd_hops - 1) * chunks + k)
            total = total + bwd_buf[bwd_hops - 1, rows].astype(jnp.float32)
        out_ref[rows] = total.astype(out_ref.dtype)
    tok_rows, width = out_ref.shape
    seqs = tok_rows // seq_len
    scored = out_ref[...].astype(jnp.float32) * head_ref[...]
    per_seq = jnp.sum(scored.reshape(seqs, seq_len, width), axis=1)
    seq_score = jnp.sum(per_seq, axis=1, keepdims=True)
    seq_out[...] = jnp.zeros(seq_out.shape, jnp.float32)
    seq_out[pl.ds(0, seqs)] = jnp.broadcast_to(seq_score, (seqs, seq_out.shape[1]))
    mate = pltpu.make_async_remote_copy(
        src_ref=seq_out,
        dst_ref=seq_in,
        send_sem=seq_sem.at[0],
        recv_sem=seq_sem.at[1],
        device_id=mate_id,
        device_id_type=MESH,
    )
    mate.start()
    mate.wait()
    mine = seq_out[...]
    theirs = seq_in[...]
    pair_out[...] = jnp.abs(mine - theirs) + 0.5 * (mine + theirs)
    for copy in sends:
        copy.wait_send()


def scatter_sums(partial, score_head, dp_count, seq_len, chunks):
    c_count, z_count, rows, width = partial.shape
    fwd_hops = z_count // 2
    bwd_hops = max(z_count - 1 - fwd_hops, 1)
    block = (rows, width)
    vmem = pl.BlockSpec(memory_space=pltpu.VMEM)
    sems = z_count + (fwd_hops + bwd_hops) * chunks
    tile = (8, 128)
    return pl.pallas_call(
        functools.partial(combine_kernel, z_count, dp_count, seq_len, chunks),
        out_shape=(
            jax.ShapeDtypeStruct(block, partial.dtype),
            jax.ShapeDtypeStruct(tile, jnp.float32),
        ),
        in_specs=[vmem, vmem],
        out_specs=(vmem, vmem),
        scratch_shapes=[
            pltpu.VMEM((z_count,) + block, partial.dtype),
            pltpu.VMEM((fwd_hops,) + block, partial.dtype),
            pltpu.VMEM((bwd_hops,) + block, partial.dtype),
            pltpu.VMEM((fwd_hops,) + block, partial.dtype),
            pltpu.VMEM((bwd_hops,) + block, partial.dtype),
            pltpu.VMEM(tile, jnp.float32),
            pltpu.VMEM(tile, jnp.float32),
            pltpu.SemaphoreType.DMA((sems,)),
            pltpu.SemaphoreType.DMA((sems,)),
            pltpu.SemaphoreType.DMA((2,)),
        ],
        compiler_params=pltpu.CompilerParams(
            collective_id=1, has_side_effects=True, vmem_limit_bytes=48 * 1024 * 1024
        ),
    )(partial, score_head.reshape(1, -1))


def body(
    tokens, expert_ids, gate_fixed, scorer_id, direction_tags, w_gate, w_up, w_down, score_head
):
    z_count = lax.axis_size("z")
    c_count = lax.axis_size("c")
    expert_count = z_count * c_count
    per_device = w_gate.shape[0]
    tok_rows, model_width = tokens.shape
    top_count = expert_ids.shape[1]
    which_tag = jnp.repeat(scorer_id, SEQ_LEN)[:, None]
    tag_rows = jnp.where(
        which_tag == 1, direction_tags[1][None, :], direction_tags[0][None, :]
    ).astype(jnp.float32)
    inputs = (tokens.astype(jnp.float32) + tag_rows).astype(jnp.bfloat16)
    rank_in = route_ranks(expert_ids, per_device * expert_count)
    routes = jnp.concatenate(
        [expert_ids, rank_in, gate_fixed // 256, gate_fixed % 256], axis=1
    ).astype(jnp.bfloat16)
    route_tile = routes.reshape(-1, 128)
    inputs_all, routes_all = gather_blocks(inputs, route_tile, z_count, 2)
    routes_all = routes_all.reshape(expert_count, tok_rows, 4 * top_count).astype(jnp.int32)
    ids_cube = routes_all[..., :top_count]
    rank_cube = routes_all[..., top_count : 2 * top_count]
    fixed_val = (
        routes_all[..., 2 * top_count : 3 * top_count] * 256 + routes_all[..., 3 * top_count :]
    ).astype(jnp.float32)
    weight_cube = fixed_val / jnp.sum(fixed_val, axis=2, keepdims=True)
    my_index = lax.axis_index("z") * c_count + lax.axis_index("c")
    local_count = per_device * MOST
    local_slot = ids_cube - my_index * per_device
    is_mine = (local_slot >= 0) & (local_slot < per_device)
    local_key = jnp.where(is_mine, local_slot * MOST + rank_cube, -1)
    match = (
        local_key[:, None, :, :] == jnp.arange(local_count, dtype=jnp.int32)[None, :, None, None]
    )
    picker = jnp.any(match, axis=3).astype(jnp.bfloat16)
    slot_weight = jnp.sum(jnp.where(match, weight_cube[:, None, :, :], 0.0), axis=(2, 3))
    picker = picker.reshape(expert_count, per_device, MOST, tok_rows).transpose(1, 0, 2, 3)
    slot_weight = slot_weight.reshape(expert_count, per_device, MOST).transpose(1, 0, 2)
    row_block = jnp.einsum(
        "esmt,std->esmd", picker, inputs_all, preferred_element_type=jnp.float32
    ).astype(jnp.bfloat16)
    gate_proj = jnp.einsum("esmd,edf->esmf", row_block, w_gate, preferred_element_type=jnp.float32)
    up_proj = jnp.einsum("esmd,edf->esmf", row_block, w_up, preferred_element_type=jnp.float32)
    hidden = (jax.nn.silu(gate_proj) * up_proj).astype(jnp.bfloat16)
    down_out = jnp.einsum("esmf,efd->esmd", hidden, w_down, preferred_element_type=jnp.float32)
    result = (slot_weight[..., None] * down_out).astype(jnp.bfloat16)
    result = lax.optimization_barrier(result)
    partial_value = jnp.einsum(
        "esmt,esmd->std", picker, result, preferred_element_type=jnp.float32
    )
    partial_value = partial_value.reshape(c_count, z_count, tok_rows, model_width)
    mixed, pair_tile = scatter_sums(
        partial_value.astype(jnp.bfloat16), score_head, lax.axis_size("dp"), SEQ_LEN, 2
    )
    pair_score = pair_tile[: tok_rows // SEQ_LEN, 0]
    return (mixed, pair_score)


def solution(mesh):
    dp_count, expert_count = mesh.devices.shape
    split = Mesh(mesh.devices.reshape(dp_count, expert_count // 2, 2), ("dp", "z", "c"))
    rows = P(("dp", "z", "c"), None)
    return jax.shard_map(
        body,
        mesh=split,
        in_specs=(
            rows,
            rows,
            rows,
            P(("dp", "z", "c")),
            P(),
            P(("z", "c"), None, None),
            P(("z", "c"), None, None),
            P(("z", "c"), None, None),
            P(),
        ),
        out_specs=(rows, P(("dp", "z", "c"))),
        check_vma=False,
    )
```

```python
import functools

import jax
import jax.numpy as jnp
from jax import lax
from jax.experimental import pallas as pl
from jax.experimental.pallas import tpu as pltpu
from jax.sharding import Mesh
from jax.sharding import PartitionSpec as P

SEQ_LEN = 16
MOST = 24


def from_partner(block, axis, bit):
    count = lax.axis_size(axis)
    route = []
    for low in range(count):
        high = low | 1 << bit
        if high != low and high < count:
            route += [(low, high), (high, low)]
    return lax.ppermute(block, axis, route)


def route_ranks(expert_ids, expert_total):
    flat_ids = expert_ids.reshape(-1)
    entry_count = flat_ids.shape[0]
    onehot = flat_ids[:, None] == jnp.arange(expert_total, dtype=jnp.int32)[None, :]
    positions = jnp.arange(entry_count, dtype=jnp.int32)
    earlier = (positions[:, None] > positions[None, :]).astype(jnp.bfloat16)
    counts = jnp.dot(earlier, onehot.astype(jnp.bfloat16), preferred_element_type=jnp.float32)
    rank_in = jnp.sum(jnp.where(onehot, counts, 0.0), axis=1).astype(jnp.int32)
    return rank_in.reshape(expert_ids.shape)


MESH = pl.DeviceIdType.MESH


def dispatch_kernel(z_count, chunks, blk_ref, out_ref, send_sem, recv_sem, local_sem):
    z = lax.axis_index("z")
    c = lax.axis_index("c")
    row = lax.axis_index("dp")
    other = 1 - c
    step = 1 - 2 * c
    fwd = lax.rem(z + step + z_count, z_count)
    bwd = lax.rem(z - step + z_count, z_count)
    fwd_id, bwd_id, pair_id = (row, fwd, c), (row, bwd, c), (row, z, other)
    piece = blk_ref.shape[0] // chunks

    barrier = pltpu.get_barrier_semaphore()
    for target in (fwd_id, bwd_id, pair_id):
        pl.semaphore_signal(barrier, 1, device_id=target, device_id_type=MESH)
    pl.semaphore_wait(barrier, 3)

    mine = c * z_count + z
    local = pltpu.make_async_copy(blk_ref, out_ref.at[mine], local_sem.at[0])
    local.start()
    sends = []

    def part(ref, k):
        return ref.at[pl.ds(k * piece, piece)]

    def send(src, slot, k, target):
        copy = pltpu.make_async_remote_copy(
            src_ref=part(src, k),
            dst_ref=part(out_ref.at[slot], k),
            send_sem=send_sem.at[len(sends)],
            recv_sem=recv_sem.at[slot * chunks + k],
            device_id=target,
            device_id_type=MESH,
        )
        copy.start()
        sends.append(copy)

    def arrive(slot, k):
        view = part(out_ref.at[slot], k)
        pltpu.make_async_remote_copy(
            src_ref=view,
            dst_ref=view,
            send_sem=send_sem.at[0],
            recv_sem=recv_sem.at[slot * chunks + k],
            device_id=pair_id,
            device_id_type=MESH,
        ).wait_recv()

    for k in range(chunks):
        send(blk_ref, mine, k, fwd_id)
        send(blk_ref, mine, k, bwd_id)
    for k in range(chunks):
        send(blk_ref, mine, k, pair_id)
    fwd_hops = z_count // 2
    bwd_hops = z_count - 1 - fwd_hops
    for hop in range(1, fwd_hops + 1):
        for k in range(chunks):
            slot = c * z_count + lax.rem(z - step * hop + 2 * z_count, z_count)
            arrive(slot, k)
            if hop < fwd_hops:
                send(out_ref.at[slot], slot, k, fwd_id)
            send(out_ref.at[slot], slot, k, pair_id)
            if hop <= bwd_hops:
                slot = c * z_count + lax.rem(z + step * hop + 2 * z_count, z_count)
                arrive(slot, k)
                if hop < bwd_hops:
                    send(out_ref.at[slot], slot, k, bwd_id)
                send(out_ref.at[slot], slot, k, pair_id)
    for zz in range(z_count):
        for k in range(chunks):
            arrive(other * z_count + zz, k)
    local.wait()
    for copy in sends:
        copy.wait_send()


def gather_blocks(block, z_count, chunks):
    count = 2 * z_count
    return pl.pallas_call(
        functools.partial(dispatch_kernel, z_count, chunks),
        out_shape=jax.ShapeDtypeStruct((count,) + block.shape, block.dtype),
        in_specs=[pl.BlockSpec(memory_space=pltpu.VMEM)],
        out_specs=pl.BlockSpec(memory_space=pltpu.VMEM),
        scratch_shapes=[
            pltpu.SemaphoreType.DMA((2 * count * chunks,)),
            pltpu.SemaphoreType.DMA((count * chunks,)),
            pltpu.SemaphoreType.DMA((1,)),
        ],
        compiler_params=pltpu.CompilerParams(
            collective_id=0, has_side_effects=True, vmem_limit_bytes=32 * 1024 * 1024
        ),
    )(block)


def combine_kernel(
    z_count, dp_count, seq_len, chunks, part_ref, head_ref, out_ref, pair_out, pair_buf,
    fwd_buf, bwd_buf, fwd_out, bwd_out, seq_out, seq_in, send_sem, recv_sem, seq_sem,
):
    z = lax.axis_index("z")
    c = lax.axis_index("c")
    row = lax.axis_index("dp")
    other = 1 - c
    step = 1 - 2 * c
    fwd = lax.rem(z + step + z_count, z_count)
    bwd = lax.rem(z - step + z_count, z_count)
    fwd_id, bwd_id, pair_id = (row, fwd, c), (row, bwd, c), (row, z, other)
    mate_id = (lax.rem(row + dp_count // 2, dp_count), z, c)
    fwd_hops = z_count // 2
    bwd_hops = z_count - 1 - fwd_hops
    piece = part_ref.shape[2] // chunks

    barrier = pltpu.get_barrier_semaphore()
    for target in (fwd_id, bwd_id, pair_id, mate_id):
        pl.semaphore_signal(barrier, 1, device_id=target, device_id_type=MESH)
    pl.semaphore_wait(barrier, 4)

    sends = []

    def send(src, dst, sem, target):
        copy = pltpu.make_async_remote_copy(
            src_ref=src,
            dst_ref=dst,
            send_sem=send_sem.at[len(sends)],
            recv_sem=recv_sem.at[sem],
            device_id=target,
            device_id_type=MESH,
        )
        copy.start()
        sends.append(copy)

    def arrive(dst, sem):
        pltpu.make_async_remote_copy(
            src_ref=dst,
            dst_ref=dst,
            send_sem=send_sem.at[0],
            recv_sem=recv_sem.at[sem],
            device_id=pair_id,
            device_id_type=MESH,
        ).wait_recv()

    def order(ring_step):
        dests = []
        for hop in range(1, fwd_hops + 1):
            dests.append(lax.rem(z + ring_step * (fwd_hops + 1 - hop) + 2 * z_count, z_count))
            if hop <= bwd_hops:
                dests.append(lax.rem(z - ring_step * (bwd_hops + 1 - hop) + 2 * z_count, z_count))
        return dests + [z]

    partner_order = order(-step)

    def send_pair(n):
        if n < len(partner_order):
            send(part_ref.at[other, partner_order[n]], pair_buf.at[n], n, pair_id)

    send_pair(0)
    send_pair(1)

    def own(dest, n, k):
        if k == 0:
            send_pair(n + 2)
            arrive(pair_buf.at[n], n)
        rows = pl.ds(k * piece, piece)
        return part_ref[c, dest, rows].astype(jnp.float32) + pair_buf[n, rows].astype(
            jnp.float32
        )

    fwd_sem = z_count
    bwd_sem = z_count + fwd_hops * chunks
    for hop in range(1, fwd_hops + 1):
        for k in range(chunks):
            rows = pl.ds(k * piece, piece)
            dest = lax.rem(z + step * (fwd_hops + 1 - hop) + 2 * z_count, z_count)
            n = hop - 1 + min(hop - 1, bwd_hops)
            total = own(dest, n, k)
            if hop > 1:
                sem = fwd_sem + (hop - 2) * chunks + k
                arrive(fwd_buf.at[hop - 2, rows], sem)
                total = total + fwd_buf[hop - 2, rows].astype(jnp.float32)
            fwd_out[hop - 1, rows] = total.astype(fwd_out.dtype)
            sem = fwd_sem + (hop - 1) * chunks + k
            send(fwd_out.at[hop - 1, rows], fwd_buf.at[hop - 1, rows], sem, fwd_id)
            if hop <= bwd_hops:
                dest = lax.rem(z - step * (bwd_hops + 1 - hop) + 2 * z_count, z_count)
                total = own(dest, n + 1, k)
                if hop > 1:
                    sem = bwd_sem + (hop - 2) * chunks + k
                    arrive(bwd_buf.at[hop - 2, rows], sem)
                    total = total + bwd_buf[hop - 2, rows].astype(jnp.float32)
                bwd_out[hop - 1, rows] = total.astype(bwd_out.dtype)
                sem = bwd_sem + (hop - 1) * chunks + k
                send(bwd_out.at[hop - 1, rows], bwd_buf.at[hop - 1, rows], sem, bwd_id)
    for k in range(chunks):
        rows = pl.ds(k * piece, piece)
        total = own(z, fwd_hops + bwd_hops, k)
        arrive(fwd_buf.at[fwd_hops - 1, rows], fwd_sem + (fwd_hops - 1) * chunks + k)
        total = total + fwd_buf[fwd_hops - 1, rows].astype(jnp.float32)
        if bwd_hops > 0:
            arrive(bwd_buf.at[bwd_hops - 1, rows], bwd_sem + (bwd_hops - 1) * chunks + k)
            total = total + bwd_buf[bwd_hops - 1, rows].astype(jnp.float32)
        out_ref[rows] = total.astype(out_ref.dtype)
    tok_rows, width = out_ref.shape
    seqs = tok_rows // seq_len
    scored = out_ref[...].astype(jnp.float32) * head_ref[...]
    per_seq = jnp.sum(scored.reshape(seqs, seq_len, width), axis=1)
    seq_score = jnp.sum(per_seq, axis=1, keepdims=True)
    seq_out[...] = jnp.zeros(seq_out.shape, jnp.float32)
    seq_out[pl.ds(0, seqs)] = jnp.broadcast_to(seq_score, (seqs, seq_out.shape[1]))
    mate = pltpu.make_async_remote_copy(
        src_ref=seq_out,
        dst_ref=seq_in,
        send_sem=seq_sem.at[0],
        recv_sem=seq_sem.at[1],
        device_id=mate_id,
        device_id_type=MESH,
    )
    mate.start()
    mate.wait()
    mine = seq_out[...]
    theirs = seq_in[...]
    pair_out[...] = jnp.abs(mine - theirs) + 0.5 * (mine + theirs)
    for copy in sends:
        copy.wait_send()


def scatter_sums(partial, score_head, dp_count, seq_len, chunks):
    c_count, z_count, rows, width = partial.shape
    fwd_hops = z_count // 2
    bwd_hops = max(z_count - 1 - fwd_hops, 1)
    block = (rows, width)
    vmem = pl.BlockSpec(memory_space=pltpu.VMEM)
    sems = z_count + (fwd_hops + bwd_hops) * chunks
    tile = (8, 128)
    return pl.pallas_call(
        functools.partial(combine_kernel, z_count, dp_count, seq_len, chunks),
        out_shape=(
            jax.ShapeDtypeStruct(block, partial.dtype),
            jax.ShapeDtypeStruct(tile, jnp.float32),
        ),
        in_specs=[vmem, vmem],
        out_specs=(vmem, vmem),
        scratch_shapes=[
            pltpu.VMEM((z_count,) + block, partial.dtype),
            pltpu.VMEM((fwd_hops,) + block, partial.dtype),
            pltpu.VMEM((bwd_hops,) + block, partial.dtype),
            pltpu.VMEM((fwd_hops,) + block, partial.dtype),
            pltpu.VMEM((bwd_hops,) + block, partial.dtype),
            pltpu.VMEM(tile, jnp.float32),
            pltpu.VMEM(tile, jnp.float32),
            pltpu.SemaphoreType.DMA((sems,)),
            pltpu.SemaphoreType.DMA((sems,)),
            pltpu.SemaphoreType.DMA((2,)),
        ],
        compiler_params=pltpu.CompilerParams(
            collective_id=1, has_side_effects=True, vmem_limit_bytes=48 * 1024 * 1024
        ),
    )(partial, score_head.reshape(1, -1))


def body(
    tokens, expert_ids, gate_fixed, scorer_id, direction_tags, w_gate, w_up, w_down, score_head
):
    z_count = lax.axis_size("z")
    c_count = lax.axis_size("c")
    expert_count = z_count * c_count
    per_device = w_gate.shape[0]
    tok_rows, model_width = tokens.shape
    top_count = expert_ids.shape[1]
    which_tag = jnp.repeat(scorer_id, SEQ_LEN)[:, None]
    tag_rows = jnp.where(
        which_tag == 1, direction_tags[1][None, :], direction_tags[0][None, :]
    ).astype(jnp.float32)
    inputs = (tokens.astype(jnp.float32) + tag_rows).astype(jnp.bfloat16)
    rank_in = route_ranks(expert_ids, per_device * expert_count)
    routes = jnp.concatenate(
        [expert_ids, rank_in, gate_fixed // 256, gate_fixed % 256], axis=1
    ).astype(jnp.bfloat16)
    routes = jnp.pad(routes, ((0, 0), (0, 128 - 4 * top_count)))
    block = jnp.concatenate([inputs, routes], axis=1)
    gathered = gather_blocks(block, z_count, 2)
    inputs_all = gathered[:, :, :model_width]
    routes_all = gathered[:, :, model_width : model_width + 4 * top_count].astype(jnp.int32)
    ids_cube = routes_all[..., :top_count]
    rank_cube = routes_all[..., top_count : 2 * top_count]
    fixed_val = (
        routes_all[..., 2 * top_count : 3 * top_count] * 256 + routes_all[..., 3 * top_count :]
    ).astype(jnp.float32)
    weight_cube = fixed_val / jnp.sum(fixed_val, axis=2, keepdims=True)
    my_index = lax.axis_index("z") * c_count + lax.axis_index("c")
    local_count = per_device * MOST
    local_slot = ids_cube - my_index * per_device
    is_mine = (local_slot >= 0) & (local_slot < per_device)
    local_key = jnp.where(is_mine, local_slot * MOST + rank_cube, -1)
    match = (
        local_key[:, None, :, :] == jnp.arange(local_count, dtype=jnp.int32)[None, :, None, None]
    )
    picker = jnp.any(match, axis=3).astype(jnp.bfloat16)
    slot_weight = jnp.sum(jnp.where(match, weight_cube[:, None, :, :], 0.0), axis=(2, 3))
    picker = picker.reshape(expert_count, per_device, MOST, tok_rows).transpose(1, 0, 2, 3)
    slot_weight = slot_weight.reshape(expert_count, per_device, MOST).transpose(1, 0, 2)
    row_block = jnp.einsum(
        "esmt,std->esmd", picker, inputs_all, preferred_element_type=jnp.float32
    ).astype(jnp.bfloat16)
    gate_proj = jnp.einsum("esmd,edf->esmf", row_block, w_gate, preferred_element_type=jnp.float32)
    up_proj = jnp.einsum("esmd,edf->esmf", row_block, w_up, preferred_element_type=jnp.float32)
    hidden = (jax.nn.silu(gate_proj) * up_proj).astype(jnp.bfloat16)
    down_out = jnp.einsum("esmf,efd->esmd", hidden, w_down, preferred_element_type=jnp.float32)
    result = (slot_weight[..., None] * down_out).astype(jnp.bfloat16)
    result = lax.optimization_barrier(result)
    partial_value = jnp.einsum(
        "esmt,esmd->std", picker, result, preferred_element_type=jnp.float32
    )
    partial_value = partial_value.reshape(c_count, z_count, tok_rows, model_width)
    mixed, pair_tile = scatter_sums(
        partial_value.astype(jnp.bfloat16), score_head, lax.axis_size("dp"), SEQ_LEN, 2
    )
    pair_score = pair_tile[: tok_rows // SEQ_LEN, 0]
    return (mixed, pair_score)


def solution(mesh):
    dp_count, expert_count = mesh.devices.shape
    split = Mesh(mesh.devices.reshape(dp_count, expert_count // 2, 2), ("dp", "z", "c"))
    rows = P(("dp", "z", "c"), None)
    return jax.shard_map(
        body,
        mesh=split,
        in_specs=(
            rows,
            rows,
            rows,
            P(("dp", "z", "c")),
            P(),
            P(("z", "c"), None, None),
            P(("z", "c"), None, None),
            P(("z", "c"), None, None),
            P(),
        ),
        out_specs=(rows, P(("dp", "z", "c"))),
        check_vma=False,
    )
```

```python
import functools

import jax
import jax.numpy as jnp
from jax import lax
from jax.experimental import pallas as pl
from jax.experimental.pallas import tpu as pltpu
from jax.sharding import Mesh
from jax.sharding import PartitionSpec as P

SEQ_LEN = 16
MOST = 24


def from_partner(block, axis, bit):
    count = lax.axis_size(axis)
    route = []
    for low in range(count):
        high = low | 1 << bit
        if high != low and high < count:
            route += [(low, high), (high, low)]
    return lax.ppermute(block, axis, route)


def route_ranks(expert_ids, expert_total):
    tok_rows = expert_ids.shape[0]
    onehot = expert_ids[:, :, None] == jnp.arange(expert_total, dtype=jnp.int32)[None, None, :]
    per_token = jnp.any(onehot, axis=1).astype(jnp.bfloat16)
    positions = jnp.arange(tok_rows, dtype=jnp.int32)
    earlier = (positions[:, None] > positions[None, :]).astype(jnp.bfloat16)
    counts = jnp.dot(earlier, per_token, preferred_element_type=jnp.float32)
    return jnp.sum(jnp.where(onehot, counts[:, None, :], 0.0), axis=2).astype(jnp.int32)


MESH = pl.DeviceIdType.MESH


def dispatch_kernel(z_count, chunks, blk_ref, out_ref, send_sem, recv_sem, local_sem):
    z = lax.axis_index("z")
    c = lax.axis_index("c")
    row = lax.axis_index("dp")
    other = 1 - c
    step = 1 - 2 * c
    fwd = lax.rem(z + step + z_count, z_count)
    bwd = lax.rem(z - step + z_count, z_count)
    fwd_id, bwd_id, pair_id = (row, fwd, c), (row, bwd, c), (row, z, other)
    piece = blk_ref.shape[0] // chunks

    barrier = pltpu.get_barrier_semaphore()
    for target in (fwd_id, bwd_id, pair_id):
        pl.semaphore_signal(barrier, 1, device_id=target, device_id_type=MESH)
    pl.semaphore_wait(barrier, 3)

    mine = c * z_count + z
    local = pltpu.make_async_copy(blk_ref, out_ref.at[mine], local_sem.at[0])
    local.start()
    sends = []

    def part(ref, k):
        return ref.at[pl.ds(k * piece, piece)]

    def send(src, slot, k, target):
        copy = pltpu.make_async_remote_copy(
            src_ref=part(src, k),
            dst_ref=part(out_ref.at[slot], k),
            send_sem=send_sem.at[len(sends)],
            recv_sem=recv_sem.at[slot * chunks + k],
            device_id=target,
            device_id_type=MESH,
        )
        copy.start()
        sends.append(copy)

    def arrive(slot, k):
        view = part(out_ref.at[slot], k)
        pltpu.make_async_remote_copy(
            src_ref=view,
            dst_ref=view,
            send_sem=send_sem.at[0],
            recv_sem=recv_sem.at[slot * chunks + k],
            device_id=pair_id,
            device_id_type=MESH,
        ).wait_recv()

    for k in range(chunks):
        send(blk_ref, mine, k, fwd_id)
        send(blk_ref, mine, k, bwd_id)
    for k in range(chunks):
        send(blk_ref, mine, k, pair_id)
    fwd_hops = z_count // 2
    bwd_hops = z_count - 1 - fwd_hops
    for hop in range(1, fwd_hops + 1):
        for k in range(chunks):
            slot = c * z_count + lax.rem(z - step * hop + 2 * z_count, z_count)
            arrive(slot, k)
            if hop < fwd_hops:
                send(out_ref.at[slot], slot, k, fwd_id)
            send(out_ref.at[slot], slot, k, pair_id)
            if hop <= bwd_hops:
                slot = c * z_count + lax.rem(z + step * hop + 2 * z_count, z_count)
                arrive(slot, k)
                if hop < bwd_hops:
                    send(out_ref.at[slot], slot, k, bwd_id)
                send(out_ref.at[slot], slot, k, pair_id)
    for zz in range(z_count):
        for k in range(chunks):
            arrive(other * z_count + zz, k)
    local.wait()
    for copy in sends:
        copy.wait_send()


def gather_blocks(block, z_count, chunks):
    count = 2 * z_count
    return pl.pallas_call(
        functools.partial(dispatch_kernel, z_count, chunks),
        out_shape=jax.ShapeDtypeStruct((count,) + block.shape, block.dtype),
        in_specs=[pl.BlockSpec(memory_space=pltpu.VMEM)],
        out_specs=pl.BlockSpec(memory_space=pltpu.VMEM),
        scratch_shapes=[
            pltpu.SemaphoreType.DMA((2 * count * chunks,)),
            pltpu.SemaphoreType.DMA((count * chunks,)),
            pltpu.SemaphoreType.DMA((1,)),
        ],
        compiler_params=pltpu.CompilerParams(
            collective_id=0, has_side_effects=True, vmem_limit_bytes=32 * 1024 * 1024
        ),
    )(block)


def combine_kernel(
    z_count, dp_count, seq_len, chunks, part_ref, head_ref, out_ref, pair_out, pair_buf,
    fwd_buf, bwd_buf, fwd_out, bwd_out, seq_out, seq_in, send_sem, recv_sem, seq_sem,
):
    z = lax.axis_index("z")
    c = lax.axis_index("c")
    row = lax.axis_index("dp")
    other = 1 - c
    step = 1 - 2 * c
    fwd = lax.rem(z + step + z_count, z_count)
    bwd = lax.rem(z - step + z_count, z_count)
    fwd_id, bwd_id, pair_id = (row, fwd, c), (row, bwd, c), (row, z, other)
    mate_id = (lax.rem(row + dp_count // 2, dp_count), z, c)
    fwd_hops = z_count // 2
    bwd_hops = z_count - 1 - fwd_hops
    piece = part_ref.shape[2] // chunks

    barrier = pltpu.get_barrier_semaphore()
    for target in (fwd_id, bwd_id, pair_id, mate_id):
        pl.semaphore_signal(barrier, 1, device_id=target, device_id_type=MESH)
    pl.semaphore_wait(barrier, 4)

    sends = []

    def send(src, dst, sem, target):
        copy = pltpu.make_async_remote_copy(
            src_ref=src,
            dst_ref=dst,
            send_sem=send_sem.at[len(sends)],
            recv_sem=recv_sem.at[sem],
            device_id=target,
            device_id_type=MESH,
        )
        copy.start()
        sends.append(copy)

    def arrive(dst, sem):
        pltpu.make_async_remote_copy(
            src_ref=dst,
            dst_ref=dst,
            send_sem=send_sem.at[0],
            recv_sem=recv_sem.at[sem],
            device_id=pair_id,
            device_id_type=MESH,
        ).wait_recv()

    def order(ring_step):
        dests = []
        for hop in range(1, fwd_hops + 1):
            dests.append(lax.rem(z + ring_step * (fwd_hops + 1 - hop) + 2 * z_count, z_count))
            if hop <= bwd_hops:
                dests.append(lax.rem(z - ring_step * (bwd_hops + 1 - hop) + 2 * z_count, z_count))
        return dests + [z]

    for n, dest in enumerate(order(-step)):
        send(part_ref.at[other, dest], pair_buf.at[n], n, pair_id)
    def own(dest, n, k):
        if k == 0:
            arrive(pair_buf.at[n], n)
        rows = pl.ds(k * piece, piece)
        return part_ref[c, dest, rows].astype(jnp.float32) + pair_buf[n, rows].astype(
            jnp.float32
        )

    fwd_sem = z_count
    bwd_sem = z_count + fwd_hops * chunks
    for hop in range(1, fwd_hops + 1):
        for k in range(chunks):
            rows = pl.ds(k * piece, piece)
            dest = lax.rem(z + step * (fwd_hops + 1 - hop) + 2 * z_count, z_count)
            n = hop - 1 + min(hop - 1, bwd_hops)
            total = own(dest, n, k)
            if hop > 1:
                sem = fwd_sem + (hop - 2) * chunks + k
                arrive(fwd_buf.at[hop - 2, rows], sem)
                total = total + fwd_buf[hop - 2, rows].astype(jnp.float32)
            fwd_out[hop - 1, rows] = total.astype(fwd_out.dtype)
            sem = fwd_sem + (hop - 1) * chunks + k
            send(fwd_out.at[hop - 1, rows], fwd_buf.at[hop - 1, rows], sem, fwd_id)
            if hop <= bwd_hops:
                dest = lax.rem(z - step * (bwd_hops + 1 - hop) + 2 * z_count, z_count)
                total = own(dest, n + 1, k)
                if hop > 1:
                    sem = bwd_sem + (hop - 2) * chunks + k
                    arrive(bwd_buf.at[hop - 2, rows], sem)
                    total = total + bwd_buf[hop - 2, rows].astype(jnp.float32)
                bwd_out[hop - 1, rows] = total.astype(bwd_out.dtype)
                sem = bwd_sem + (hop - 1) * chunks + k
                send(bwd_out.at[hop - 1, rows], bwd_buf.at[hop - 1, rows], sem, bwd_id)
    for k in range(chunks):
        rows = pl.ds(k * piece, piece)
        total = own(z, fwd_hops + bwd_hops, k)
        arrive(fwd_buf.at[fwd_hops - 1, rows], fwd_sem + (fwd_hops - 1) * chunks + k)
        total = total + fwd_buf[fwd_hops - 1, rows].astype(jnp.float32)
        if bwd_hops > 0:
            arrive(bwd_buf.at[bwd_hops - 1, rows], bwd_sem + (bwd_hops - 1) * chunks + k)
            total = total + bwd_buf[bwd_hops - 1, rows].astype(jnp.float32)
        out_ref[rows] = total.astype(out_ref.dtype)
    tok_rows, width = out_ref.shape
    seqs = tok_rows // seq_len
    scored = out_ref[...].astype(jnp.float32) * head_ref[...]
    per_seq = jnp.sum(scored.reshape(seqs, seq_len, width), axis=1)
    seq_score = jnp.sum(per_seq, axis=1, keepdims=True)
    seq_out[...] = jnp.zeros(seq_out.shape, jnp.float32)
    seq_out[pl.ds(0, seqs)] = jnp.broadcast_to(seq_score, (seqs, seq_out.shape[1]))
    mate = pltpu.make_async_remote_copy(
        src_ref=seq_out,
        dst_ref=seq_in,
        send_sem=seq_sem.at[0],
        recv_sem=seq_sem.at[1],
        device_id=mate_id,
        device_id_type=MESH,
    )
    mate.start()
    mate.wait()
    mine = seq_out[...]
    theirs = seq_in[...]
    pair_out[...] = jnp.abs(mine - theirs) + 0.5 * (mine + theirs)
    for copy in sends:
        copy.wait_send()


def scatter_sums(partial, score_head, dp_count, seq_len, chunks):
    c_count, z_count, rows, width = partial.shape
    fwd_hops = z_count // 2
    bwd_hops = max(z_count - 1 - fwd_hops, 1)
    block = (rows, width)
    vmem = pl.BlockSpec(memory_space=pltpu.VMEM)
    sems = z_count + (fwd_hops + bwd_hops) * chunks
    tile = (8, 128)
    return pl.pallas_call(
        functools.partial(combine_kernel, z_count, dp_count, seq_len, chunks),
        out_shape=(
            jax.ShapeDtypeStruct(block, partial.dtype),
            jax.ShapeDtypeStruct(tile, jnp.float32),
        ),
        in_specs=[vmem, vmem],
        out_specs=(vmem, vmem),
        scratch_shapes=[
            pltpu.VMEM((z_count,) + block, partial.dtype),
            pltpu.VMEM((fwd_hops,) + block, partial.dtype),
            pltpu.VMEM((bwd_hops,) + block, partial.dtype),
            pltpu.VMEM((fwd_hops,) + block, partial.dtype),
            pltpu.VMEM((bwd_hops,) + block, partial.dtype),
            pltpu.VMEM(tile, jnp.float32),
            pltpu.VMEM(tile, jnp.float32),
            pltpu.SemaphoreType.DMA((sems,)),
            pltpu.SemaphoreType.DMA((sems,)),
            pltpu.SemaphoreType.DMA((2,)),
        ],
        compiler_params=pltpu.CompilerParams(
            collective_id=1, has_side_effects=True, vmem_limit_bytes=48 * 1024 * 1024
        ),
    )(partial, score_head.reshape(1, -1))


def body(
    tokens, expert_ids, gate_fixed, scorer_id, direction_tags, w_gate, w_up, w_down, score_head
):
    z_count = lax.axis_size("z")
    c_count = lax.axis_size("c")
    expert_count = z_count * c_count
    per_device = w_gate.shape[0]
    tok_rows, model_width = tokens.shape
    top_count = expert_ids.shape[1]
    which_tag = jnp.repeat(scorer_id, SEQ_LEN)[:, None]
    tag_rows = jnp.where(
        which_tag == 1, direction_tags[1][None, :], direction_tags[0][None, :]
    ).astype(jnp.float32)
    inputs = (tokens.astype(jnp.float32) + tag_rows).astype(jnp.bfloat16)
    rank_in = route_ranks(expert_ids, per_device * expert_count)
    routes = jnp.concatenate(
        [expert_ids, rank_in, gate_fixed // 256, gate_fixed % 256], axis=1
    ).astype(jnp.bfloat16)
    routes = jnp.pad(routes, ((0, 0), (0, 128 - 4 * top_count)))
    block = jnp.concatenate([inputs, routes], axis=1)
    gathered = gather_blocks(block, z_count, 2)
    inputs_all = gathered[:, :, :model_width]
    routes_all = gathered[:, :, model_width : model_width + 4 * top_count].astype(jnp.int32)
    ids_cube = routes_all[..., :top_count]
    rank_cube = routes_all[..., top_count : 2 * top_count]
    fixed_val = (
        routes_all[..., 2 * top_count : 3 * top_count] * 256 + routes_all[..., 3 * top_count :]
    ).astype(jnp.float32)
    weight_cube = fixed_val / jnp.sum(fixed_val, axis=2, keepdims=True)
    my_index = lax.axis_index("z") * c_count + lax.axis_index("c")
    local_count = per_device * MOST
    local_slot = ids_cube - my_index * per_device
    is_mine = (local_slot >= 0) & (local_slot < per_device)
    local_key = jnp.where(is_mine, local_slot * MOST + rank_cube, -1)
    match = (
        local_key[:, None, :, :] == jnp.arange(local_count, dtype=jnp.int32)[None, :, None, None]
    )
    picker = jnp.any(match, axis=3).astype(jnp.bfloat16)
    slot_weight = jnp.sum(jnp.where(match, weight_cube[:, None, :, :], 0.0), axis=(2, 3))
    picker = picker.reshape(expert_count, per_device, MOST, tok_rows).transpose(1, 0, 2, 3)
    slot_weight = slot_weight.reshape(expert_count, per_device, MOST).transpose(1, 0, 2)
    row_block = jnp.einsum(
        "esmt,std->esmd", picker, inputs_all, preferred_element_type=jnp.float32
    ).astype(jnp.bfloat16)
    gate_proj = jnp.einsum("esmd,edf->esmf", row_block, w_gate, preferred_element_type=jnp.float32)
    up_proj = jnp.einsum("esmd,edf->esmf", row_block, w_up, preferred_element_type=jnp.float32)
    hidden = (jax.nn.silu(gate_proj) * up_proj).astype(jnp.bfloat16)
    down_out = jnp.einsum("esmf,efd->esmd", hidden, w_down, preferred_element_type=jnp.float32)
    result = (slot_weight[..., None] * down_out).astype(jnp.bfloat16)
    result = lax.optimization_barrier(result)
    partial_value = jnp.einsum(
        "esmt,esmd->std", picker, result, preferred_element_type=jnp.float32
    )
    partial_value = partial_value.reshape(c_count, z_count, tok_rows, model_width)
    mixed, pair_tile = scatter_sums(
        partial_value.astype(jnp.bfloat16), score_head, lax.axis_size("dp"), SEQ_LEN, 2
    )
    pair_score = pair_tile[: tok_rows // SEQ_LEN, 0]
    return (mixed, pair_score)


def solution(mesh):
    dp_count, expert_count = mesh.devices.shape
    split = Mesh(mesh.devices.reshape(dp_count, expert_count // 2, 2), ("dp", "z", "c"))
    rows = P(("dp", "z", "c"), None)
    return jax.shard_map(
        body,
        mesh=split,
        in_specs=(
            rows,
            rows,
            rows,
            P(("dp", "z", "c")),
            P(),
            P(("z", "c"), None, None),
            P(("z", "c"), None, None),
            P(("z", "c"), None, None),
            P(),
        ),
        out_specs=(rows, P(("dp", "z", "c"))),
        check_vma=False,
    )
```

```python
import functools

import jax
import jax.numpy as jnp
from jax import lax
from jax.experimental import pallas as pl
from jax.experimental.pallas import tpu as pltpu
from jax.sharding import Mesh
from jax.sharding import PartitionSpec as P

SEQ_LEN = 16
MOST = 24


def from_partner(block, axis, bit):
    count = lax.axis_size(axis)
    route = []
    for low in range(count):
        high = low | 1 << bit
        if high != low and high < count:
            route += [(low, high), (high, low)]
    return lax.ppermute(block, axis, route)


def route_ranks(expert_ids, expert_total):
    flat_ids = expert_ids.reshape(-1)
    entry_count = flat_ids.shape[0]
    onehot = flat_ids[:, None] == jnp.arange(expert_total, dtype=jnp.int32)[None, :]
    positions = jnp.arange(entry_count, dtype=jnp.int32)
    earlier = (positions[:, None] > positions[None, :]).astype(jnp.bfloat16)
    counts = jnp.dot(earlier, onehot.astype(jnp.bfloat16), preferred_element_type=jnp.float32)
    rank_in = jnp.sum(jnp.where(onehot, counts, 0.0), axis=1).astype(jnp.int32)
    return rank_in.reshape(expert_ids.shape)


MESH = pl.DeviceIdType.MESH


def dispatch_kernel(z_count, chunks, blk_ref, out_ref, send_sem, recv_sem, local_sem):
    z = lax.axis_index("z")
    c = lax.axis_index("c")
    row = lax.axis_index("dp")
    other = 1 - c
    step = 1 - 2 * c
    fwd = lax.rem(z + step + z_count, z_count)
    bwd = lax.rem(z - step + z_count, z_count)
    fwd_id, bwd_id, pair_id = (row, fwd, c), (row, bwd, c), (row, z, other)
    piece = blk_ref.shape[0] // chunks

    barrier = pltpu.get_barrier_semaphore()
    for target in (fwd_id, bwd_id, pair_id):
        pl.semaphore_signal(barrier, 1, device_id=target, device_id_type=MESH)
    pl.semaphore_wait(barrier, 3)

    mine = c * z_count + z
    local = pltpu.make_async_copy(blk_ref, out_ref.at[mine], local_sem.at[0])
    local.start()
    sends = []

    def part(ref, k):
        return ref.at[pl.ds(k * piece, piece)]

    def send(src, slot, k, target):
        copy = pltpu.make_async_remote_copy(
            src_ref=part(src, k),
            dst_ref=part(out_ref.at[slot], k),
            send_sem=send_sem.at[len(sends)],
            recv_sem=recv_sem.at[slot * chunks + k],
            device_id=target,
            device_id_type=MESH,
        )
        copy.start()
        sends.append(copy)

    def arrive(slot, k):
        view = part(out_ref.at[slot], k)
        pltpu.make_async_remote_copy(
            src_ref=view,
            dst_ref=view,
            send_sem=send_sem.at[0],
            recv_sem=recv_sem.at[slot * chunks + k],
            device_id=pair_id,
            device_id_type=MESH,
        ).wait_recv()

    for k in range(chunks):
        send(blk_ref, mine, k, fwd_id)
        send(blk_ref, mine, k, bwd_id)
    for k in range(chunks):
        send(blk_ref, mine, k, pair_id)
    fwd_hops = z_count // 2
    bwd_hops = z_count - 1 - fwd_hops
    for hop in range(1, fwd_hops + 1):
        for k in range(chunks):
            slot = c * z_count + lax.rem(z - step * hop + 2 * z_count, z_count)
            arrive(slot, k)
            if hop < fwd_hops:
                send(out_ref.at[slot], slot, k, fwd_id)
            send(out_ref.at[slot], slot, k, pair_id)
            if hop <= bwd_hops:
                slot = c * z_count + lax.rem(z + step * hop + 2 * z_count, z_count)
                arrive(slot, k)
                if hop < bwd_hops:
                    send(out_ref.at[slot], slot, k, bwd_id)
                send(out_ref.at[slot], slot, k, pair_id)
    for zz in range(z_count):
        for k in range(chunks):
            arrive(other * z_count + zz, k)
    local.wait()
    for copy in sends:
        copy.wait_send()


def gather_blocks(block, z_count, chunks):
    count = 2 * z_count
    return pl.pallas_call(
        functools.partial(dispatch_kernel, z_count, chunks),
        out_shape=jax.ShapeDtypeStruct((count,) + block.shape, block.dtype),
        in_specs=[pl.BlockSpec(memory_space=pltpu.VMEM)],
        out_specs=pl.BlockSpec(memory_space=pltpu.VMEM),
        scratch_shapes=[
            pltpu.SemaphoreType.DMA((2 * count * chunks,)),
            pltpu.SemaphoreType.DMA((count * chunks,)),
            pltpu.SemaphoreType.DMA((1,)),
        ],
        compiler_params=pltpu.CompilerParams(
            collective_id=0, has_side_effects=True, vmem_limit_bytes=32 * 1024 * 1024
        ),
    )(block)


def combine_kernel(
    z_count, dp_count, seq_len, chunks, part_ref, head_ref, out_ref, pair_out, pair_buf,
    fwd_buf, bwd_buf, fwd_out, bwd_out, seq_out, seq_in, send_sem, recv_sem, seq_sem,
):
    z = lax.axis_index("z")
    c = lax.axis_index("c")
    row = lax.axis_index("dp")
    other = 1 - c
    step = 1 - 2 * c
    fwd = lax.rem(z + step + z_count, z_count)
    bwd = lax.rem(z - step + z_count, z_count)
    fwd_id, bwd_id, pair_id = (row, fwd, c), (row, bwd, c), (row, z, other)
    mate_id = (lax.rem(row + dp_count // 2, dp_count), z, c)
    fwd_hops = z_count // 2
    bwd_hops = z_count - 1 - fwd_hops
    piece = part_ref.shape[2] // chunks

    barrier = pltpu.get_barrier_semaphore()
    for target in (fwd_id, bwd_id, pair_id, mate_id):
        pl.semaphore_signal(barrier, 1, device_id=target, device_id_type=MESH)
    pl.semaphore_wait(barrier, 4)

    sends = []

    def send(src, dst, sem, target):
        copy = pltpu.make_async_remote_copy(
            src_ref=src,
            dst_ref=dst,
            send_sem=send_sem.at[len(sends)],
            recv_sem=recv_sem.at[sem],
            device_id=target,
            device_id_type=MESH,
        )
        copy.start()
        sends.append(copy)

    def arrive(dst, sem):
        pltpu.make_async_remote_copy(
            src_ref=dst,
            dst_ref=dst,
            send_sem=send_sem.at[0],
            recv_sem=recv_sem.at[sem],
            device_id=pair_id,
            device_id_type=MESH,
        ).wait_recv()

    def order(ring_step):
        dests = []
        for hop in range(1, fwd_hops + 1):
            dests.append(lax.rem(z + ring_step * (fwd_hops + 1 - hop) + 2 * z_count, z_count))
            if hop <= bwd_hops:
                dests.append(lax.rem(z - ring_step * (bwd_hops + 1 - hop) + 2 * z_count, z_count))
        return dests + [z]

    for n, dest in enumerate(order(-step)):
        send(part_ref.at[other, dest], pair_buf.at[n], n, pair_id)
    def own(dest, n, k):
        if k == 0:
            arrive(pair_buf.at[n], n)
        rows = pl.ds(k * piece, piece)
        return part_ref[c, dest, rows].astype(jnp.float32) + pair_buf[n, rows].astype(
            jnp.float32
        )

    fwd_sem = z_count
    bwd_sem = z_count + fwd_hops * chunks
    for hop in range(1, fwd_hops + 1):
        for k in range(chunks):
            rows = pl.ds(k * piece, piece)
            dest = lax.rem(z + step * (fwd_hops + 1 - hop) + 2 * z_count, z_count)
            n = hop - 1 + min(hop - 1, bwd_hops)
            total = own(dest, n, k)
            if hop > 1:
                sem = fwd_sem + (hop - 2) * chunks + k
                arrive(fwd_buf.at[hop - 2, rows], sem)
                total = total + fwd_buf[hop - 2, rows].astype(jnp.float32)
            fwd_out[hop - 1, rows] = total.astype(fwd_out.dtype)
            sem = fwd_sem + (hop - 1) * chunks + k
            send(fwd_out.at[hop - 1, rows], fwd_buf.at[hop - 1, rows], sem, fwd_id)
            if hop <= bwd_hops:
                dest = lax.rem(z - step * (bwd_hops + 1 - hop) + 2 * z_count, z_count)
                total = own(dest, n + 1, k)
                if hop > 1:
                    sem = bwd_sem + (hop - 2) * chunks + k
                    arrive(bwd_buf.at[hop - 2, rows], sem)
                    total = total + bwd_buf[hop - 2, rows].astype(jnp.float32)
                bwd_out[hop - 1, rows] = total.astype(bwd_out.dtype)
                sem = bwd_sem + (hop - 1) * chunks + k
                send(bwd_out.at[hop - 1, rows], bwd_buf.at[hop - 1, rows], sem, bwd_id)
    for k in range(chunks):
        rows = pl.ds(k * piece, piece)
        total = own(z, fwd_hops + bwd_hops, k)
        arrive(fwd_buf.at[fwd_hops - 1, rows], fwd_sem + (fwd_hops - 1) * chunks + k)
        total = total + fwd_buf[fwd_hops - 1, rows].astype(jnp.float32)
        if bwd_hops > 0:
            arrive(bwd_buf.at[bwd_hops - 1, rows], bwd_sem + (bwd_hops - 1) * chunks + k)
            total = total + bwd_buf[bwd_hops - 1, rows].astype(jnp.float32)
        out_ref[rows] = total.astype(out_ref.dtype)
    tok_rows, width = out_ref.shape
    seqs = tok_rows // seq_len
    scored = out_ref[...].astype(jnp.float32) * head_ref[...]
    per_seq = jnp.sum(scored.reshape(seqs, seq_len, width), axis=1)
    seq_score = jnp.sum(per_seq, axis=1, keepdims=True)
    seq_out[...] = jnp.zeros(seq_out.shape, jnp.float32)
    seq_out[pl.ds(0, seqs)] = jnp.broadcast_to(seq_score, (seqs, seq_out.shape[1]))
    mate = pltpu.make_async_remote_copy(
        src_ref=seq_out,
        dst_ref=seq_in,
        send_sem=seq_sem.at[0],
        recv_sem=seq_sem.at[1],
        device_id=mate_id,
        device_id_type=MESH,
    )
    mate.start()
    mate.wait()
    mine = seq_out[...]
    theirs = seq_in[...]
    pair_out[...] = jnp.abs(mine - theirs) + 0.5 * (mine + theirs)
    for copy in sends:
        copy.wait_send()


def scatter_sums(partial, score_head, dp_count, seq_len, chunks):
    c_count, z_count, rows, width = partial.shape
    fwd_hops = z_count // 2
    bwd_hops = max(z_count - 1 - fwd_hops, 1)
    block = (rows, width)
    vmem = pl.BlockSpec(memory_space=pltpu.VMEM)
    sems = z_count + (fwd_hops + bwd_hops) * chunks
    tile = (8, 128)
    return pl.pallas_call(
        functools.partial(combine_kernel, z_count, dp_count, seq_len, chunks),
        out_shape=(
            jax.ShapeDtypeStruct(block, partial.dtype),
            jax.ShapeDtypeStruct(tile, jnp.float32),
        ),
        in_specs=[vmem, vmem],
        out_specs=(vmem, vmem),
        scratch_shapes=[
            pltpu.VMEM((z_count,) + block, partial.dtype),
            pltpu.VMEM((fwd_hops,) + block, partial.dtype),
            pltpu.VMEM((bwd_hops,) + block, partial.dtype),
            pltpu.VMEM((fwd_hops,) + block, partial.dtype),
            pltpu.VMEM((bwd_hops,) + block, partial.dtype),
            pltpu.VMEM(tile, jnp.float32),
            pltpu.VMEM(tile, jnp.float32),
            pltpu.SemaphoreType.DMA((sems,)),
            pltpu.SemaphoreType.DMA((sems,)),
            pltpu.SemaphoreType.DMA((2,)),
        ],
        compiler_params=pltpu.CompilerParams(
            collective_id=1, has_side_effects=True, vmem_limit_bytes=48 * 1024 * 1024
        ),
    )(partial, score_head.reshape(1, -1))


def body(
    tokens, expert_ids, gate_fixed, scorer_id, direction_tags, w_gate, w_up, w_down, score_head
):
    z_count = lax.axis_size("z")
    c_count = lax.axis_size("c")
    expert_count = z_count * c_count
    per_device = w_gate.shape[0]
    tok_rows, model_width = tokens.shape
    top_count = expert_ids.shape[1]
    which_tag = jnp.repeat(scorer_id, SEQ_LEN)[:, None]
    tag_rows = jnp.where(
        which_tag == 1, direction_tags[1][None, :], direction_tags[0][None, :]
    ).astype(jnp.float32)
    inputs = (tokens.astype(jnp.float32) + tag_rows).astype(jnp.bfloat16)
    rank_in = route_ranks(expert_ids, per_device * expert_count)
    routes = jnp.concatenate(
        [expert_ids, rank_in, gate_fixed // 256, gate_fixed % 256], axis=1
    ).astype(jnp.bfloat16)
    routes = jnp.pad(routes, ((0, 0), (0, 128 - 4 * top_count)))
    block = jnp.concatenate([inputs, routes], axis=1)
    gathered = gather_blocks(block, z_count, 2)
    inputs_all = gathered[:, :, :model_width]
    routes_all = gathered[:, :, model_width : model_width + 4 * top_count].astype(jnp.int32)
    ids_cube = routes_all[..., :top_count]
    rank_cube = routes_all[..., top_count : 2 * top_count]
    fixed_val = (
        routes_all[..., 2 * top_count : 3 * top_count] * 256 + routes_all[..., 3 * top_count :]
    ).astype(jnp.float32)
    weight_cube = fixed_val / jnp.sum(fixed_val, axis=2, keepdims=True)
    my_index = lax.axis_index("z") * c_count + lax.axis_index("c")
    local_count = per_device * MOST
    local_slot = ids_cube - my_index * per_device
    is_mine = (local_slot >= 0) & (local_slot < per_device)
    local_key = jnp.where(is_mine, local_slot * MOST + rank_cube, -1)
    match = (
        local_key[:, None, :, :] == jnp.arange(local_count, dtype=jnp.int32)[None, :, None, None]
    )
    picker = jnp.any(match, axis=3).astype(jnp.bfloat16)
    slot_weight = jnp.sum(jnp.where(match, weight_cube[:, None, :, :], 0.0), axis=(2, 3))
    picker = picker.reshape(expert_count, per_device, MOST, tok_rows).transpose(1, 0, 2, 3)
    slot_weight = slot_weight.reshape(expert_count, per_device, MOST).transpose(1, 0, 2)
    token_of = jnp.argmax(picker, axis=3)
    source_of = jnp.arange(expert_count, dtype=jnp.int32)[None, :, None]
    row_block = inputs_all[source_of, token_of]
    gate_proj = jnp.einsum("esmd,edf->esmf", row_block, w_gate, preferred_element_type=jnp.float32)
    up_proj = jnp.einsum("esmd,edf->esmf", row_block, w_up, preferred_element_type=jnp.float32)
    hidden = (jax.nn.silu(gate_proj) * up_proj).astype(jnp.bfloat16)
    down_out = jnp.einsum("esmf,efd->esmd", hidden, w_down, preferred_element_type=jnp.float32)
    result = (slot_weight[..., None] * down_out).astype(jnp.bfloat16)
    result = lax.optimization_barrier(result)
    partial_value = jnp.einsum(
        "esmt,esmd->std", picker, result, preferred_element_type=jnp.float32
    )
    partial_value = partial_value.reshape(c_count, z_count, tok_rows, model_width)
    mixed, pair_tile = scatter_sums(
        partial_value.astype(jnp.bfloat16), score_head, lax.axis_size("dp"), SEQ_LEN, 2
    )
    pair_score = pair_tile[: tok_rows // SEQ_LEN, 0]
    return (mixed, pair_score)


def solution(mesh):
    dp_count, expert_count = mesh.devices.shape
    split = Mesh(mesh.devices.reshape(dp_count, expert_count // 2, 2), ("dp", "z", "c"))
    rows = P(("dp", "z", "c"), None)
    return jax.shard_map(
        body,
        mesh=split,
        in_specs=(
            rows,
            rows,
            rows,
            P(("dp", "z", "c")),
            P(),
            P(("z", "c"), None, None),
            P(("z", "c"), None, None),
            P(("z", "c"), None, None),
            P(),
        ),
        out_specs=(rows, P(("dp", "z", "c"))),
        check_vma=False,
    )
```

```python
import functools

import jax
import jax.numpy as jnp
from jax import lax
from jax.experimental import pallas as pl
from jax.experimental.pallas import tpu as pltpu
from jax.sharding import Mesh
from jax.sharding import PartitionSpec as P

SEQ_LEN = 16
MOST = 24


def from_partner(block, axis, bit):
    count = lax.axis_size(axis)
    route = []
    for low in range(count):
        high = low | 1 << bit
        if high != low and high < count:
            route += [(low, high), (high, low)]
    return lax.ppermute(block, axis, route)


def route_ranks(expert_ids, expert_total):
    flat_ids = expert_ids.reshape(-1)
    entry_count = flat_ids.shape[0]
    onehot = flat_ids[:, None] == jnp.arange(expert_total, dtype=jnp.int32)[None, :]
    positions = jnp.arange(entry_count, dtype=jnp.int32)
    earlier = (positions[:, None] > positions[None, :]).astype(jnp.bfloat16)
    counts = jnp.dot(earlier, onehot.astype(jnp.bfloat16), preferred_element_type=jnp.float32)
    rank_in = jnp.sum(jnp.where(onehot, counts, 0.0), axis=1).astype(jnp.int32)
    return rank_in.reshape(expert_ids.shape)


MESH = pl.DeviceIdType.MESH


def dispatch_kernel(z_count, chunks, blk_ref, out_ref, send_sem, recv_sem, local_sem):
    z = lax.axis_index("z")
    c = lax.axis_index("c")
    row = lax.axis_index("dp")
    other = 1 - c
    step = 1 - 2 * c
    fwd = lax.rem(z + step + z_count, z_count)
    bwd = lax.rem(z - step + z_count, z_count)
    fwd_id, bwd_id, pair_id = (row, fwd, c), (row, bwd, c), (row, z, other)
    piece = blk_ref.shape[0] // chunks

    barrier = pltpu.get_barrier_semaphore()
    for target in (fwd_id, bwd_id, pair_id):
        pl.semaphore_signal(barrier, 1, device_id=target, device_id_type=MESH)
    pl.semaphore_wait(barrier, 3)

    mine = c * z_count + z
    local = pltpu.make_async_copy(blk_ref, out_ref.at[mine], local_sem.at[0])
    local.start()
    sends = []

    def part(ref, k):
        return ref.at[pl.ds(k * piece, piece)]

    def send(src, slot, k, target):
        copy = pltpu.make_async_remote_copy(
            src_ref=part(src, k),
            dst_ref=part(out_ref.at[slot], k),
            send_sem=send_sem.at[len(sends)],
            recv_sem=recv_sem.at[slot * chunks + k],
            device_id=target,
            device_id_type=MESH,
        )
        copy.start()
        sends.append(copy)

    def arrive(slot, k):
        view = part(out_ref.at[slot], k)
        pltpu.make_async_remote_copy(
            src_ref=view,
            dst_ref=view,
            send_sem=send_sem.at[0],
            recv_sem=recv_sem.at[slot * chunks + k],
            device_id=pair_id,
            device_id_type=MESH,
        ).wait_recv()

    for k in range(chunks):
        send(blk_ref, mine, k, fwd_id)
        send(blk_ref, mine, k, bwd_id)
    for k in range(chunks):
        send(blk_ref, mine, k, pair_id)
    fwd_hops = z_count // 2
    bwd_hops = z_count - 1 - fwd_hops
    for hop in range(1, fwd_hops + 1):
        for k in range(chunks):
            slot = c * z_count + lax.rem(z - step * hop + 2 * z_count, z_count)
            arrive(slot, k)
            if hop < fwd_hops:
                send(out_ref.at[slot], slot, k, fwd_id)
            send(out_ref.at[slot], slot, k, pair_id)
            if hop <= bwd_hops:
                slot = c * z_count + lax.rem(z + step * hop + 2 * z_count, z_count)
                arrive(slot, k)
                if hop < bwd_hops:
                    send(out_ref.at[slot], slot, k, bwd_id)
                send(out_ref.at[slot], slot, k, pair_id)
    for zz in range(z_count):
        for k in range(chunks):
            arrive(other * z_count + zz, k)
    local.wait()
    for copy in sends:
        copy.wait_send()


def gather_blocks(block, z_count, chunks):
    count = 2 * z_count
    return pl.pallas_call(
        functools.partial(dispatch_kernel, z_count, chunks),
        out_shape=jax.ShapeDtypeStruct((count,) + block.shape, block.dtype),
        in_specs=[pl.BlockSpec(memory_space=pltpu.VMEM)],
        out_specs=pl.BlockSpec(memory_space=pltpu.VMEM),
        scratch_shapes=[
            pltpu.SemaphoreType.DMA((2 * count * chunks,)),
            pltpu.SemaphoreType.DMA((count * chunks,)),
            pltpu.SemaphoreType.DMA((1,)),
        ],
        compiler_params=pltpu.CompilerParams(
            collective_id=0, has_side_effects=True, vmem_limit_bytes=32 * 1024 * 1024
        ),
    )(block)


def combine_kernel(
    z_count, chunks, part_ref, out_ref, pair_buf, fwd_buf, bwd_buf, fwd_out, bwd_out,
    send_sem, recv_sem,
):
    z = lax.axis_index("z")
    c = lax.axis_index("c")
    row = lax.axis_index("dp")
    other = 1 - c
    step = 1 - 2 * c
    fwd = lax.rem(z + step + z_count, z_count)
    bwd = lax.rem(z - step + z_count, z_count)
    fwd_id, bwd_id, pair_id = (row, fwd, c), (row, bwd, c), (row, z, other)
    fwd_hops = z_count // 2
    bwd_hops = z_count - 1 - fwd_hops
    piece = part_ref.shape[2] // chunks

    barrier = pltpu.get_barrier_semaphore()
    for target in (fwd_id, bwd_id, pair_id):
        pl.semaphore_signal(barrier, 1, device_id=target, device_id_type=MESH)
    pl.semaphore_wait(barrier, 3)

    sends = []

    def send(src, dst, sem, target):
        copy = pltpu.make_async_remote_copy(
            src_ref=src,
            dst_ref=dst,
            send_sem=send_sem.at[len(sends)],
            recv_sem=recv_sem.at[sem],
            device_id=target,
            device_id_type=MESH,
        )
        copy.start()
        sends.append(copy)

    def arrive(dst, sem):
        pltpu.make_async_remote_copy(
            src_ref=dst,
            dst_ref=dst,
            send_sem=send_sem.at[0],
            recv_sem=recv_sem.at[sem],
            device_id=pair_id,
            device_id_type=MESH,
        ).wait_recv()

    def order(ring_step):
        dests = []
        for hop in range(1, fwd_hops + 1):
            dests.append(lax.rem(z + ring_step * (fwd_hops + 1 - hop) + 2 * z_count, z_count))
            if hop <= bwd_hops:
                dests.append(lax.rem(z - ring_step * (bwd_hops + 1 - hop) + 2 * z_count, z_count))
        return dests + [z]

    for n, dest in enumerate(order(-step)):
        send(part_ref.at[other, dest], pair_buf.at[n], n, pair_id)
    def own(dest, n, k):
        if k == 0:
            arrive(pair_buf.at[n], n)
        rows = pl.ds(k * piece, piece)
        return part_ref[c, dest, rows].astype(jnp.float32) + pair_buf[n, rows].astype(
            jnp.float32
        )

    fwd_sem = z_count
    bwd_sem = z_count + fwd_hops * chunks
    for hop in range(1, fwd_hops + 1):
        for k in range(chunks):
            rows = pl.ds(k * piece, piece)
            dest = lax.rem(z + step * (fwd_hops + 1 - hop) + 2 * z_count, z_count)
            n = hop - 1 + min(hop - 1, bwd_hops)
            total = own(dest, n, k)
            if hop > 1:
                sem = fwd_sem + (hop - 2) * chunks + k
                arrive(fwd_buf.at[hop - 2, rows], sem)
                total = total + fwd_buf[hop - 2, rows].astype(jnp.float32)
            fwd_out[hop - 1, rows] = total.astype(fwd_out.dtype)
            sem = fwd_sem + (hop - 1) * chunks + k
            send(fwd_out.at[hop - 1, rows], fwd_buf.at[hop - 1, rows], sem, fwd_id)
            if hop <= bwd_hops:
                dest = lax.rem(z - step * (bwd_hops + 1 - hop) + 2 * z_count, z_count)
                total = own(dest, n + 1, k)
                if hop > 1:
                    sem = bwd_sem + (hop - 2) * chunks + k
                    arrive(bwd_buf.at[hop - 2, rows], sem)
                    total = total + bwd_buf[hop - 2, rows].astype(jnp.float32)
                bwd_out[hop - 1, rows] = total.astype(bwd_out.dtype)
                sem = bwd_sem + (hop - 1) * chunks + k
                send(bwd_out.at[hop - 1, rows], bwd_buf.at[hop - 1, rows], sem, bwd_id)
    for k in range(chunks):
        rows = pl.ds(k * piece, piece)
        total = own(z, fwd_hops + bwd_hops, k)
        arrive(fwd_buf.at[fwd_hops - 1, rows], fwd_sem + (fwd_hops - 1) * chunks + k)
        total = total + fwd_buf[fwd_hops - 1, rows].astype(jnp.float32)
        if bwd_hops > 0:
            arrive(bwd_buf.at[bwd_hops - 1, rows], bwd_sem + (bwd_hops - 1) * chunks + k)
            total = total + bwd_buf[bwd_hops - 1, rows].astype(jnp.float32)
        out_ref[rows] = total.astype(out_ref.dtype)
    for copy in sends:
        copy.wait_send()


def score_kernel(dp_count, seq_len, mixed_ref, head_ref, pair_out, seq_out, seq_in, seq_sem):
    z = lax.axis_index("z")
    c = lax.axis_index("c")
    row = lax.axis_index("dp")
    mate_id = (lax.rem(row + dp_count // 2, dp_count), z, c)
    barrier = pltpu.get_barrier_semaphore()
    pl.semaphore_signal(barrier, 1, device_id=mate_id, device_id_type=MESH)
    pl.semaphore_wait(barrier, 1)
    tok_rows, width = mixed_ref.shape
    seqs = tok_rows // seq_len
    scored = mixed_ref[...].astype(jnp.float32) * head_ref[...]
    per_seq = jnp.sum(scored.reshape(seqs, seq_len, width), axis=1)
    seq_score = jnp.sum(per_seq, axis=1, keepdims=True)
    seq_out[...] = jnp.zeros(seq_out.shape, jnp.float32)
    seq_out[pl.ds(0, seqs)] = jnp.broadcast_to(seq_score, (seqs, seq_out.shape[1]))
    mate = pltpu.make_async_remote_copy(
        src_ref=seq_out,
        dst_ref=seq_in,
        send_sem=seq_sem.at[0],
        recv_sem=seq_sem.at[1],
        device_id=mate_id,
        device_id_type=MESH,
    )
    mate.start()
    mate.wait()
    mine = seq_out[...]
    theirs = seq_in[...]
    pair_out[...] = jnp.abs(mine - theirs) + 0.5 * (mine + theirs)


def scatter_sums(partial, score_head, dp_count, seq_len, chunks):
    c_count, z_count, rows, width = partial.shape
    fwd_hops = z_count // 2
    bwd_hops = max(z_count - 1 - fwd_hops, 1)
    block = (rows, width)
    vmem = pl.BlockSpec(memory_space=pltpu.VMEM)
    sems = z_count + (fwd_hops + bwd_hops) * chunks
    tile = (8, 128)
    mixed = pl.pallas_call(
        functools.partial(combine_kernel, z_count, chunks),
        out_shape=jax.ShapeDtypeStruct(block, partial.dtype),
        in_specs=[vmem],
        out_specs=vmem,
        scratch_shapes=[
            pltpu.VMEM((z_count,) + block, partial.dtype),
            pltpu.VMEM((fwd_hops,) + block, partial.dtype),
            pltpu.VMEM((bwd_hops,) + block, partial.dtype),
            pltpu.VMEM((fwd_hops,) + block, partial.dtype),
            pltpu.VMEM((bwd_hops,) + block, partial.dtype),
            pltpu.SemaphoreType.DMA((sems,)),
            pltpu.SemaphoreType.DMA((sems,)),
        ],
        compiler_params=pltpu.CompilerParams(
            collective_id=1, has_side_effects=True, vmem_limit_bytes=48 * 1024 * 1024
        ),
    )(partial)
    pair_tile = pl.pallas_call(
        functools.partial(score_kernel, dp_count, seq_len),
        out_shape=jax.ShapeDtypeStruct(tile, jnp.float32),
        in_specs=[vmem, vmem],
        out_specs=vmem,
        scratch_shapes=[
            pltpu.VMEM(tile, jnp.float32),
            pltpu.VMEM(tile, jnp.float32),
            pltpu.SemaphoreType.DMA((2,)),
        ],
        compiler_params=pltpu.CompilerParams(collective_id=2, has_side_effects=True),
    )(mixed, score_head.reshape(1, -1))
    return mixed, pair_tile


def body(
    tokens, expert_ids, gate_fixed, scorer_id, direction_tags, w_gate, w_up, w_down, score_head
):
    z_count = lax.axis_size("z")
    c_count = lax.axis_size("c")
    expert_count = z_count * c_count
    per_device = w_gate.shape[0]
    tok_rows, model_width = tokens.shape
    top_count = expert_ids.shape[1]
    which_tag = jnp.repeat(scorer_id, SEQ_LEN)[:, None]
    tag_rows = jnp.where(
        which_tag == 1, direction_tags[1][None, :], direction_tags[0][None, :]
    ).astype(jnp.float32)
    inputs = (tokens.astype(jnp.float32) + tag_rows).astype(jnp.bfloat16)
    rank_in = route_ranks(expert_ids, per_device * expert_count)
    routes = jnp.concatenate(
        [expert_ids, rank_in, gate_fixed // 256, gate_fixed % 256], axis=1
    ).astype(jnp.bfloat16)
    routes = jnp.pad(routes, ((0, 0), (0, 128 - 4 * top_count)))
    block = jnp.concatenate([inputs, routes], axis=1)
    gathered = gather_blocks(block, z_count, 2)
    inputs_all = gathered[:, :, :model_width]
    routes_all = gathered[:, :, model_width : model_width + 4 * top_count].astype(jnp.int32)
    ids_cube = routes_all[..., :top_count]
    rank_cube = routes_all[..., top_count : 2 * top_count]
    fixed_val = (
        routes_all[..., 2 * top_count : 3 * top_count] * 256 + routes_all[..., 3 * top_count :]
    ).astype(jnp.float32)
    weight_cube = fixed_val / jnp.sum(fixed_val, axis=2, keepdims=True)
    my_index = lax.axis_index("z") * c_count + lax.axis_index("c")
    local_count = per_device * MOST
    local_slot = ids_cube - my_index * per_device
    is_mine = (local_slot >= 0) & (local_slot < per_device)
    local_key = jnp.where(is_mine, local_slot * MOST + rank_cube, -1)
    match = (
        local_key[:, None, :, :] == jnp.arange(local_count, dtype=jnp.int32)[None, :, None, None]
    )
    picker = jnp.any(match, axis=3).astype(jnp.bfloat16)
    slot_weight = jnp.sum(jnp.where(match, weight_cube[:, None, :, :], 0.0), axis=(2, 3))
    picker = picker.reshape(expert_count, per_device, MOST, tok_rows).transpose(1, 0, 2, 3)
    slot_weight = slot_weight.reshape(expert_count, per_device, MOST).transpose(1, 0, 2)
    row_block = jnp.einsum(
        "esmt,std->esmd", picker, inputs_all, preferred_element_type=jnp.float32
    ).astype(jnp.bfloat16)
    gate_proj = jnp.einsum("esmd,edf->esmf", row_block, w_gate, preferred_element_type=jnp.float32)
    up_proj = jnp.einsum("esmd,edf->esmf", row_block, w_up, preferred_element_type=jnp.float32)
    hidden = (jax.nn.silu(gate_proj) * up_proj).astype(jnp.bfloat16)
    down_out = jnp.einsum("esmf,efd->esmd", hidden, w_down, preferred_element_type=jnp.float32)
    result = (slot_weight[..., None] * down_out).astype(jnp.bfloat16)
    result = lax.optimization_barrier(result)
    partial_value = jnp.einsum(
        "esmt,esmd->std", picker, result, preferred_element_type=jnp.float32
    )
    partial_value = partial_value.reshape(c_count, z_count, tok_rows, model_width)
    mixed, pair_tile = scatter_sums(
        partial_value.astype(jnp.bfloat16), score_head, lax.axis_size("dp"), SEQ_LEN, 2
    )
    pair_score = pair_tile[: tok_rows // SEQ_LEN, 0]
    return (mixed, pair_score)


def solution(mesh):
    dp_count, expert_count = mesh.devices.shape
    split = Mesh(mesh.devices.reshape(dp_count, expert_count // 2, 2), ("dp", "z", "c"))
    rows = P(("dp", "z", "c"), None)
    return jax.shard_map(
        body,
        mesh=split,
        in_specs=(
            rows,
            rows,
            rows,
            P(("dp", "z", "c")),
            P(),
            P(("z", "c"), None, None),
            P(("z", "c"), None, None),
            P(("z", "c"), None, None),
            P(),
        ),
        out_specs=(rows, P(("dp", "z", "c"))),
        check_vma=False,
    )
```

```python
import functools

import jax
import jax.numpy as jnp
from jax import lax
from jax.experimental import pallas as pl
from jax.experimental.pallas import tpu as pltpu
from jax.sharding import Mesh
from jax.sharding import PartitionSpec as P

SEQ_LEN = 16
MOST = 24


def from_partner(block, axis, bit):
    count = lax.axis_size(axis)
    route = []
    for low in range(count):
        high = low | 1 << bit
        if high != low and high < count:
            route += [(low, high), (high, low)]
    return lax.ppermute(block, axis, route)


def route_ranks(expert_ids, expert_total):
    flat_ids = expert_ids.reshape(-1)
    entry_count = flat_ids.shape[0]
    onehot = flat_ids[:, None] == jnp.arange(expert_total, dtype=jnp.int32)[None, :]
    positions = jnp.arange(entry_count, dtype=jnp.int32)
    earlier = (positions[:, None] > positions[None, :]).astype(jnp.bfloat16)
    counts = jnp.dot(earlier, onehot.astype(jnp.bfloat16), preferred_element_type=jnp.float32)
    rank_in = jnp.sum(jnp.where(onehot, counts, 0.0), axis=1).astype(jnp.int32)
    return rank_in.reshape(expert_ids.shape)


MESH = pl.DeviceIdType.MESH


def dispatch_kernel(z_count, chunks, blk_ref, out_ref, send_sem, recv_sem, local_sem):
    z = lax.axis_index("z")
    c = lax.axis_index("c")
    row = lax.axis_index("dp")
    other = 1 - c
    step = 1 - 2 * c
    fwd = lax.rem(z + step + z_count, z_count)
    bwd = lax.rem(z - step + z_count, z_count)
    fwd_id, bwd_id, pair_id = (row, fwd, c), (row, bwd, c), (row, z, other)
    piece = blk_ref.shape[0] // chunks

    barrier = pltpu.get_barrier_semaphore()
    for target in (fwd_id, bwd_id, pair_id):
        pl.semaphore_signal(barrier, 1, device_id=target, device_id_type=MESH)
    pl.semaphore_wait(barrier, 3)

    mine = c * z_count + z
    local = pltpu.make_async_copy(blk_ref, out_ref.at[mine], local_sem.at[0])
    local.start()
    sends = []

    def part(ref, k):
        return ref.at[pl.ds(k * piece, piece)]

    def send(src, slot, k, target):
        copy = pltpu.make_async_remote_copy(
            src_ref=part(src, k),
            dst_ref=part(out_ref.at[slot], k),
            send_sem=send_sem.at[len(sends)],
            recv_sem=recv_sem.at[slot * chunks + k],
            device_id=target,
            device_id_type=MESH,
        )
        copy.start()
        sends.append(copy)

    def arrive(slot, k):
        view = part(out_ref.at[slot], k)
        pltpu.make_async_remote_copy(
            src_ref=view,
            dst_ref=view,
            send_sem=send_sem.at[0],
            recv_sem=recv_sem.at[slot * chunks + k],
            device_id=pair_id,
            device_id_type=MESH,
        ).wait_recv()

    for k in range(chunks):
        send(blk_ref, mine, k, fwd_id)
        send(blk_ref, mine, k, bwd_id)
    for k in range(chunks):
        send(blk_ref, mine, k, pair_id)
    fwd_hops = z_count // 2
    bwd_hops = z_count - 1 - fwd_hops
    for hop in range(1, fwd_hops + 1):
        for k in range(chunks):
            slot = c * z_count + lax.rem(z - step * hop + 2 * z_count, z_count)
            arrive(slot, k)
            if hop < fwd_hops:
                send(out_ref.at[slot], slot, k, fwd_id)
            send(out_ref.at[slot], slot, k, pair_id)
            if hop <= bwd_hops:
                slot = c * z_count + lax.rem(z + step * hop + 2 * z_count, z_count)
                arrive(slot, k)
                if hop < bwd_hops:
                    send(out_ref.at[slot], slot, k, bwd_id)
                send(out_ref.at[slot], slot, k, pair_id)
    for zz in range(z_count):
        for k in range(chunks):
            arrive(other * z_count + zz, k)
    local.wait()
    for copy in sends:
        copy.wait_send()


def gather_blocks(block, z_count, chunks):
    count = 2 * z_count
    return pl.pallas_call(
        functools.partial(dispatch_kernel, z_count, chunks),
        out_shape=jax.ShapeDtypeStruct((count,) + block.shape, block.dtype),
        in_specs=[pl.BlockSpec(memory_space=pltpu.VMEM)],
        out_specs=pl.BlockSpec(memory_space=pltpu.VMEM),
        scratch_shapes=[
            pltpu.SemaphoreType.DMA((2 * count * chunks,)),
            pltpu.SemaphoreType.DMA((count * chunks,)),
            pltpu.SemaphoreType.DMA((1,)),
        ],
        compiler_params=pltpu.CompilerParams(
            collective_id=0, has_side_effects=True, vmem_limit_bytes=32 * 1024 * 1024
        ),
    )(block)


def combine_kernel(
    z_count, dp_count, seq_len, chunks, part_ref, head_ref, out_ref, pair_out, pair_buf,
    fwd_buf, bwd_buf, fwd_out, bwd_out, seq_out, seq_in, send_sem, recv_sem, seq_sem,
):
    z = lax.axis_index("z")
    c = lax.axis_index("c")
    row = lax.axis_index("dp")
    other = 1 - c
    step = 1 - 2 * c
    fwd = lax.rem(z + step + z_count, z_count)
    bwd = lax.rem(z - step + z_count, z_count)
    fwd_id, bwd_id, pair_id = (row, fwd, c), (row, bwd, c), (row, z, other)
    mate_id = (lax.rem(row + dp_count // 2, dp_count), z, c)
    fwd_hops = z_count // 2
    bwd_hops = z_count - 1 - fwd_hops
    piece = part_ref.shape[2] // chunks

    barrier = pltpu.get_barrier_semaphore()
    for target in (fwd_id, bwd_id, pair_id, mate_id):
        pl.semaphore_signal(barrier, 1, device_id=target, device_id_type=MESH)
    pl.semaphore_wait(barrier, 4)

    sends = []

    def send(src, dst, sem, target):
        copy = pltpu.make_async_remote_copy(
            src_ref=src,
            dst_ref=dst,
            send_sem=send_sem.at[len(sends)],
            recv_sem=recv_sem.at[sem],
            device_id=target,
            device_id_type=MESH,
        )
        copy.start()
        sends.append(copy)

    def arrive(dst, sem):
        pltpu.make_async_remote_copy(
            src_ref=dst,
            dst_ref=dst,
            send_sem=send_sem.at[0],
            recv_sem=recv_sem.at[sem],
            device_id=pair_id,
            device_id_type=MESH,
        ).wait_recv()

    def order(ring_step):
        dests = []
        for hop in range(1, fwd_hops + 1):
            dests.append(lax.rem(z + ring_step * (fwd_hops + 1 - hop) + 2 * z_count, z_count))
            if hop <= bwd_hops:
                dests.append(lax.rem(z - ring_step * (bwd_hops + 1 - hop) + 2 * z_count, z_count))
        return dests + [z]

    for n, dest in enumerate(order(-step)):
        send(part_ref.at[other, dest], pair_buf.at[n], n, pair_id)
    def own(dest, n, k):
        if k == 0:
            arrive(pair_buf.at[n], n)
        rows = pl.ds(k * piece, piece)
        return part_ref[c, dest, rows].astype(jnp.float32) + pair_buf[n, rows].astype(
            jnp.float32
        )

    fwd_sem = z_count
    bwd_sem = z_count + fwd_hops * chunks
    for hop in range(1, fwd_hops + 1):
        for k in range(chunks):
            rows = pl.ds(k * piece, piece)
            dest = lax.rem(z + step * (fwd_hops + 1 - hop) + 2 * z_count, z_count)
            n = hop - 1 + min(hop - 1, bwd_hops)
            total = own(dest, n, k)
            if hop > 1:
                sem = fwd_sem + (hop - 2) * chunks + k
                arrive(fwd_buf.at[hop - 2, rows], sem)
                total = total + fwd_buf[hop - 2, rows].astype(jnp.float32)
            fwd_out[hop - 1, rows] = total.astype(fwd_out.dtype)
            sem = fwd_sem + (hop - 1) * chunks + k
            send(fwd_out.at[hop - 1, rows], fwd_buf.at[hop - 1, rows], sem, fwd_id)
            if hop <= bwd_hops:
                dest = lax.rem(z - step * (bwd_hops + 1 - hop) + 2 * z_count, z_count)
                total = own(dest, n + 1, k)
                if hop > 1:
                    sem = bwd_sem + (hop - 2) * chunks + k
                    arrive(bwd_buf.at[hop - 2, rows], sem)
                    total = total + bwd_buf[hop - 2, rows].astype(jnp.float32)
                bwd_out[hop - 1, rows] = total.astype(bwd_out.dtype)
                sem = bwd_sem + (hop - 1) * chunks + k
                send(bwd_out.at[hop - 1, rows], bwd_buf.at[hop - 1, rows], sem, bwd_id)
    for k in range(chunks):
        rows = pl.ds(k * piece, piece)
        total = own(z, fwd_hops + bwd_hops, k)
        arrive(fwd_buf.at[fwd_hops - 1, rows], fwd_sem + (fwd_hops - 1) * chunks + k)
        total = total + fwd_buf[fwd_hops - 1, rows].astype(jnp.float32)
        if bwd_hops > 0:
            arrive(bwd_buf.at[bwd_hops - 1, rows], bwd_sem + (bwd_hops - 1) * chunks + k)
            total = total + bwd_buf[bwd_hops - 1, rows].astype(jnp.float32)
        out_ref[rows] = total.astype(out_ref.dtype)
    tok_rows, width = out_ref.shape
    seqs = tok_rows // seq_len
    scored = out_ref[...].astype(jnp.float32) * head_ref[...]
    per_seq = jnp.sum(scored.reshape(seqs, seq_len, width), axis=1)
    seq_score = jnp.sum(per_seq, axis=1, keepdims=True)
    seq_out[...] = jnp.zeros(seq_out.shape, jnp.float32)
    seq_out[pl.ds(0, seqs)] = jnp.broadcast_to(seq_score, (seqs, seq_out.shape[1]))
    mate = pltpu.make_async_remote_copy(
        src_ref=seq_out,
        dst_ref=seq_in,
        send_sem=seq_sem.at[0],
        recv_sem=seq_sem.at[1],
        device_id=mate_id,
        device_id_type=MESH,
    )
    mate.start()
    mate.wait()
    mine = seq_out[...]
    theirs = seq_in[...]
    pair_out[...] = jnp.abs(mine - theirs) + 0.5 * (mine + theirs)
    for copy in sends:
        copy.wait_send()


def scatter_sums(partial, score_head, dp_count, seq_len, chunks):
    c_count, z_count, rows, width = partial.shape
    fwd_hops = z_count // 2
    bwd_hops = max(z_count - 1 - fwd_hops, 1)
    block = (rows, width)
    vmem = pl.BlockSpec(memory_space=pltpu.VMEM)
    sems = z_count + (fwd_hops + bwd_hops) * chunks
    tile = (8, 128)
    return pl.pallas_call(
        functools.partial(combine_kernel, z_count, dp_count, seq_len, chunks),
        out_shape=(
            jax.ShapeDtypeStruct(block, partial.dtype),
            jax.ShapeDtypeStruct(tile, jnp.float32),
        ),
        in_specs=[vmem, vmem],
        out_specs=(vmem, vmem),
        scratch_shapes=[
            pltpu.VMEM((z_count,) + block, partial.dtype),
            pltpu.VMEM((fwd_hops,) + block, partial.dtype),
            pltpu.VMEM((bwd_hops,) + block, partial.dtype),
            pltpu.VMEM((fwd_hops,) + block, partial.dtype),
            pltpu.VMEM((bwd_hops,) + block, partial.dtype),
            pltpu.VMEM(tile, jnp.float32),
            pltpu.VMEM(tile, jnp.float32),
            pltpu.SemaphoreType.DMA((sems,)),
            pltpu.SemaphoreType.DMA((sems,)),
            pltpu.SemaphoreType.DMA((2,)),
        ],
        compiler_params=pltpu.CompilerParams(
            collective_id=1, has_side_effects=True, vmem_limit_bytes=48 * 1024 * 1024
        ),
    )(partial, score_head.reshape(1, -1))


def body(
    tokens, expert_ids, gate_fixed, scorer_id, direction_tags, w_gate, w_up, w_down, score_head
):
    z_count = lax.axis_size("z")
    c_count = lax.axis_size("c")
    expert_count = z_count * c_count
    per_device = w_gate.shape[0]
    tok_rows, model_width = tokens.shape
    top_count = expert_ids.shape[1]
    which_tag = jnp.repeat(scorer_id, SEQ_LEN)[:, None]
    tag_rows = jnp.where(
        which_tag == 1, direction_tags[1][None, :], direction_tags[0][None, :]
    ).astype(jnp.float32)
    inputs = (tokens.astype(jnp.float32) + tag_rows).astype(jnp.bfloat16)
    rank_in = route_ranks(expert_ids, per_device * expert_count)
    routes = jnp.concatenate(
        [expert_ids, rank_in, gate_fixed // 256, gate_fixed % 256], axis=1
    ).astype(jnp.bfloat16)
    routes = jnp.pad(routes, ((0, 0), (0, 128 - 4 * top_count)))
    block = jnp.concatenate([inputs, routes], axis=1)
    gathered = gather_blocks(block, z_count, 2)
    inputs_all = gathered[:, :, :model_width]
    routes_all = gathered[:, :, model_width : model_width + 4 * top_count].astype(jnp.int32)
    ids_cube = routes_all[..., :top_count]
    rank_cube = routes_all[..., top_count : 2 * top_count]
    fixed_val = (
        routes_all[..., 2 * top_count : 3 * top_count] * 256 + routes_all[..., 3 * top_count :]
    ).astype(jnp.float32)
    weight_cube = fixed_val / jnp.sum(fixed_val, axis=2, keepdims=True)
    my_index = lax.axis_index("z") * c_count + lax.axis_index("c")
    local_count = per_device * MOST
    local_slot = ids_cube - my_index * per_device
    is_mine = (local_slot >= 0) & (local_slot < per_device)
    local_key = jnp.where(is_mine, local_slot * MOST + rank_cube, -1)
    match = (
        local_key[:, None, :, :] == jnp.arange(local_count, dtype=jnp.int32)[None, :, None, None]
    )
    picker = jnp.any(match, axis=3).astype(jnp.bfloat16)
    picker = picker.reshape(expert_count, per_device, MOST, tok_rows).transpose(1, 0, 2, 3)
    token_weight = jnp.stack(
        [jnp.sum(jnp.where(local_slot == e, weight_cube, 0.0), axis=2) for e in range(per_device)]
    )
    slot_weight = jnp.sum(picker.astype(jnp.float32) * token_weight[:, :, None, :], axis=3)
    row_block = jnp.einsum(
        "esmt,std->esmd", picker, inputs_all, preferred_element_type=jnp.float32
    ).astype(jnp.bfloat16)
    gate_proj = jnp.einsum("esmd,edf->esmf", row_block, w_gate, preferred_element_type=jnp.float32)
    up_proj = jnp.einsum("esmd,edf->esmf", row_block, w_up, preferred_element_type=jnp.float32)
    hidden = (jax.nn.silu(gate_proj) * up_proj).astype(jnp.bfloat16)
    down_out = jnp.einsum("esmf,efd->esmd", hidden, w_down, preferred_element_type=jnp.float32)
    result = (slot_weight[..., None] * down_out).astype(jnp.bfloat16)
    result = lax.optimization_barrier(result)
    partial_value = jnp.einsum(
        "esmt,esmd->std", picker, result, preferred_element_type=jnp.float32
    )
    partial_value = partial_value.reshape(c_count, z_count, tok_rows, model_width)
    mixed, pair_tile = scatter_sums(
        partial_value.astype(jnp.bfloat16), score_head, lax.axis_size("dp"), SEQ_LEN, 2
    )
    pair_score = pair_tile[: tok_rows // SEQ_LEN, 0]
    return (mixed, pair_score)


def solution(mesh):
    dp_count, expert_count = mesh.devices.shape
    split = Mesh(mesh.devices.reshape(dp_count, expert_count // 2, 2), ("dp", "z", "c"))
    rows = P(("dp", "z", "c"), None)
    return jax.shard_map(
        body,
        mesh=split,
        in_specs=(
            rows,
            rows,
            rows,
            P(("dp", "z", "c")),
            P(),
            P(("z", "c"), None, None),
            P(("z", "c"), None, None),
            P(("z", "c"), None, None),
            P(),
        ),
        out_specs=(rows, P(("dp", "z", "c"))),
        check_vma=False,
    )
```

```python
import functools

import jax
import jax.numpy as jnp
from jax import lax
from jax.experimental import pallas as pl
from jax.experimental.pallas import tpu as pltpu
from jax.sharding import Mesh
from jax.sharding import PartitionSpec as P

SEQ_LEN = 16
MOST = 24


def from_partner(block, axis, bit):
    count = lax.axis_size(axis)
    route = []
    for low in range(count):
        high = low | 1 << bit
        if high != low and high < count:
            route += [(low, high), (high, low)]
    return lax.ppermute(block, axis, route)


def route_ranks(expert_ids, expert_total):
    flat_ids = expert_ids.reshape(-1)
    entry_count = flat_ids.shape[0]
    onehot = flat_ids[:, None] == jnp.arange(expert_total, dtype=jnp.int32)[None, :]
    positions = jnp.arange(entry_count, dtype=jnp.int32)
    earlier = (positions[:, None] > positions[None, :]).astype(jnp.bfloat16)
    counts = jnp.dot(earlier, onehot.astype(jnp.bfloat16), preferred_element_type=jnp.float32)
    rank_in = jnp.sum(jnp.where(onehot, counts, 0.0), axis=1).astype(jnp.int32)
    return rank_in.reshape(expert_ids.shape)


MESH = pl.DeviceIdType.MESH


def dispatch_kernel(
    z_count, chunks, blk_ref, rt_ref, out_ref, rt_out, send_sem, recv_sem, rt_sem, local_sem
):
    z = lax.axis_index("z")
    c = lax.axis_index("c")
    row = lax.axis_index("dp")
    other = 1 - c
    step = 1 - 2 * c
    fwd = lax.rem(z + step + z_count, z_count)
    bwd = lax.rem(z - step + z_count, z_count)
    fwd_id, bwd_id, pair_id = (row, fwd, c), (row, bwd, c), (row, z, other)
    piece = blk_ref.shape[0] // chunks

    barrier = pltpu.get_barrier_semaphore()
    for target in (fwd_id, bwd_id, pair_id):
        pl.semaphore_signal(barrier, 1, device_id=target, device_id_type=MESH)
    pl.semaphore_wait(barrier, 3)

    mine = c * z_count + z
    local = pltpu.make_async_copy(blk_ref, out_ref.at[mine], local_sem.at[0])
    local.start()
    local_rt = pltpu.make_async_copy(rt_ref, rt_out.at[mine], local_sem.at[1])
    local_rt.start()
    sends = []

    def part(ref, k):
        return ref.at[pl.ds(k * piece, piece)]

    def remote(src, dst, sem, target):
        copy = pltpu.make_async_remote_copy(
            src_ref=src,
            dst_ref=dst,
            send_sem=send_sem.at[len(sends)],
            recv_sem=sem,
            device_id=target,
            device_id_type=MESH,
        )
        copy.start()
        sends.append(copy)

    def send(src, rt_src, slot, k, target):
        remote(part(src, k), part(out_ref.at[slot], k), recv_sem.at[slot * chunks + k], target)
        if k == 0:
            remote(rt_src, rt_out.at[slot], rt_sem.at[slot], target)

    def wait_for(view, sem):
        pltpu.make_async_remote_copy(
            src_ref=view,
            dst_ref=view,
            send_sem=send_sem.at[0],
            recv_sem=sem,
            device_id=pair_id,
            device_id_type=MESH,
        ).wait_recv()

    def arrive(slot, k):
        wait_for(part(out_ref.at[slot], k), recv_sem.at[slot * chunks + k])
        if k == 0:
            wait_for(rt_out.at[slot], rt_sem.at[slot])

    for k in range(chunks):
        send(blk_ref, rt_ref, mine, k, fwd_id)
        send(blk_ref, rt_ref, mine, k, bwd_id)
    for k in range(chunks):
        send(blk_ref, rt_ref, mine, k, pair_id)
    fwd_hops = z_count // 2
    bwd_hops = z_count - 1 - fwd_hops
    for hop in range(1, fwd_hops + 1):
        for k in range(chunks):
            slot = c * z_count + lax.rem(z - step * hop + 2 * z_count, z_count)
            arrive(slot, k)
            if hop < fwd_hops:
                send(out_ref.at[slot], rt_out.at[slot], slot, k, fwd_id)
            send(out_ref.at[slot], rt_out.at[slot], slot, k, pair_id)
            if hop <= bwd_hops:
                slot = c * z_count + lax.rem(z + step * hop + 2 * z_count, z_count)
                arrive(slot, k)
                if hop < bwd_hops:
                    send(out_ref.at[slot], rt_out.at[slot], slot, k, bwd_id)
                send(out_ref.at[slot], rt_out.at[slot], slot, k, pair_id)
    for zz in range(z_count):
        for k in range(chunks):
            arrive(other * z_count + zz, k)
    local.wait()
    local_rt.wait()
    for copy in sends:
        copy.wait_send()


def gather_blocks(block, route_tile, z_count, chunks):
    count = 2 * z_count
    vmem = pl.BlockSpec(memory_space=pltpu.VMEM)
    return pl.pallas_call(
        functools.partial(dispatch_kernel, z_count, chunks),
        out_shape=(
            jax.ShapeDtypeStruct((count,) + block.shape, block.dtype),
            jax.ShapeDtypeStruct((count,) + route_tile.shape, route_tile.dtype),
        ),
        in_specs=[vmem, vmem],
        out_specs=(vmem, vmem),
        scratch_shapes=[
            pltpu.SemaphoreType.DMA((3 * count * chunks,)),
            pltpu.SemaphoreType.DMA((count * chunks,)),
            pltpu.SemaphoreType.DMA((count,)),
            pltpu.SemaphoreType.DMA((2,)),
        ],
        compiler_params=pltpu.CompilerParams(
            collective_id=0, has_side_effects=True, vmem_limit_bytes=32 * 1024 * 1024
        ),
    )(block, route_tile)


def combine_kernel(
    z_count, dp_count, seq_len, chunks, part_ref, head_ref, out_ref, pair_out, pair_buf,
    fwd_buf, bwd_buf, fwd_out, bwd_out, seq_out, seq_in, send_sem, recv_sem, seq_sem,
):
    z = lax.axis_index("z")
    c = lax.axis_index("c")
    row = lax.axis_index("dp")
    other = 1 - c
    step = 1 - 2 * c
    fwd = lax.rem(z + step + z_count, z_count)
    bwd = lax.rem(z - step + z_count, z_count)
    fwd_id, bwd_id, pair_id = (row, fwd, c), (row, bwd, c), (row, z, other)
    mate_id = (lax.rem(row + dp_count // 2, dp_count), z, c)
    fwd_hops = z_count // 2
    bwd_hops = z_count - 1 - fwd_hops
    piece = part_ref.shape[2] // chunks

    barrier = pltpu.get_barrier_semaphore()
    for target in (fwd_id, bwd_id, pair_id, mate_id):
        pl.semaphore_signal(barrier, 1, device_id=target, device_id_type=MESH)
    pl.semaphore_wait(barrier, 4)

    sends = []

    def send(src, dst, sem, target):
        copy = pltpu.make_async_remote_copy(
            src_ref=src,
            dst_ref=dst,
            send_sem=send_sem.at[len(sends)],
            recv_sem=recv_sem.at[sem],
            device_id=target,
            device_id_type=MESH,
        )
        copy.start()
        sends.append(copy)

    def arrive(dst, sem):
        pltpu.make_async_remote_copy(
            src_ref=dst,
            dst_ref=dst,
            send_sem=send_sem.at[0],
            recv_sem=recv_sem.at[sem],
            device_id=pair_id,
            device_id_type=MESH,
        ).wait_recv()

    def order(ring_step):
        dests = []
        for hop in range(1, fwd_hops + 1):
            dests.append(lax.rem(z + ring_step * (fwd_hops + 1 - hop) + 2 * z_count, z_count))
            if hop <= bwd_hops:
                dests.append(lax.rem(z - ring_step * (bwd_hops + 1 - hop) + 2 * z_count, z_count))
        return dests + [z]

    for n, dest in enumerate(order(-step)):
        send(part_ref.at[other, dest], pair_buf.at[n], n, pair_id)
    def own(dest, n, k):
        if k == 0:
            arrive(pair_buf.at[n], n)
        rows = pl.ds(k * piece, piece)
        return part_ref[c, dest, rows].astype(jnp.float32) + pair_buf[n, rows].astype(
            jnp.float32
        )

    fwd_sem = z_count
    bwd_sem = z_count + fwd_hops * chunks
    for hop in range(1, fwd_hops + 1):
        for k in range(chunks):
            rows = pl.ds(k * piece, piece)
            dest = lax.rem(z + step * (fwd_hops + 1 - hop) + 2 * z_count, z_count)
            n = hop - 1 + min(hop - 1, bwd_hops)
            total = own(dest, n, k)
            if hop > 1:
                sem = fwd_sem + (hop - 2) * chunks + k
                arrive(fwd_buf.at[hop - 2, rows], sem)
                total = total + fwd_buf[hop - 2, rows].astype(jnp.float32)
            fwd_out[hop - 1, rows] = total.astype(fwd_out.dtype)
            sem = fwd_sem + (hop - 1) * chunks + k
            send(fwd_out.at[hop - 1, rows], fwd_buf.at[hop - 1, rows], sem, fwd_id)
            if hop <= bwd_hops:
                dest = lax.rem(z - step * (bwd_hops + 1 - hop) + 2 * z_count, z_count)
                total = own(dest, n + 1, k)
                if hop > 1:
                    sem = bwd_sem + (hop - 2) * chunks + k
                    arrive(bwd_buf.at[hop - 2, rows], sem)
                    total = total + bwd_buf[hop - 2, rows].astype(jnp.float32)
                bwd_out[hop - 1, rows] = total.astype(bwd_out.dtype)
                sem = bwd_sem + (hop - 1) * chunks + k
                send(bwd_out.at[hop - 1, rows], bwd_buf.at[hop - 1, rows], sem, bwd_id)
    for k in range(chunks):
        rows = pl.ds(k * piece, piece)
        total = own(z, fwd_hops + bwd_hops, k)
        arrive(fwd_buf.at[fwd_hops - 1, rows], fwd_sem + (fwd_hops - 1) * chunks + k)
        total = total + fwd_buf[fwd_hops - 1, rows].astype(jnp.float32)
        if bwd_hops > 0:
            arrive(bwd_buf.at[bwd_hops - 1, rows], bwd_sem + (bwd_hops - 1) * chunks + k)
            total = total + bwd_buf[bwd_hops - 1, rows].astype(jnp.float32)
        out_ref[rows] = total.astype(out_ref.dtype)
    tok_rows, width = out_ref.shape
    seqs = tok_rows // seq_len
    scored = out_ref[...].astype(jnp.float32) * head_ref[...]
    per_seq = jnp.sum(scored.reshape(seqs, seq_len, width), axis=1)
    seq_score = jnp.sum(per_seq, axis=1, keepdims=True)
    seq_out[...] = jnp.zeros(seq_out.shape, jnp.float32)
    seq_out[pl.ds(0, seqs)] = jnp.broadcast_to(seq_score, (seqs, seq_out.shape[1]))
    mate = pltpu.make_async_remote_copy(
        src_ref=seq_out,
        dst_ref=seq_in,
        send_sem=seq_sem.at[0],
        recv_sem=seq_sem.at[1],
        device_id=mate_id,
        device_id_type=MESH,
    )
    mate.start()
    mate.wait()
    mine = seq_out[...]
    theirs = seq_in[...]
    pair_out[...] = jnp.abs(mine - theirs) + 0.5 * (mine + theirs)
    for copy in sends:
        copy.wait_send()


def scatter_sums(partial, score_head, dp_count, seq_len, chunks):
    c_count, z_count, rows, width = partial.shape
    fwd_hops = z_count // 2
    bwd_hops = max(z_count - 1 - fwd_hops, 1)
    block = (rows, width)
    vmem = pl.BlockSpec(memory_space=pltpu.VMEM)
    sems = z_count + (fwd_hops + bwd_hops) * chunks
    tile = (8, 128)
    return pl.pallas_call(
        functools.partial(combine_kernel, z_count, dp_count, seq_len, chunks),
        out_shape=(
            jax.ShapeDtypeStruct(block, partial.dtype),
            jax.ShapeDtypeStruct(tile, jnp.float32),
        ),
        in_specs=[vmem, vmem],
        out_specs=(vmem, vmem),
        scratch_shapes=[
            pltpu.VMEM((z_count,) + block, partial.dtype),
            pltpu.VMEM((fwd_hops,) + block, partial.dtype),
            pltpu.VMEM((bwd_hops,) + block, partial.dtype),
            pltpu.VMEM((fwd_hops,) + block, partial.dtype),
            pltpu.VMEM((bwd_hops,) + block, partial.dtype),
            pltpu.VMEM(tile, jnp.float32),
            pltpu.VMEM(tile, jnp.float32),
            pltpu.SemaphoreType.DMA((sems,)),
            pltpu.SemaphoreType.DMA((sems,)),
            pltpu.SemaphoreType.DMA((2,)),
        ],
        compiler_params=pltpu.CompilerParams(
            collective_id=1, has_side_effects=True, vmem_limit_bytes=48 * 1024 * 1024
        ),
    )(partial, score_head.reshape(1, -1))


def body(
    tokens, expert_ids, gate_fixed, scorer_id, direction_tags, w_gate, w_up, w_down, score_head
):
    z_count = lax.axis_size("z")
    c_count = lax.axis_size("c")
    expert_count = z_count * c_count
    per_device = w_gate.shape[0]
    tok_rows, model_width = tokens.shape
    top_count = expert_ids.shape[1]
    which_tag = jnp.repeat(scorer_id, SEQ_LEN)[:, None]
    tag_rows = jnp.where(
        which_tag == 1, direction_tags[1][None, :], direction_tags[0][None, :]
    ).astype(jnp.float32)
    inputs = (tokens.astype(jnp.float32) + tag_rows).astype(jnp.bfloat16)
    rank_in = route_ranks(expert_ids, per_device * expert_count)
    routes = jnp.concatenate(
        [expert_ids, rank_in, gate_fixed // 256, gate_fixed % 256], axis=1
    ).astype(jnp.bfloat16)
    route_tile = routes.reshape(-1, 128)
    inputs_all, routes_all = gather_blocks(inputs, route_tile, z_count, 2)
    routes_all = routes_all.reshape(expert_count, tok_rows, 4 * top_count).astype(jnp.int32)
    ids_cube = routes_all[..., :top_count]
    rank_cube = routes_all[..., top_count : 2 * top_count]
    fixed_val = (
        routes_all[..., 2 * top_count : 3 * top_count] * 256 + routes_all[..., 3 * top_count :]
    ).astype(jnp.float32)
    weight_cube = fixed_val / jnp.sum(fixed_val, axis=2, keepdims=True)
    my_index = lax.axis_index("z") * c_count + lax.axis_index("c")
    local_count = per_device * MOST
    local_slot = ids_cube - my_index * per_device
    is_mine = (local_slot >= 0) & (local_slot < per_device)
    local_key = jnp.where(is_mine, local_slot * MOST + rank_cube, -1)
    match = (
        local_key[:, None, :, :] == jnp.arange(local_count, dtype=jnp.int32)[None, :, None, None]
    )
    picker = jnp.any(match, axis=3).astype(jnp.bfloat16)
    slot_weight = jnp.sum(jnp.where(match, weight_cube[:, None, :, :], 0.0), axis=(2, 3))
    picker = picker.reshape(expert_count, per_device, MOST, tok_rows).transpose(1, 0, 2, 3)
    slot_weight = slot_weight.reshape(expert_count, per_device, MOST).transpose(1, 0, 2)
    row_block = jnp.einsum(
        "esmt,std->esmd", picker, inputs_all, preferred_element_type=jnp.float32
    ).astype(jnp.bfloat16)
    gate_proj = jnp.einsum("esmd,edf->esmf", row_block, w_gate, preferred_element_type=jnp.float32)
    up_proj = jnp.einsum("esmd,edf->esmf", row_block, w_up, preferred_element_type=jnp.float32)
    hidden = (jax.nn.silu(gate_proj) * up_proj).astype(jnp.bfloat16)
    down_out = jnp.einsum("esmf,efd->esmd", hidden, w_down, preferred_element_type=jnp.float32)
    result = (slot_weight[..., None] * down_out).astype(jnp.bfloat16)
    result = lax.optimization_barrier(result)
    partial_value = jnp.einsum(
        "esmt,esmd->std", picker, result, preferred_element_type=jnp.float32
    )
    partial_value = partial_value.reshape(c_count, z_count, tok_rows, model_width)
    mixed, pair_tile = scatter_sums(
        partial_value.astype(jnp.bfloat16), score_head, lax.axis_size("dp"), SEQ_LEN, 1
    )
    pair_score = pair_tile[: tok_rows // SEQ_LEN, 0]
    return (mixed, pair_score)


def solution(mesh):
    dp_count, expert_count = mesh.devices.shape
    split = Mesh(mesh.devices.reshape(dp_count, expert_count // 2, 2), ("dp", "z", "c"))
    rows = P(("dp", "z", "c"), None)
    return jax.shard_map(
        body,
        mesh=split,
        in_specs=(
            rows,
            rows,
            rows,
            P(("dp", "z", "c")),
            P(),
            P(("z", "c"), None, None),
            P(("z", "c"), None, None),
            P(("z", "c"), None, None),
            P(),
        ),
        out_specs=(rows, P(("dp", "z", "c"))),
        check_vma=False,
    )
```

```python
import functools

import jax
import jax.numpy as jnp
from jax import lax
from jax.experimental import pallas as pl
from jax.experimental.pallas import tpu as pltpu
from jax.sharding import Mesh
from jax.sharding import PartitionSpec as P

SEQ_LEN = 16
MOST = 24


def from_partner(block, axis, bit):
    count = lax.axis_size(axis)
    route = []
    for low in range(count):
        high = low | 1 << bit
        if high != low and high < count:
            route += [(low, high), (high, low)]
    return lax.ppermute(block, axis, route)


def route_ranks(expert_ids, expert_total):
    flat_ids = expert_ids.reshape(-1)
    entry_count = flat_ids.shape[0]
    onehot = flat_ids[:, None] == jnp.arange(expert_total, dtype=jnp.int32)[None, :]
    positions = jnp.arange(entry_count, dtype=jnp.int32)
    earlier = (positions[:, None] > positions[None, :]).astype(jnp.bfloat16)
    counts = jnp.dot(earlier, onehot.astype(jnp.bfloat16), preferred_element_type=jnp.float32)
    rank_in = jnp.sum(jnp.where(onehot, counts, 0.0), axis=1).astype(jnp.int32)
    return rank_in.reshape(expert_ids.shape)


MESH = pl.DeviceIdType.MESH


def dispatch_kernel(
    z_count, chunks, blk_ref, rt_ref, out_ref, rt_out, send_sem, recv_sem, rt_sem, local_sem
):
    z = lax.axis_index("z")
    c = lax.axis_index("c")
    row = lax.axis_index("dp")
    other = 1 - c
    step = 1 - 2 * c
    fwd = lax.rem(z + step + z_count, z_count)
    bwd = lax.rem(z - step + z_count, z_count)
    fwd_id, bwd_id, pair_id = (row, fwd, c), (row, bwd, c), (row, z, other)
    piece = blk_ref.shape[0] // chunks

    barrier = pltpu.get_barrier_semaphore()
    for target in (fwd_id, bwd_id, pair_id):
        pl.semaphore_signal(barrier, 1, device_id=target, device_id_type=MESH)
    pl.semaphore_wait(barrier, 3)

    mine = c * z_count + z
    local = pltpu.make_async_copy(blk_ref, out_ref.at[mine], local_sem.at[0])
    local.start()
    local_rt = pltpu.make_async_copy(rt_ref, rt_out.at[mine], local_sem.at[1])
    local_rt.start()
    sends = []

    def part(ref, k):
        return ref.at[pl.ds(k * piece, piece)]

    def remote(src, dst, sem, target):
        copy = pltpu.make_async_remote_copy(
            src_ref=src,
            dst_ref=dst,
            send_sem=send_sem.at[len(sends)],
            recv_sem=sem,
            device_id=target,
            device_id_type=MESH,
        )
        copy.start()
        sends.append(copy)

    def send(src, rt_src, slot, k, target):
        remote(part(src, k), part(out_ref.at[slot], k), recv_sem.at[slot * chunks + k], target)
        if k == 0:
            remote(rt_src, rt_out.at[slot], rt_sem.at[slot], target)

    def wait_for(view, sem):
        pltpu.make_async_remote_copy(
            src_ref=view,
            dst_ref=view,
            send_sem=send_sem.at[0],
            recv_sem=sem,
            device_id=pair_id,
            device_id_type=MESH,
        ).wait_recv()

    def arrive(slot, k):
        wait_for(part(out_ref.at[slot], k), recv_sem.at[slot * chunks + k])
        if k == 0:
            wait_for(rt_out.at[slot], rt_sem.at[slot])

    for k in range(chunks):
        send(blk_ref, rt_ref, mine, k, fwd_id)
        send(blk_ref, rt_ref, mine, k, bwd_id)
    for k in range(chunks):
        send(blk_ref, rt_ref, mine, k, pair_id)
    fwd_hops = z_count // 2
    bwd_hops = z_count - 1 - fwd_hops
    for hop in range(1, fwd_hops + 1):
        for k in range(chunks):
            slot = c * z_count + lax.rem(z - step * hop + 2 * z_count, z_count)
            arrive(slot, k)
            if hop < fwd_hops:
                send(out_ref.at[slot], rt_out.at[slot], slot, k, fwd_id)
            send(out_ref.at[slot], rt_out.at[slot], slot, k, pair_id)
            if hop <= bwd_hops:
                slot = c * z_count + lax.rem(z + step * hop + 2 * z_count, z_count)
                arrive(slot, k)
                if hop < bwd_hops:
                    send(out_ref.at[slot], rt_out.at[slot], slot, k, bwd_id)
                send(out_ref.at[slot], rt_out.at[slot], slot, k, pair_id)
    for zz in range(z_count):
        for k in range(chunks):
            arrive(other * z_count + zz, k)
    local.wait()
    local_rt.wait()
    for copy in sends:
        copy.wait_send()


def gather_blocks(block, route_tile, z_count, chunks):
    count = 2 * z_count
    vmem = pl.BlockSpec(memory_space=pltpu.VMEM)
    return pl.pallas_call(
        functools.partial(dispatch_kernel, z_count, chunks),
        out_shape=(
            jax.ShapeDtypeStruct((count,) + block.shape, block.dtype),
            jax.ShapeDtypeStruct((count,) + route_tile.shape, route_tile.dtype),
        ),
        in_specs=[vmem, vmem],
        out_specs=(vmem, vmem),
        scratch_shapes=[
            pltpu.SemaphoreType.DMA((3 * count * chunks,)),
            pltpu.SemaphoreType.DMA((count * chunks,)),
            pltpu.SemaphoreType.DMA((count,)),
            pltpu.SemaphoreType.DMA((2,)),
        ],
        compiler_params=pltpu.CompilerParams(
            collective_id=0, has_side_effects=True, vmem_limit_bytes=32 * 1024 * 1024
        ),
    )(block, route_tile)


def combine_kernel(
    z_count, dp_count, seq_len, chunks, part_ref, head_ref, out_ref, pair_out, pair_buf,
    fwd_buf, bwd_buf, fwd_out, bwd_out, seq_out, seq_in, send_sem, recv_sem, seq_sem,
):
    z = lax.axis_index("z")
    c = lax.axis_index("c")
    row = lax.axis_index("dp")
    other = 1 - c
    step = 1 - 2 * c
    fwd = lax.rem(z + step + z_count, z_count)
    bwd = lax.rem(z - step + z_count, z_count)
    fwd_id, bwd_id, pair_id = (row, fwd, c), (row, bwd, c), (row, z, other)
    mate_id = (lax.rem(row + dp_count // 2, dp_count), z, c)
    fwd_hops = z_count // 2
    bwd_hops = z_count - 1 - fwd_hops
    piece = part_ref.shape[2] // chunks

    barrier = pltpu.get_barrier_semaphore()
    for target in (fwd_id, bwd_id, pair_id, mate_id):
        pl.semaphore_signal(barrier, 1, device_id=target, device_id_type=MESH)
    pl.semaphore_wait(barrier, 4)

    sends = []

    def send(src, dst, sem, target):
        copy = pltpu.make_async_remote_copy(
            src_ref=src,
            dst_ref=dst,
            send_sem=send_sem.at[len(sends)],
            recv_sem=recv_sem.at[sem],
            device_id=target,
            device_id_type=MESH,
        )
        copy.start()
        sends.append(copy)

    def arrive(dst, sem):
        pltpu.make_async_remote_copy(
            src_ref=dst,
            dst_ref=dst,
            send_sem=send_sem.at[0],
            recv_sem=recv_sem.at[sem],
            device_id=pair_id,
            device_id_type=MESH,
        ).wait_recv()

    def order(ring_step):
        dests = []
        for hop in range(1, fwd_hops + 1):
            dests.append(lax.rem(z + ring_step * (fwd_hops + 1 - hop) + 2 * z_count, z_count))
            if hop <= bwd_hops:
                dests.append(lax.rem(z - ring_step * (bwd_hops + 1 - hop) + 2 * z_count, z_count))
        return dests + [z]

    for n, dest in enumerate(order(-step)):
        send(part_ref.at[other, dest], pair_buf.at[n], n, pair_id)
    def own(dest, n, k):
        if k == 0:
            arrive(pair_buf.at[n], n)
        rows = pl.ds(k * piece, piece)
        return part_ref[c, dest, rows].astype(jnp.float32) + pair_buf[n, rows].astype(
            jnp.float32
        )

    fwd_sem = z_count
    bwd_sem = z_count + fwd_hops * chunks
    for hop in range(1, fwd_hops + 1):
        for k in range(chunks):
            rows = pl.ds(k * piece, piece)
            dest = lax.rem(z + step * (fwd_hops + 1 - hop) + 2 * z_count, z_count)
            n = hop - 1 + min(hop - 1, bwd_hops)
            total = own(dest, n, k)
            if hop > 1:
                sem = fwd_sem + (hop - 2) * chunks + k
                arrive(fwd_buf.at[hop - 2, rows], sem)
                total = total + fwd_buf[hop - 2, rows].astype(jnp.float32)
            fwd_out[hop - 1, rows] = total.astype(fwd_out.dtype)
            sem = fwd_sem + (hop - 1) * chunks + k
            send(fwd_out.at[hop - 1, rows], fwd_buf.at[hop - 1, rows], sem, fwd_id)
            if hop <= bwd_hops:
                dest = lax.rem(z - step * (bwd_hops + 1 - hop) + 2 * z_count, z_count)
                total = own(dest, n + 1, k)
                if hop > 1:
                    sem = bwd_sem + (hop - 2) * chunks + k
                    arrive(bwd_buf.at[hop - 2, rows], sem)
                    total = total + bwd_buf[hop - 2, rows].astype(jnp.float32)
                bwd_out[hop - 1, rows] = total.astype(bwd_out.dtype)
                sem = bwd_sem + (hop - 1) * chunks + k
                send(bwd_out.at[hop - 1, rows], bwd_buf.at[hop - 1, rows], sem, bwd_id)
    for k in range(chunks):
        rows = pl.ds(k * piece, piece)
        total = own(z, fwd_hops + bwd_hops, k)
        arrive(fwd_buf.at[fwd_hops - 1, rows], fwd_sem + (fwd_hops - 1) * chunks + k)
        total = total + fwd_buf[fwd_hops - 1, rows].astype(jnp.float32)
        if bwd_hops > 0:
            arrive(bwd_buf.at[bwd_hops - 1, rows], bwd_sem + (bwd_hops - 1) * chunks + k)
            total = total + bwd_buf[bwd_hops - 1, rows].astype(jnp.float32)
        out_ref[rows] = total.astype(out_ref.dtype)
    tok_rows, width = out_ref.shape
    seqs = tok_rows // seq_len
    scored = out_ref[...].astype(jnp.float32) * head_ref[...]
    per_seq = jnp.sum(scored.reshape(seqs, seq_len, width), axis=1)
    seq_score = jnp.sum(per_seq, axis=1, keepdims=True)
    seq_out[...] = jnp.zeros(seq_out.shape, jnp.float32)
    seq_out[pl.ds(0, seqs)] = jnp.broadcast_to(seq_score, (seqs, seq_out.shape[1]))
    mate = pltpu.make_async_remote_copy(
        src_ref=seq_out,
        dst_ref=seq_in,
        send_sem=seq_sem.at[0],
        recv_sem=seq_sem.at[1],
        device_id=mate_id,
        device_id_type=MESH,
    )
    mate.start()
    mate.wait()
    mine = seq_out[...]
    theirs = seq_in[...]
    pair_out[...] = jnp.abs(mine - theirs) + 0.5 * (mine + theirs)
    for copy in sends:
        copy.wait_send()


def scatter_sums(partial, score_head, dp_count, seq_len, chunks):
    c_count, z_count, rows, width = partial.shape
    fwd_hops = z_count // 2
    bwd_hops = max(z_count - 1 - fwd_hops, 1)
    block = (rows, width)
    vmem = pl.BlockSpec(memory_space=pltpu.VMEM)
    sems = z_count + (fwd_hops + bwd_hops) * chunks
    tile = (8, 128)
    return pl.pallas_call(
        functools.partial(combine_kernel, z_count, dp_count, seq_len, chunks),
        out_shape=(
            jax.ShapeDtypeStruct(block, partial.dtype),
            jax.ShapeDtypeStruct(tile, jnp.float32),
        ),
        in_specs=[vmem, vmem],
        out_specs=(vmem, vmem),
        scratch_shapes=[
            pltpu.VMEM((z_count,) + block, partial.dtype),
            pltpu.VMEM((fwd_hops,) + block, partial.dtype),
            pltpu.VMEM((bwd_hops,) + block, partial.dtype),
            pltpu.VMEM((fwd_hops,) + block, partial.dtype),
            pltpu.VMEM((bwd_hops,) + block, partial.dtype),
            pltpu.VMEM(tile, jnp.float32),
            pltpu.VMEM(tile, jnp.float32),
            pltpu.SemaphoreType.DMA((sems,)),
            pltpu.SemaphoreType.DMA((sems,)),
            pltpu.SemaphoreType.DMA((2,)),
        ],
        compiler_params=pltpu.CompilerParams(
            collective_id=1, has_side_effects=True, vmem_limit_bytes=48 * 1024 * 1024
        ),
    )(partial, score_head.reshape(1, -1))


def body(
    tokens, expert_ids, gate_fixed, scorer_id, direction_tags, w_gate, w_up, w_down, score_head
):
    z_count = lax.axis_size("z")
    c_count = lax.axis_size("c")
    expert_count = z_count * c_count
    per_device = w_gate.shape[0]
    tok_rows, model_width = tokens.shape
    top_count = expert_ids.shape[1]
    which_tag = jnp.repeat(scorer_id, SEQ_LEN)[:, None]
    tag_rows = jnp.where(
        which_tag == 1, direction_tags[1][None, :], direction_tags[0][None, :]
    ).astype(jnp.float32)
    inputs = (tokens.astype(jnp.float32) + tag_rows).astype(jnp.bfloat16)
    rank_in = route_ranks(expert_ids, per_device * expert_count)
    routes = jnp.concatenate(
        [expert_ids, rank_in, gate_fixed // 256, gate_fixed % 256], axis=1
    ).astype(jnp.bfloat16)
    route_tile = routes.reshape(-1, 128)
    inputs_all, routes_all = gather_blocks(inputs, route_tile, z_count, 2)
    routes_all = routes_all.reshape(expert_count, tok_rows, 4 * top_count).astype(jnp.int32)
    ids_cube = routes_all[..., :top_count]
    rank_cube = routes_all[..., top_count : 2 * top_count]
    fixed_val = (
        routes_all[..., 2 * top_count : 3 * top_count] * 256 + routes_all[..., 3 * top_count :]
    ).astype(jnp.float32)
    weight_cube = fixed_val / jnp.sum(fixed_val, axis=2, keepdims=True)
    my_index = lax.axis_index("z") * c_count + lax.axis_index("c")
    local_count = per_device * MOST
    local_slot = ids_cube - my_index * per_device
    is_mine = (local_slot >= 0) & (local_slot < per_device)
    local_key = jnp.where(is_mine, local_slot * MOST + rank_cube, -1)
    match = (
        local_key[:, None, :, :] == jnp.arange(local_count, dtype=jnp.int32)[None, :, None, None]
    )
    picker = jnp.any(match, axis=3).astype(jnp.bfloat16)
    slot_weight = jnp.sum(jnp.where(match, weight_cube[:, None, :, :], 0.0), axis=(2, 3))
    picker = picker.reshape(expert_count, per_device, MOST, tok_rows).transpose(1, 0, 2, 3)
    slot_weight = slot_weight.reshape(expert_count, per_device, MOST).transpose(1, 0, 2)
    row_block = jnp.einsum(
        "esmt,std->esmd", picker, inputs_all, preferred_element_type=jnp.float32
    ).astype(jnp.bfloat16)
    gate_proj = jnp.einsum("esmd,edf->esmf", row_block, w_gate, preferred_element_type=jnp.float32)
    up_proj = jnp.einsum("esmd,edf->esmf", row_block, w_up, preferred_element_type=jnp.float32)
    hidden = (jax.nn.silu(gate_proj) * up_proj).astype(jnp.bfloat16)
    down_out = jnp.einsum("esmf,efd->esmd", hidden, w_down, preferred_element_type=jnp.float32)
    result = (slot_weight[..., None] * down_out).astype(jnp.bfloat16)
    result = lax.optimization_barrier(result)
    partial_value = jnp.einsum(
        "esmt,esmd->std", picker, result, preferred_element_type=jnp.float32
    )
    partial_value = partial_value.reshape(c_count, z_count, tok_rows, model_width)
    mixed, pair_tile = scatter_sums(
        partial_value.astype(jnp.bfloat16), score_head, lax.axis_size("dp"), SEQ_LEN, 4
    )
    pair_score = pair_tile[: tok_rows // SEQ_LEN, 0]
    return (mixed, pair_score)


def solution(mesh):
    dp_count, expert_count = mesh.devices.shape
    split = Mesh(mesh.devices.reshape(dp_count, expert_count // 2, 2), ("dp", "z", "c"))
    rows = P(("dp", "z", "c"), None)
    return jax.shard_map(
        body,
        mesh=split,
        in_specs=(
            rows,
            rows,
            rows,
            P(("dp", "z", "c")),
            P(),
            P(("z", "c"), None, None),
            P(("z", "c"), None, None),
            P(("z", "c"), None, None),
            P(),
        ),
        out_specs=(rows, P(("dp", "z", "c"))),
        check_vma=False,
    )
```

```python
import functools

import jax
import jax.numpy as jnp
from jax import lax
from jax.experimental import pallas as pl
from jax.experimental.pallas import tpu as pltpu
from jax.sharding import Mesh
from jax.sharding import PartitionSpec as P

SEQ_LEN = 16
MOST = 24


def from_partner(block, axis, bit):
    count = lax.axis_size(axis)
    route = []
    for low in range(count):
        high = low | 1 << bit
        if high != low and high < count:
            route += [(low, high), (high, low)]
    return lax.ppermute(block, axis, route)


def route_ranks(expert_ids, expert_total):
    flat_ids = expert_ids.reshape(-1)
    entry_count = flat_ids.shape[0]
    onehot = flat_ids[:, None] == jnp.arange(expert_total, dtype=jnp.int32)[None, :]
    positions = jnp.arange(entry_count, dtype=jnp.int32)
    earlier = (positions[:, None] > positions[None, :]).astype(jnp.bfloat16)
    counts = jnp.dot(earlier, onehot.astype(jnp.bfloat16), preferred_element_type=jnp.float32)
    rank_in = jnp.sum(jnp.where(onehot, counts, 0.0), axis=1).astype(jnp.int32)
    return rank_in.reshape(expert_ids.shape)


MESH = pl.DeviceIdType.MESH


def dispatch_kernel(
    z_count, chunks, blk_ref, rt_ref, out_ref, rt_out, send_sem, recv_sem, rt_sem, local_sem
):
    z = lax.axis_index("z")
    c = lax.axis_index("c")
    row = lax.axis_index("dp")
    other = 1 - c
    step = 1 - 2 * c
    fwd = lax.rem(z + step + z_count, z_count)
    bwd = lax.rem(z - step + z_count, z_count)
    fwd_id, bwd_id, pair_id = (row, fwd, c), (row, bwd, c), (row, z, other)
    piece = blk_ref.shape[0] // chunks

    barrier = pltpu.get_barrier_semaphore()
    for target in (fwd_id, bwd_id, pair_id):
        pl.semaphore_signal(barrier, 1, device_id=target, device_id_type=MESH)
    pl.semaphore_wait(barrier, 3)

    mine = c * z_count + z
    local = pltpu.make_async_copy(blk_ref, out_ref.at[mine], local_sem.at[0])
    local.start()
    local_rt = pltpu.make_async_copy(rt_ref, rt_out.at[mine], local_sem.at[1])
    local_rt.start()
    sends = []

    def part(ref, k):
        return ref.at[pl.ds(k * piece, piece)]

    def remote(src, dst, sem, target):
        copy = pltpu.make_async_remote_copy(
            src_ref=src,
            dst_ref=dst,
            send_sem=send_sem.at[len(sends)],
            recv_sem=sem,
            device_id=target,
            device_id_type=MESH,
        )
        copy.start()
        sends.append(copy)

    def send(src, rt_src, slot, k, target):
        remote(part(src, k), part(out_ref.at[slot], k), recv_sem.at[slot * chunks + k], target)
        if k == 0:
            remote(rt_src, rt_out.at[slot], rt_sem.at[slot], target)

    def wait_for(view, sem):
        pltpu.make_async_remote_copy(
            src_ref=view,
            dst_ref=view,
            send_sem=send_sem.at[0],
            recv_sem=sem,
            device_id=pair_id,
            device_id_type=MESH,
        ).wait_recv()

    def arrive(slot, k):
        wait_for(part(out_ref.at[slot], k), recv_sem.at[slot * chunks + k])
        if k == 0:
            wait_for(rt_out.at[slot], rt_sem.at[slot])

    for k in range(chunks):
        send(blk_ref, rt_ref, mine, k, fwd_id)
        send(blk_ref, rt_ref, mine, k, bwd_id)
    for k in range(chunks):
        send(blk_ref, rt_ref, mine, k, pair_id)
    fwd_hops = z_count // 2
    bwd_hops = z_count - 1 - fwd_hops
    for hop in range(1, fwd_hops + 1):
        for k in range(chunks):
            slot = c * z_count + lax.rem(z - step * hop + 2 * z_count, z_count)
            arrive(slot, k)
            if hop < fwd_hops:
                send(out_ref.at[slot], rt_out.at[slot], slot, k, fwd_id)
            send(out_ref.at[slot], rt_out.at[slot], slot, k, pair_id)
            if hop <= bwd_hops:
                slot = c * z_count + lax.rem(z + step * hop + 2 * z_count, z_count)
                arrive(slot, k)
                if hop < bwd_hops:
                    send(out_ref.at[slot], rt_out.at[slot], slot, k, bwd_id)
                send(out_ref.at[slot], rt_out.at[slot], slot, k, pair_id)
    for zz in range(z_count):
        for k in range(chunks):
            arrive(other * z_count + zz, k)
    local.wait()
    local_rt.wait()
    for copy in sends:
        copy.wait_send()


def gather_blocks(block, route_tile, z_count, chunks):
    count = 2 * z_count
    vmem = pl.BlockSpec(memory_space=pltpu.VMEM)
    return pl.pallas_call(
        functools.partial(dispatch_kernel, z_count, chunks),
        out_shape=(
            jax.ShapeDtypeStruct((count,) + block.shape, block.dtype),
            jax.ShapeDtypeStruct((count,) + route_tile.shape, route_tile.dtype),
        ),
        in_specs=[vmem, vmem],
        out_specs=(vmem, vmem),
        scratch_shapes=[
            pltpu.SemaphoreType.DMA((3 * count * chunks,)),
            pltpu.SemaphoreType.DMA((count * chunks,)),
            pltpu.SemaphoreType.DMA((count,)),
            pltpu.SemaphoreType.DMA((2,)),
        ],
        compiler_params=pltpu.CompilerParams(
            collective_id=0, has_side_effects=True, vmem_limit_bytes=32 * 1024 * 1024
        ),
    )(block, route_tile)


def combine_kernel(
    z_count, dp_count, seq_len, chunks, part_ref, head_ref, out_ref, pair_out, pair_buf,
    fwd_buf, bwd_buf, fwd_out, bwd_out, seq_out, seq_in, send_sem, recv_sem, seq_sem,
):
    z = lax.axis_index("z")
    c = lax.axis_index("c")
    row = lax.axis_index("dp")
    other = 1 - c
    step = 1 - 2 * c
    fwd = lax.rem(z + step + z_count, z_count)
    bwd = lax.rem(z - step + z_count, z_count)
    fwd_id, bwd_id, pair_id = (row, fwd, c), (row, bwd, c), (row, z, other)
    mate_id = (lax.rem(row + dp_count // 2, dp_count), z, c)
    fwd_hops = z_count // 2
    bwd_hops = z_count - 1 - fwd_hops
    piece = part_ref.shape[2] // chunks

    barrier = pltpu.get_barrier_semaphore()
    for target in (fwd_id, bwd_id, pair_id, mate_id):
        pl.semaphore_signal(barrier, 1, device_id=target, device_id_type=MESH)
    pl.semaphore_wait(barrier, 4)

    sends = []

    def send(src, dst, sem, target):
        copy = pltpu.make_async_remote_copy(
            src_ref=src,
            dst_ref=dst,
            send_sem=send_sem.at[len(sends)],
            recv_sem=recv_sem.at[sem],
            device_id=target,
            device_id_type=MESH,
        )
        copy.start()
        sends.append(copy)

    def arrive(dst, sem):
        pltpu.make_async_remote_copy(
            src_ref=dst,
            dst_ref=dst,
            send_sem=send_sem.at[0],
            recv_sem=recv_sem.at[sem],
            device_id=pair_id,
            device_id_type=MESH,
        ).wait_recv()

    def order(ring_step):
        dests = []
        for hop in range(1, fwd_hops + 1):
            dests.append(lax.rem(z + ring_step * (fwd_hops + 1 - hop) + 2 * z_count, z_count))
            if hop <= bwd_hops:
                dests.append(lax.rem(z - ring_step * (bwd_hops + 1 - hop) + 2 * z_count, z_count))
        return dests + [z]

    for n, dest in enumerate(order(-step)):
        send(part_ref.at[other, dest], pair_buf.at[n], n, pair_id)
    def own(dest, n, k):
        if k == 0:
            arrive(pair_buf.at[n], n)
        rows = pl.ds(k * piece, piece)
        return part_ref[c, dest, rows].astype(jnp.float32) + pair_buf[n, rows].astype(
            jnp.float32
        )

    fwd_sem = z_count
    bwd_sem = z_count + fwd_hops * chunks
    for hop in range(1, fwd_hops + 1):
        for k in range(chunks):
            rows = pl.ds(k * piece, piece)
            dest = lax.rem(z + step * (fwd_hops + 1 - hop) + 2 * z_count, z_count)
            n = hop - 1 + min(hop - 1, bwd_hops)
            total = own(dest, n, k)
            if hop > 1:
                sem = fwd_sem + (hop - 2) * chunks + k
                arrive(fwd_buf.at[hop - 2, rows], sem)
                total = total + fwd_buf[hop - 2, rows].astype(jnp.float32)
            fwd_out[hop - 1, rows] = total.astype(fwd_out.dtype)
            sem = fwd_sem + (hop - 1) * chunks + k
            send(fwd_out.at[hop - 1, rows], fwd_buf.at[hop - 1, rows], sem, fwd_id)
            if hop <= bwd_hops:
                dest = lax.rem(z - step * (bwd_hops + 1 - hop) + 2 * z_count, z_count)
                total = own(dest, n + 1, k)
                if hop > 1:
                    sem = bwd_sem + (hop - 2) * chunks + k
                    arrive(bwd_buf.at[hop - 2, rows], sem)
                    total = total + bwd_buf[hop - 2, rows].astype(jnp.float32)
                bwd_out[hop - 1, rows] = total.astype(bwd_out.dtype)
                sem = bwd_sem + (hop - 1) * chunks + k
                send(bwd_out.at[hop - 1, rows], bwd_buf.at[hop - 1, rows], sem, bwd_id)
    width = out_ref.shape[1]
    per_chunk = piece // seq_len
    seq_out[...] = jnp.zeros(seq_out.shape, jnp.float32)
    for k in range(chunks):
        rows = pl.ds(k * piece, piece)
        total = own(z, fwd_hops + bwd_hops, k)
        arrive(fwd_buf.at[fwd_hops - 1, rows], fwd_sem + (fwd_hops - 1) * chunks + k)
        total = total + fwd_buf[fwd_hops - 1, rows].astype(jnp.float32)
        if bwd_hops > 0:
            arrive(bwd_buf.at[bwd_hops - 1, rows], bwd_sem + (bwd_hops - 1) * chunks + k)
            total = total + bwd_buf[bwd_hops - 1, rows].astype(jnp.float32)
        rounded = total.astype(out_ref.dtype)
        out_ref[rows] = rounded
        scored = rounded.astype(jnp.float32) * head_ref[...]
        per_seq = jnp.sum(scored.reshape(per_chunk, seq_len, width), axis=1)
        seq_score = jnp.sum(per_seq, axis=1, keepdims=True)
        seq_out[pl.ds(k * per_chunk, per_chunk)] = jnp.broadcast_to(
            seq_score, (per_chunk, seq_out.shape[1])
        )
    mate = pltpu.make_async_remote_copy(
        src_ref=seq_out,
        dst_ref=seq_in,
        send_sem=seq_sem.at[0],
        recv_sem=seq_sem.at[1],
        device_id=mate_id,
        device_id_type=MESH,
    )
    mate.start()
    mate.wait()
    mine = seq_out[...]
    theirs = seq_in[...]
    pair_out[...] = jnp.abs(mine - theirs) + 0.5 * (mine + theirs)
    for copy in sends:
        copy.wait_send()


def scatter_sums(partial, score_head, dp_count, seq_len, chunks):
    c_count, z_count, rows, width = partial.shape
    fwd_hops = z_count // 2
    bwd_hops = max(z_count - 1 - fwd_hops, 1)
    block = (rows, width)
    vmem = pl.BlockSpec(memory_space=pltpu.VMEM)
    sems = z_count + (fwd_hops + bwd_hops) * chunks
    tile = (8, 128)
    return pl.pallas_call(
        functools.partial(combine_kernel, z_count, dp_count, seq_len, chunks),
        out_shape=(
            jax.ShapeDtypeStruct(block, partial.dtype),
            jax.ShapeDtypeStruct(tile, jnp.float32),
        ),
        in_specs=[vmem, vmem],
        out_specs=(vmem, vmem),
        scratch_shapes=[
            pltpu.VMEM((z_count,) + block, partial.dtype),
            pltpu.VMEM((fwd_hops,) + block, partial.dtype),
            pltpu.VMEM((bwd_hops,) + block, partial.dtype),
            pltpu.VMEM((fwd_hops,) + block, partial.dtype),
            pltpu.VMEM((bwd_hops,) + block, partial.dtype),
            pltpu.VMEM(tile, jnp.float32),
            pltpu.VMEM(tile, jnp.float32),
            pltpu.SemaphoreType.DMA((sems,)),
            pltpu.SemaphoreType.DMA((sems,)),
            pltpu.SemaphoreType.DMA((2,)),
        ],
        compiler_params=pltpu.CompilerParams(
            collective_id=1, has_side_effects=True, vmem_limit_bytes=48 * 1024 * 1024
        ),
    )(partial, score_head.reshape(1, -1))


def body(
    tokens, expert_ids, gate_fixed, scorer_id, direction_tags, w_gate, w_up, w_down, score_head
):
    z_count = lax.axis_size("z")
    c_count = lax.axis_size("c")
    expert_count = z_count * c_count
    per_device = w_gate.shape[0]
    tok_rows, model_width = tokens.shape
    top_count = expert_ids.shape[1]
    which_tag = jnp.repeat(scorer_id, SEQ_LEN)[:, None]
    tag_rows = jnp.where(
        which_tag == 1, direction_tags[1][None, :], direction_tags[0][None, :]
    ).astype(jnp.float32)
    inputs = (tokens.astype(jnp.float32) + tag_rows).astype(jnp.bfloat16)
    rank_in = route_ranks(expert_ids, per_device * expert_count)
    routes = jnp.concatenate(
        [expert_ids, rank_in, gate_fixed // 256, gate_fixed % 256], axis=1
    ).astype(jnp.bfloat16)
    route_tile = routes.reshape(-1, 128)
    inputs_all, routes_all = gather_blocks(inputs, route_tile, z_count, 2)
    routes_all = routes_all.reshape(expert_count, tok_rows, 4 * top_count).astype(jnp.int32)
    ids_cube = routes_all[..., :top_count]
    rank_cube = routes_all[..., top_count : 2 * top_count]
    fixed_val = (
        routes_all[..., 2 * top_count : 3 * top_count] * 256 + routes_all[..., 3 * top_count :]
    ).astype(jnp.float32)
    weight_cube = fixed_val / jnp.sum(fixed_val, axis=2, keepdims=True)
    my_index = lax.axis_index("z") * c_count + lax.axis_index("c")
    local_count = per_device * MOST
    local_slot = ids_cube - my_index * per_device
    is_mine = (local_slot >= 0) & (local_slot < per_device)
    local_key = jnp.where(is_mine, local_slot * MOST + rank_cube, -1)
    match = (
        local_key[:, None, :, :] == jnp.arange(local_count, dtype=jnp.int32)[None, :, None, None]
    )
    picker = jnp.any(match, axis=3).astype(jnp.bfloat16)
    slot_weight = jnp.sum(jnp.where(match, weight_cube[:, None, :, :], 0.0), axis=(2, 3))
    picker = picker.reshape(expert_count, per_device, MOST, tok_rows).transpose(1, 0, 2, 3)
    slot_weight = slot_weight.reshape(expert_count, per_device, MOST).transpose(1, 0, 2)
    row_block = jnp.einsum(
        "esmt,std->esmd", picker, inputs_all, preferred_element_type=jnp.float32
    ).astype(jnp.bfloat16)
    gate_proj = jnp.einsum("esmd,edf->esmf", row_block, w_gate, preferred_element_type=jnp.float32)
    up_proj = jnp.einsum("esmd,edf->esmf", row_block, w_up, preferred_element_type=jnp.float32)
    hidden = (jax.nn.silu(gate_proj) * up_proj).astype(jnp.bfloat16)
    down_out = jnp.einsum("esmf,efd->esmd", hidden, w_down, preferred_element_type=jnp.float32)
    result = (slot_weight[..., None] * down_out).astype(jnp.bfloat16)
    result = lax.optimization_barrier(result)
    partial_value = jnp.einsum(
        "esmt,esmd->std", picker, result, preferred_element_type=jnp.float32
    )
    partial_value = partial_value.reshape(c_count, z_count, tok_rows, model_width)
    mixed, pair_tile = scatter_sums(
        partial_value.astype(jnp.bfloat16), score_head, lax.axis_size("dp"), SEQ_LEN, 4
    )
    pair_score = pair_tile[: tok_rows // SEQ_LEN, 0]
    return (mixed, pair_score)


def solution(mesh):
    dp_count, expert_count = mesh.devices.shape
    split = Mesh(mesh.devices.reshape(dp_count, expert_count // 2, 2), ("dp", "z", "c"))
    rows = P(("dp", "z", "c"), None)
    return jax.shard_map(
        body,
        mesh=split,
        in_specs=(
            rows,
            rows,
            rows,
            P(("dp", "z", "c")),
            P(),
            P(("z", "c"), None, None),
            P(("z", "c"), None, None),
            P(("z", "c"), None, None),
            P(),
        ),
        out_specs=(rows, P(("dp", "z", "c"))),
        check_vma=False,
    )
```
